256 devices in a mesh: ctx: 64 (over y, z, x_hi), tp: 4 (over x_lo, core).
Axes of the slice: x: 4 (x_hi: 2, x_lo: 2; x = x_hi * 2 + x_lo), y: 4, z: 8, core: 2. Of those that a mesh axis runs over, the one named last changes fastest.
Arguments:
- queries: bfloat16 [4096, 3584], P('ctx', 'tp'), may hold values from -6 to 6
- keys: bfloat16 [4096, 512], P('ctx', 'tp'), may hold values from -5 to 5
- values: bfloat16 [4096, 512], P('ctx', 'tp'), may hold values from -6 to 6
- block_table: int32 [64], replicated, may hold values from 0 to 63, each once
- residual: bfloat16 [4096, 3584], P(('ctx', 'tp')), may hold values from -6 to 6
- out_weight: bfloat16 [3584, 3584], P('tp'), may hold values from -0.5 to 0.5
- norm_gain: bfloat16 [3584], replicated, may hold values from 0.099609375 to 1.8984375
- gate_logit_weight: bfloat16 [3584], replicated, may hold values from -0.09375 to 0.09375
- gate_weight: bfloat16 [3584, 20480], P(None, 'ctx'), may hold values from -0.09375 to 0.09375
- up_weight: bfloat16 [3584, 20480], P(None, 'ctx'), may hold values from -0.09375 to 0.09375
- down_weight: bfloat16 [20480, 3584], P('ctx'), may hold values from -0.0390625 to 0.0390625
Outputs:
- layer_out: bfloat16 [4096, 3584], P(('ctx', 'tp'))
The draws below stay inside these ranges and needn't reach their ends.
Inputs may be any that keep to these rules, and one draw needn't show every extreme that they name: Each entry names a different pair; slot c holds blocks block_table[c] and its mirror, counted from the end of the prompt.
All inputs are finite; a program needn't handle non-finite values.
Results may differ from the reference program's by a relative error of at most 0.017.
Values may be sent and summed in bfloat16 or wider, within the bound.
No kernel may reach another device: no remote copies, remote signals or barrier semaphores. Data moves between devices by JAX's collectives and lax.ppermute only.
A program may use at most 128 MiB of HBM per device.

```python
import math
import jax
import jax.numpy as jnp
from jax import lax

D = 3584
HEADS = 28
KV_HEADS = 4
HEAD_DIM = 128
FF = 20480
TOK_DEV = 64
SEQ = 4096
N_CTX = 64


def draw_queries(key, part):
    base = jax.random.normal(jax.random.fold_in(key, 11), (SEQ, HEADS * HEAD_DIM), jnp.float32)
    base = jnp.clip(base, -4.5, 4.5)
    return base.astype(jnp.bfloat16)


def draw_keys(key, part):
    base = jax.random.normal(jax.random.fold_in(key, 12), (SEQ, KV_HEADS * HEAD_DIM), jnp.float32)
    base = jnp.clip(base, -5.0, 5.0)
    return base.astype(jnp.bfloat16)


def shard_levels(own_key, shape, pieces, low, high):
    def one(position, shards_of):
        draws = jax.random.uniform(jax.random.fold_in(jax.random.fold_in(own_key, 6), position), (shards_of,), jnp.float32, low / len(pieces), high / len(pieces))
        return jnp.repeat(jnp.exp(draws), shape[position] // shards_of).reshape((-1,) + (1,) * (len(shape) - position - 1))

    level = one(*pieces[0])
    for cut in pieces[1:]:
        level = level * one(*cut)
    return level


def normal_values(own_key, shape, spread, bound, shards=(), kind=jnp.bfloat16):
    factor_of = shard_levels(own_key, shape, shards, -0.22, 0.18) if shards else 1.0
    values = jax.random.normal(own_key, shape, jnp.float32) * spread * factor_of
    return jnp.minimum(jnp.maximum(values, -bound), bound).astype(kind)


def setup_inputs(seed: int = 0) -> dict:
    splits = jax.random.split(jax.random.key(seed), 12)
    return {
        "queries": draw_queries(jax.random.fold_in(splits[11], 71), 0),
        "keys": draw_keys(jax.random.fold_in(splits[11], 71), 0),
        "values": normal_values(splits[2], (SEQ, KV_HEADS * HEAD_DIM), 1.0, 6.0, ((0, 64), (1, 4))),
        "block_table": jax.random.permutation(splits[3], N_CTX).astype(jnp.int32),
        "residual": normal_values(splits[4], (SEQ, D), 1.0, 6.0, ((0, 256),)),
        "out_weight": normal_values(splits[5], (HEADS * HEAD_DIM, D), HEAD_DIM ** -0.5, 0.5, ((0, 4),)),
        "norm_gain": jnp.clip(1.0 + 0.18 * jax.random.normal(splits[6], (D,), jnp.float32), 0.099609375, 1.8984375).astype(jnp.bfloat16),
        "gate_logit_weight": normal_values(splits[7], (D,), D ** -0.5, 0.09375),
        "gate_weight": normal_values(splits[8], (D, FF), D ** -0.5, 0.09375, ((1, 64),)),
        "up_weight": normal_values(splits[9], (D, FF), D ** -0.5, 0.09375, ((1, 64),)),
        "down_weight": normal_values(splits[10], (FF, D), FF ** -0.5, 0.0390625, ((0, 64),)),
    }


def positions(block_table):
    rows = jnp.arange(SEQ, dtype=jnp.int32)
    owner = rows // TOK_DEV
    local = rows % TOK_DEV
    pair = block_table[owner].astype(jnp.int32)
    half = TOK_DEV // 2
    return jnp.where(local < half, pair * half + local, (2 * N_CTX - 1 - pair) * half + local - half)

def reference(queries, keys, values, block_table, residual, out_weight, norm_gain, gate_logit_weight, gate_weight, up_weight, down_weight):
    place = positions(block_table)
    group = HEADS // KV_HEADS
    scale = HEAD_DIM ** (-0.5)
    query_heads = queries.reshape(SEQ, KV_HEADS, group, HEAD_DIM).astype(jnp.float32)
    key_heads = keys.reshape(SEQ, KV_HEADS, HEAD_DIM).astype(jnp.float32)
    value_heads = values.reshape(SEQ, KV_HEADS, HEAD_DIM).astype(jnp.float32)
    rows_block = math.gcd(SEQ, 512)

    def attend_block(index):
        first = (index * rows_block).astype(jnp.int32)
        query_block = lax.dynamic_slice_in_dim(query_heads, first, rows_block, 0)
        query_place = lax.dynamic_slice_in_dim(place, first, rows_block, 0)
        score = jnp.einsum('tkgd,pkd->kgtp', query_block, key_heads) * scale
        visible = place[None, :] <= query_place[:, None]
        score = jnp.where(visible, score, -1e+30)
        top = lax.optimization_barrier(jnp.max(score, axis=-1, keepdims=True))
        weight = jnp.where(visible, jnp.exp(score - top), 0.0)
        total = lax.optimization_barrier(jnp.sum(weight, axis=-1))
        weight_bf = weight.astype(jnp.bfloat16).astype(jnp.float32)
        summed = jnp.einsum('kgtp,pkd->kgtd', weight_bf, value_heads) / total[..., None]
        summed = jnp.transpose(summed, (2, 0, 1, 3))
        return summed.astype(jnp.bfloat16).reshape(rows_block, HEADS * HEAD_DIM)
    blocks = lax.map(attend_block, jnp.arange(SEQ // rows_block, dtype=jnp.int32))
    attended_heads = blocks.reshape(SEQ, HEADS * HEAD_DIM)
    projected = jnp.dot(attended_heads, out_weight, preferred_element_type=jnp.float32)
    attended = (residual.astype(jnp.float32) + projected).astype(jnp.bfloat16)
    attended = lax.optimization_barrier(attended)
    attended_f = attended.astype(jnp.float32)
    mean_square = lax.optimization_barrier(jnp.mean(attended_f * attended_f, axis=-1, keepdims=True))
    normed = (attended_f * lax.rsqrt(mean_square + 1e-06) * norm_gain.astype(jnp.float32)).astype(jnp.bfloat16)
    gate_prob = jax.nn.sigmoid(jnp.dot(normed, gate_logit_weight, preferred_element_type=jnp.float32))
    gate_part = jnp.dot(normed, gate_weight, preferred_element_type=jnp.float32)
    up_part = jnp.dot(normed, up_weight, preferred_element_type=jnp.float32)
    hidden = (jax.nn.silu(gate_part) * up_part).astype(jnp.bfloat16)
    shared = jnp.dot(hidden, down_weight, preferred_element_type=jnp.float32)
    return (attended_f + gate_prob[:, None] * shared).astype(jnp.bfloat16)
```

```python
import functools

import jax
import jax.numpy as jnp
from jax import lax
from jax.experimental import pallas as pl
from jax.experimental.pallas import tpu as pltpu
from jax.sharding import Mesh
from jax.sharding import PartitionSpec as P

HEADS = 28
KV_HEADS = 4
HEAD_DIM = 128
GROUP = HEADS // KV_HEADS
SIZES = {"y": 4, "z": 8, "xh": 2, "xl": 2, "core": 2}
CTX = ("y", "z", "xh")
TP = ("xl", "core")
f32 = jnp.float32
bf16 = jnp.bfloat16
VMEM = pl.BlockSpec(memory_space=pltpu.VMEM)
SMEM = pl.BlockSpec(memory_space=pltpu.SMEM)
ANY = pl.BlockSpec(memory_space=pl.ANY)
NEG = -1e30
FLOOR = -1e29
EXP2 = 1.4426950408889634


def fetch(x, axis, k):
    n = SIZES[axis]
    k %= n
    if k == 0:
        return x
    return lax.ppermute(x, axis, [((i + k) % n, i) for i in range(n)])


def gather_direct(x, axis):
    return [fetch(x, axis, k) for k in range(SIZES[axis])]


def gather_ring(x, axis):
    n = SIZES[axis]
    r = [None] * n
    r[0] = x
    for k in range(1, n // 2 + 1):
        r[k] = fetch(r[k - 1], axis, 1)
        if n - k > n // 2:
            r[n - k] = fetch(r[(n - k + 1) % n], axis, -1)
    return r


def add_kernel(n_in, *refs):
    ins, outs = refs[:n_in], refs[n_in:]
    rows = outs[0].shape[0]
    for i, out in enumerate(outs):
        part = ins[0][i * rows : (i + 1) * rows, :].astype(f32)
        for other in ins[1:]:
            part += other[i * rows : (i + 1) * rows, :].astype(f32)
        out[...] = part.astype(out.dtype)


def add(xs, pieces=1):
    rows, width = xs[0].shape
    size = rows * width
    out = pl.pallas_call(
        functools.partial(add_kernel, len(xs)),
        out_shape=[jax.ShapeDtypeStruct((rows // pieces, width), bf16)] * pieces,
        in_specs=[VMEM] * len(xs),
        out_specs=[VMEM] * pieces,
        cost_estimate=pl.CostEstimate(
            flops=size * len(xs), bytes_accessed=2 * size * (len(xs) + 1), transcendentals=0
        ),
    )(*xs)
    return out[0] if pieces == 1 else out


def scatter_direct(chunks, axis):
    return [chunks[0]] + [fetch(chunks[k], axis, -k) for k in range(1, SIZES[axis])]


def scatter_ring(chunks, axis):
    n = SIZES[axis]
    h = n // 2
    up = fetch(chunks[h], axis, -1)
    down = fetch(chunks[h + 1], axis, 1)
    for k in range(h - 1, 0, -1):
        up = fetch(add([chunks[k], up]), axis, -1)
        if k > 1:
            down = fetch(add([chunks[n - k + 1], down]), axis, 1)
    return [chunks[0], up, down]


def attention_kernel(t_ref, q_ref, kp_ref, qp_ref, *refs):
    kvs, w_any, outs, (w_ref, sem) = refs[:8], refs[8], refs[9:13], refs[13:]
    copy = pltpu.make_async_copy(w_any, w_ref, sem)
    copy.start()
    t = t_ref[0]
    quarter = q_ref.shape[0] // 4
    rows = [
        q_ref[pl.ds(pl.multiple_of((t ^ k) * quarter, quarter), quarter), :] for k in range(4)
    ]
    q = jnp.concatenate(rows, axis=0)
    tokens = q.shape[0]
    q = jnp.concatenate([q[:, g * HEAD_DIM : (g + 1) * HEAD_DIM] for g in range(GROUP)], axis=0)
    qp = qp_ref[...]
    total_rows = GROUP * tokens
    top = jnp.full((total_rows, 1), FLOOR, f32)
    total = jnp.zeros((total_rows, 1), f32)
    acc = jnp.zeros((total_rows, HEAD_DIM), f32)
    for j in range(8):
        k = kvs[j][:, :HEAD_DIM]
        v = kvs[j][:, HEAD_DIM:]
        count = k.shape[0]
        score = lax.dot_general(q, k, (((1,), (1,)), ((), ())), preferred_element_type=f32)
        score = score * (HEAD_DIM**-0.5 * EXP2)
        visible = kp_ref[j : j + 1, :] <= qp
        score = jnp.where(visible[None], score.reshape(GROUP, tokens, count), NEG)
        score = score.reshape(total_rows, count)
        new_top = jnp.maximum(top, jnp.max(score, axis=-1, keepdims=True))
        weight = jnp.exp2(score - new_top)
        keep = jnp.exp2(top - new_top)
        total = total * keep + jnp.sum(weight, axis=-1, keepdims=True)
        acc = acc * keep + jnp.dot(weight.astype(bf16), v, preferred_element_type=f32)
        top = new_top
    summed = (acc / total).astype(bf16)
    heads = jnp.concatenate([summed[g * tokens : (g + 1) * tokens] for g in range(GROUP)], axis=1)
    copy.wait()
    width = 512
    for n in range(w_ref.shape[1] // width):
        cols = slice(n * width, (n + 1) * width)
        part = jnp.dot(heads, w_ref[:, cols], preferred_element_type=f32).astype(bf16)
        for k in range(4):
            outs[k][:, cols] = part[k * quarter : (k + 1) * quarter]


def norm_kernel(p0, p1, p2, p3, residual, gain, gate_w, attended, first, second, prob):
    head_sum = p0[...].astype(f32) + p1[...].astype(f32) + p2[...].astype(f32) + p3[...].astype(f32)
    kept = (residual[...].astype(f32) + head_sum).astype(bf16)
    attended[...] = kept
    wide = kept.astype(f32)
    mean_square = jnp.mean(wide * wide, axis=-1, keepdims=True)
    normed = (wide * lax.rsqrt(mean_square + 1e-06) * gain[...].astype(f32)).astype(bf16)
    half = first.shape[0]
    first[...] = normed[:half]
    second[...] = normed[half:]
    logit = jnp.sum(normed.astype(f32) * gate_w[...].astype(f32), axis=-1, keepdims=True)
    prob[...] = jnp.broadcast_to(1.0 / (1.0 + jnp.exp(-logit)), prob.shape)


def expert_kernel(*refs):
    xs, (g_any, u_any, d_any, a_any, b_any) = refs[:12], refs[12:17]
    outs = refs[17:29]
    x_ref, w_ref, d_ref, h_ref, sems = refs[29:]
    own = g_any.shape[0]
    swap = a_any.shape[0] // 3
    block = 128
    blocks = (own + 2 * swap) // block
    waits = []

    def start(src, dst, slot):
        copy = pltpu.make_async_copy(src, dst, sems.at[slot])
        copy.start()
        return copy

    row = 0
    for x in xs:
        n = x.shape[0]
        waits.append(start(x, x_ref.at[pl.ds(row, n)], len(waits)))
        row += n
    by_block = [[] for _ in range(blocks)]
    slot = len(waits)
    for part in range(2):
        pos = 0
        for source, at, length in (
            ((g_any, u_any)[part], 0, own),
            (a_any, part * swap, swap),
            (b_any, part * swap, swap),
        ):
            done = 0
            while done < length:
                b, inside = divmod(pos, block)
                n = min(block - inside, length - done)
                by_block[b].append((source, at + done, b * 2 * block + part * block + inside, n))
                done += n
                pos += n
    block_waits = []
    for b in range(blocks):
        mine = []
        for source, at, to, n in by_block[b]:
            mine.append(start(source.at[pl.ds(at, n)], w_ref.at[pl.ds(to, n)], slot))
            slot += 1
        block_waits.append(mine)
    down_waits = [
        start(d_any, d_ref.at[pl.ds(0, own)], slot),
        start(a_any.at[pl.ds(2 * swap, swap)], d_ref.at[pl.ds(own, swap)], slot + 1),
        start(b_any.at[pl.ds(2 * swap, swap)], d_ref.at[pl.ds(own + swap, swap)], slot + 2),
    ]
    for copy in waits:
        copy.wait()
    for b in range(blocks):
        for copy in block_waits[b]:
            copy.wait()
        both = lax.dot_general(
            x_ref[...],
            w_ref[b * 2 * block : (b + 1) * 2 * block, :],
            (((1,), (1,)), ((), ())),
            preferred_element_type=f32,
        )
        gate, up = both[:, :block], both[:, block:]
        h_ref[:, b * block : (b + 1) * block] = (gate / (1.0 + jnp.exp(-gate)) * up).astype(bf16)
    for copy in down_waits:
        copy.wait()
    width = 256
    for n in range(d_ref.shape[1] // width):
        cols = slice(n * width, (n + 1) * width)
        part = jnp.dot(h_ref[...], d_ref[:, cols], preferred_element_type=f32).astype(bf16)
        row = 0
        for out in outs:
            out[:, cols] = part[row : row + out.shape[0]]
            row += out.shape[0]


def final_kernel(*refs):
    attended, prob = refs[:2]
    first, second, out = refs[2:6], refs[6:14], refs[14]
    half = first[0].shape[0]

    def total(terms):
        t = terms[0][...].astype(f32)
        for term in terms[1:]:
            t += term[...].astype(f32)
        return t

    for i, terms in enumerate((first, second)):
        rows = slice(i * half, (i + 1) * half)
        out[rows, :] = (
            attended[rows, :].astype(f32) + prob[rows, :1] * total(terms)
        ).astype(bf16)


def per_device(
    queries,
    keys,
    values,
    block_table,
    residual,
    out_weight,
    norm_gain,
    gate_logit_weight,
    gate_weight,
    up_weight,
    down_weight,
):
    tokens = queries.shape[0]
    half = tokens // 2
    quarter = tokens // 4
    width = residual.shape[1]
    hidden = down_weight.shape[0]
    y, z, xh = (lax.axis_index(a) for a in CTX)
    core = lax.axis_index("core")
    t = lax.axis_index(TP)

    gate_t, up_t = gate_weight.T, up_weight.T
    piece = hidden // 2
    to_send = jnp.concatenate(
        [
            lax.dynamic_slice_in_dim(w, core * piece, piece, 0)
            for w in (gate_t, up_t, down_weight)
        ],
        axis=0,
    )
    swap_a = lax.ppermute(to_send, ("xh", "xl"), [(0, 3), (3, 0), (1, 2), (2, 1)])
    swap_b = fetch(swap_a, "core", 1)

    kv = jnp.concatenate([keys, values], axis=1)
    along_z = jnp.concatenate(gather_direct(kv, "z"), axis=0)
    across = fetch(along_z, "xh", 1)
    kvs = gather_direct(along_z, "y") + gather_direct(across, "y")

    ids = jnp.arange(64, dtype=jnp.int32)
    slot = (
        ((y + (ids // 8) % 4) % 4 * 8 + (z + ids % 8) % 8) * 2 + (xh + ids // 32) % 2
    ).astype(jnp.int32)
    all_slots = jnp.arange(block_table.shape[0], dtype=jnp.int32)
    mirror = 2 * block_table.shape[0] - 1

    def pair_of(s):
        onehot = (s[:, None] == all_slots[None, :]).astype(jnp.int32)
        return jnp.sum(onehot * block_table[None, :], axis=1)

    def place(pair, local):
        return jnp.where(local < half, pair * half + local, (mirror - pair) * half + local - half)

    pairs = pair_of(slot)
    local = jnp.arange(tokens, dtype=jnp.int32)
    key_place = place(pairs[:, None], local[None, :]).reshape(8, 8 * tokens)
    rel = jnp.arange(tokens, dtype=jnp.int32)
    own_local = ((rel // quarter) ^ t.astype(jnp.int32)) * quarter + rel % quarter
    query_place = place(pairs[0], own_local)[:, None]

    rows = GROUP * tokens
    span = 64 * tokens
    partial = pl.pallas_call(
        attention_kernel,
        out_shape=[jax.ShapeDtypeStruct((quarter, width), bf16)] * 4,
        in_specs=[SMEM, VMEM, VMEM, VMEM] + [VMEM] * 8 + [ANY],
        out_specs=[VMEM] * 4,
        scratch_shapes=[pltpu.VMEM(out_weight.shape, bf16), pltpu.SemaphoreType.DMA],
        compiler_params=pltpu.CompilerParams(vmem_limit_bytes=40 << 20),
        cost_estimate=pl.CostEstimate(
            flops=4 * rows * span * HEAD_DIM + 2 * tokens * out_weight.size,
            bytes_accessed=2 * out_weight.size + 4 * span * HEAD_DIM,
            transcendentals=rows * span,
        ),
    )(t.astype(jnp.int32)[None], queries, key_place, query_place, *kvs, out_weight)

    terms = [partial[0]] + [
        lax.ppermute(partial[k], TP, [(i, i ^ k) for i in range(4)]) for k in (1, 2, 3)
    ]
    eighth = quarter // 2
    attended, first, second, prob = pl.pallas_call(
        norm_kernel,
        out_shape=[
            jax.ShapeDtypeStruct((quarter, width), bf16),
            jax.ShapeDtypeStruct((eighth, width), bf16),
            jax.ShapeDtypeStruct((eighth, width), bf16),
            jax.ShapeDtypeStruct((quarter, 128), f32),
        ],
        in_specs=[VMEM] * 7,
        out_specs=[VMEM] * 4,
        cost_estimate=pl.CostEstimate(
            flops=10 * quarter * width, bytes_accessed=14 * quarter * width, transcendentals=quarter
        ),
    )(*terms, residual, norm_gain[None, :], gate_logit_weight[None, :])

    first_y = jnp.concatenate(gather_direct(first, "y"), axis=0)
    second_z = jnp.concatenate(gather_direct(second, "z"), axis=0)
    pieces = gather_ring(first_y, "z") + gather_direct(second_z, "y")
    n_rows = sum(p.shape[0] for p in pieces)
    n_hidden = 2 * hidden
    parts = pl.pallas_call(
        expert_kernel,
        out_shape=[jax.ShapeDtypeStruct(p.shape, bf16) for p in pieces],
        in_specs=[ANY] * 17,
        out_specs=[VMEM] * 12,
        scratch_shapes=[
            pltpu.VMEM((n_rows, width), bf16),
            pltpu.VMEM((2 * n_hidden, width), bf16),
            pltpu.VMEM((n_hidden, width), bf16),
            pltpu.VMEM((n_rows, n_hidden), bf16),
            pltpu.SemaphoreType.DMA((40,)),
        ],
        compiler_params=pltpu.CompilerParams(vmem_limit_bytes=44 << 20),
        cost_estimate=pl.CostEstimate(
            flops=6 * n_rows * n_hidden * width,
            bytes_accessed=6 * n_hidden * width + 4 * n_rows * width,
            transcendentals=n_rows * n_hidden,
        ),
    )(*pieces, gate_t, up_t, down_weight, swap_a, swap_b)

    first_sum = add(scatter_ring(parts[:8], "z"), pieces=4)
    second_sum = add(scatter_direct(parts[8:], "y"), pieces=8)
    first_terms = scatter_direct(first_sum, "y")
    second_terms = scatter_direct(second_sum, "z")
    return pl.pallas_call(
        final_kernel,
        out_shape=jax.ShapeDtypeStruct((quarter, width), bf16),
        in_specs=[VMEM] * 14,
        out_specs=VMEM,
        cost_estimate=pl.CostEstimate(
            flops=10 * quarter * width, bytes_accessed=16 * quarter * width, transcendentals=0
        ),
    )(attended, prob, *first_terms, *second_terms)


def solution(mesh):
    fine = Mesh(mesh.devices.reshape(tuple(SIZES.values())), tuple(SIZES))
    return jax.shard_map(
        per_device,
        mesh=fine,
        in_specs=(
            P(CTX, TP),
            P(CTX, TP),
            P(CTX, TP),
            P(),
            P(CTX + TP, None),
            P(TP, None),
            P(),
            P(),
            P(None, CTX),
            P(None, CTX),
            P(CTX, None),
        ),
        out_specs=P(CTX + TP, None),
        check_vma=False,
    )
```

```python
import functools

import jax
import jax.numpy as jnp
from jax import lax
from jax.experimental import pallas as pl
from jax.experimental.pallas import tpu as pltpu
from jax.sharding import Mesh
from jax.sharding import PartitionSpec as P

HEADS = 28
KV_HEADS = 4
HEAD_DIM = 128
GROUP = HEADS // KV_HEADS
SIZES = {"y": 4, "z": 8, "xh": 2, "xl": 2, "core": 2}
CTX = ("y", "z", "xh")
TP = ("xl", "core")
f32 = jnp.float32
bf16 = jnp.bfloat16
VMEM = pl.BlockSpec(memory_space=pltpu.VMEM)
SMEM = pl.BlockSpec(memory_space=pltpu.SMEM)
HBM = pl.BlockSpec(memory_space=pltpu.HBM)
SMALL = pltpu.CompilerParams(vmem_limit_bytes=8 << 20)
NEG = -1e30
FLOOR = -1e29
EXP2 = 1.4426950408889634


def fetch(x, axis, k):
    n = SIZES[axis]
    k %= n
    if k == 0:
        return x
    return lax.ppermute(x, axis, [((i + k) % n, i) for i in range(n)])


def gather_direct(x, axis):
    return [fetch(x, axis, k) for k in range(SIZES[axis])]


def gather_ring(x, axis):
    n = SIZES[axis]
    r = [None] * n
    r[0] = x
    for k in range(1, n // 2 + 1):
        r[k] = fetch(r[k - 1], axis, 1)
        if n - k > n // 2:
            r[n - k] = fetch(r[(n - k + 1) % n], axis, -1)
    return r


def add_kernel(n_in, *refs):
    ins, outs = refs[:n_in], refs[n_in:]
    rows = outs[0].shape[0]
    for i, out in enumerate(outs):
        part = ins[0][i * rows : (i + 1) * rows, :].astype(f32)
        for other in ins[1:]:
            part += other[i * rows : (i + 1) * rows, :].astype(f32)
        out[...] = part.astype(out.dtype)


def add(xs, pieces=1):
    rows, width = xs[0].shape
    size = rows * width
    out = pl.pallas_call(
        functools.partial(add_kernel, len(xs)),
        out_shape=[jax.ShapeDtypeStruct((rows // pieces, width), bf16)] * pieces,
        in_specs=[VMEM] * len(xs),
        out_specs=[VMEM] * pieces,
        compiler_params=SMALL,
        cost_estimate=pl.CostEstimate(
            flops=size * len(xs), bytes_accessed=2 * size * (len(xs) + 1), transcendentals=0
        ),
    )(*xs)
    return out[0] if pieces == 1 else out


def scatter_direct(chunks, axis):
    return [chunks[0]] + [fetch(chunks[k], axis, -k) for k in range(1, SIZES[axis])]


def scatter_ring(chunks, axis):
    n = SIZES[axis]
    h = n // 2
    up = fetch(chunks[h], axis, -1)
    down = fetch(chunks[h + 1], axis, 1)
    for k in range(h - 1, 0, -1):
        up = fetch(add([chunks[k], up]), axis, -1)
        if k > 1:
            down = fetch(add([chunks[n - k + 1], down]), axis, 1)
    return [chunks[0], up, down]


def attention_kernel(t_ref, q_ref, kp_ref, qp_ref, *refs):
    kvs, w_any, outs, (w_ref, sem) = refs[:8], refs[8], refs[9:13], refs[13:]
    copy = pltpu.make_async_copy(w_any, w_ref, sem)
    copy.start()
    t = t_ref[0]
    quarter = q_ref.shape[0] // 4
    rows = [
        q_ref[pl.ds(pl.multiple_of((t ^ k) * quarter, quarter), quarter), :] for k in range(4)
    ]
    q = jnp.concatenate(rows, axis=0)
    tokens = q.shape[0]
    q = jnp.concatenate([q[:, g * HEAD_DIM : (g + 1) * HEAD_DIM] for g in range(GROUP)], axis=0)
    qp = qp_ref[...]
    total_rows = GROUP * tokens
    top = jnp.full((total_rows, 1), FLOOR, f32)
    total = jnp.zeros((total_rows, 1), f32)
    acc = jnp.zeros((total_rows, HEAD_DIM), f32)
    for j in range(8):
        k = kvs[j][:, :HEAD_DIM]
        v = kvs[j][:, HEAD_DIM:]
        count = k.shape[0]
        score = lax.dot_general(q, k, (((1,), (1,)), ((), ())), preferred_element_type=f32)
        score = score * (HEAD_DIM**-0.5 * EXP2)
        visible = kp_ref[j : j + 1, :] <= qp
        score = jnp.where(visible[None], score.reshape(GROUP, tokens, count), NEG)
        score = score.reshape(total_rows, count)
        new_top = jnp.maximum(top, jnp.max(score, axis=-1, keepdims=True))
        weight = jnp.exp2(score - new_top)
        keep = jnp.exp2(top - new_top)
        total = total * keep + jnp.sum(weight, axis=-1, keepdims=True)
        acc = acc * keep + jnp.dot(weight.astype(bf16), v, preferred_element_type=f32)
        top = new_top
    summed = (acc / total).astype(bf16)
    heads = jnp.concatenate([summed[g * tokens : (g + 1) * tokens] for g in range(GROUP)], axis=1)
    copy.wait()
    width = 512

    @pl.loop(0, w_ref.shape[1] // width)
    def _(n):
        cols = pl.ds(pl.multiple_of(n * width, width), width)
        part = jnp.dot(heads, w_ref[:, cols], preferred_element_type=f32).astype(bf16)
        for k in range(4):
            outs[k][:, cols] = part[k * quarter : (k + 1) * quarter]


def norm_kernel(p0, p1, p2, p3, residual, gain, gate_w, attended, first, second, prob):
    head_sum = p0[...].astype(f32) + p1[...].astype(f32) + p2[...].astype(f32) + p3[...].astype(f32)
    kept = (residual[...].astype(f32) + head_sum).astype(bf16)
    attended[...] = kept
    wide = kept.astype(f32)
    mean_square = jnp.mean(wide * wide, axis=-1, keepdims=True)
    normed = (wide * lax.rsqrt(mean_square + 1e-06) * gain[...].astype(f32)).astype(bf16)
    half = first.shape[0]
    first[...] = normed[:half]
    second[...] = normed[half:]
    logit = jnp.sum(normed.astype(f32) * gate_w[...].astype(f32), axis=-1, keepdims=True)
    prob[...] = jnp.broadcast_to(1.0 / (1.0 + jnp.exp(-logit)), prob.shape)


def send_kernel(core_ref, g_any, u_any, d_any, out_any, sems):
    n = out_any.shape[0] // 3
    at = pl.multiple_of(core_ref[0] * n, n)
    copies = [
        pltpu.make_async_copy(w.at[pl.ds(at, n)], out_any.at[pl.ds(i * n, n)], sems.at[i])
        for i, w in enumerate((g_any, u_any, d_any))
    ]
    for copy in copies:
        copy.start()
    for copy in copies:
        copy.wait()


def assemble_kernel(g_any, u_any, d_any, a_any, b_any, w_ref, d_ref, sems):
    own = g_any.shape[0]
    swap = a_any.shape[0] // 3
    block = 128
    copies = []

    def start(src, at, dst, to, n):
        copy = pltpu.make_async_copy(
            src.at[pl.ds(at, n)], dst.at[pl.ds(to, n)], sems.at[len(copies)]
        )
        copy.start()
        copies.append(copy)

    for part in range(2):
        pos = 0
        for source, at, length in (
            ((g_any, u_any)[part], 0, own),
            (a_any, part * swap, swap),
            (b_any, part * swap, swap),
        ):
            done = 0
            while done < length:
                b, inside = divmod(pos, block)
                n = min(block - inside, length - done)
                start(source, at + done, w_ref, b * 2 * block + part * block + inside, n)
                done += n
                pos += n
    start(d_any, 0, d_ref, 0, own)
    start(a_any, 2 * swap, d_ref, own, swap)
    start(b_any, 2 * swap, d_ref, own + swap, swap)
    for copy in copies:
        copy.wait()


def expert_kernel(count, *refs):
    xs, w_ref, d_ref, outs = refs[:count], refs[count], refs[count + 1], refs[count + 2 : -2]
    x_ref, h_ref = refs[-2:]
    n = xs[0].shape[0]
    for i, x in enumerate(xs):
        x_ref[i * n : (i + 1) * n, :] = x[...]
    block = 128

    @pl.loop(0, w_ref.shape[0] // (2 * block))
    def _(b):
        both = lax.dot_general(
            x_ref[...],
            w_ref[pl.ds(pl.multiple_of(b * 2 * block, 2 * block), 2 * block), :],
            (((1,), (1,)), ((), ())),
            preferred_element_type=f32,
        )
        gate, up = both[:, :block], both[:, block:]
        value = (gate / (1.0 + jnp.exp(-gate)) * up).astype(bf16)
        h_ref[:, pl.ds(pl.multiple_of(b * block, block), block)] = value

    width = 512

    @pl.loop(0, d_ref.shape[1] // width)
    def _(c):
        cols = pl.ds(pl.multiple_of(c * width, width), width)
        part = jnp.dot(h_ref[...], d_ref[:, cols], preferred_element_type=f32).astype(bf16)
        for i, out in enumerate(outs):
            out[:, cols] = part[i * n : (i + 1) * n]


def join_kernel(*refs):
    out = refs[-1]
    n = refs[0].shape[0]
    for i, ref in enumerate(refs[:-1]):
        out[i * n : (i + 1) * n, :] = ref[...]


def join(xs):
    rows, width = xs[0].shape
    return pl.pallas_call(
        join_kernel,
        out_shape=jax.ShapeDtypeStruct((rows * len(xs), width), bf16),
        in_specs=[VMEM] * len(xs),
        out_specs=VMEM,
        compiler_params=SMALL,
        cost_estimate=pl.CostEstimate(
            flops=0, bytes_accessed=4 * rows * len(xs) * width, transcendentals=0
        ),
    )(*xs)


def expert(xs, weights):
    w, d = weights
    rows, width = sum(x.shape[0] for x in xs), xs[0].shape[1]
    units = d.shape[0]
    return pl.pallas_call(
        functools.partial(expert_kernel, len(xs)),
        out_shape=[jax.ShapeDtypeStruct(x.shape, bf16) for x in xs],
        in_specs=[VMEM] * (len(xs) + 2),
        out_specs=[VMEM] * len(xs),
        scratch_shapes=[pltpu.VMEM((rows, width), bf16), pltpu.VMEM((rows, units), bf16)],
        compiler_params=pltpu.CompilerParams(vmem_limit_bytes=30 << 20),
        cost_estimate=pl.CostEstimate(
            flops=6 * rows * units * width,
            bytes_accessed=6 * units * width + 4 * rows * width,
            transcendentals=rows * units,
        ),
    )(*xs, w, d)


def final_kernel(*refs):
    attended, prob = refs[:2]
    first, second, out = refs[2:6], refs[6:14], refs[14]
    half = first[0].shape[0]

    def total(terms):
        t = terms[0][...].astype(f32)
        for term in terms[1:]:
            t += term[...].astype(f32)
        return t

    for i, terms in enumerate((first, second)):
        rows = slice(i * half, (i + 1) * half)
        out[rows, :] = (
            attended[rows, :].astype(f32) + prob[rows, :1] * total(terms)
        ).astype(bf16)


def per_device(
    queries,
    keys,
    values,
    block_table,
    residual,
    out_weight,
    norm_gain,
    gate_logit_weight,
    gate_weight,
    up_weight,
    down_weight,
):
    tokens = queries.shape[0]
    half = tokens // 2
    quarter = tokens // 4
    width = residual.shape[1]
    hidden = down_weight.shape[0]
    y, z, xh = (lax.axis_index(a) for a in CTX)
    core = lax.axis_index("core")
    t = lax.axis_index(TP)

    gate_t, up_t = gate_weight.T, up_weight.T
    piece = hidden // 2
    to_send = pl.pallas_call(
        send_kernel,
        out_shape=jax.ShapeDtypeStruct((3 * piece, width), bf16),
        in_specs=[SMEM, HBM, HBM, HBM],
        out_specs=HBM,
        scratch_shapes=[pltpu.SemaphoreType.DMA((3,))],
        cost_estimate=pl.CostEstimate(
            flops=0, bytes_accessed=12 * piece * width, transcendentals=0
        ),
    )(core.astype(jnp.int32)[None], gate_t, up_t, down_weight)
    swap_a = lax.ppermute(to_send, ("xh", "xl"), [(0, 3), (3, 0), (1, 2), (2, 1)])

    kv = jnp.concatenate([keys, values], axis=1)
    along_z = jnp.concatenate(gather_direct(kv, "z"), axis=0)
    across = fetch(along_z, "xh", 1)
    kvs = gather_direct(along_z, "y") + gather_direct(across, "y")

    ids = jnp.arange(64, dtype=jnp.int32)
    slot = (
        ((y + (ids // 8) % 4) % 4 * 8 + (z + ids % 8) % 8) * 2 + (xh + ids // 32) % 2
    ).astype(jnp.int32)
    all_slots = jnp.arange(block_table.shape[0], dtype=jnp.int32)
    mirror = 2 * block_table.shape[0] - 1

    def pair_of(s):
        onehot = (s[:, None] == all_slots[None, :]).astype(jnp.int32)
        return jnp.sum(onehot * block_table[None, :], axis=1)

    def place(pair, local):
        return jnp.where(local < half, pair * half + local, (mirror - pair) * half + local - half)

    pairs = pair_of(slot)
    local = jnp.arange(tokens, dtype=jnp.int32)
    key_place = place(pairs[:, None], local[None, :]).reshape(8, 8 * tokens)
    rel = jnp.arange(tokens, dtype=jnp.int32)
    own_local = ((rel // quarter) ^ t.astype(jnp.int32)) * quarter + rel % quarter
    query_place = place(pairs[0], own_local)[:, None]

    rows = GROUP * tokens
    span = 64 * tokens
    partial = pl.pallas_call(
        attention_kernel,
        out_shape=[jax.ShapeDtypeStruct((quarter, width), bf16)] * 4,
        in_specs=[SMEM, VMEM, VMEM, VMEM] + [VMEM] * 8 + [HBM],
        out_specs=[VMEM] * 4,
        scratch_shapes=[pltpu.VMEM(out_weight.shape, bf16), pltpu.SemaphoreType.DMA],
        compiler_params=pltpu.CompilerParams(vmem_limit_bytes=46 << 20),
        cost_estimate=pl.CostEstimate(
            flops=4 * rows * span * HEAD_DIM + 2 * tokens * out_weight.size,
            bytes_accessed=2 * out_weight.size + 4 * span * HEAD_DIM,
            transcendentals=rows * span,
        ),
    )(t.astype(jnp.int32)[None], queries, key_place, query_place, *kvs, out_weight)

    terms = [partial[0]] + [
        lax.ppermute(partial[k], TP, [(i, i ^ k) for i in range(4)]) for k in (1, 2, 3)
    ]
    eighth = quarter // 2
    attended, first, second, prob = pl.pallas_call(
        norm_kernel,
        out_shape=[
            jax.ShapeDtypeStruct((quarter, width), bf16),
            jax.ShapeDtypeStruct((eighth, width), bf16),
            jax.ShapeDtypeStruct((eighth, width), bf16),
            jax.ShapeDtypeStruct((quarter, 128), f32),
        ],
        in_specs=[VMEM] * 7,
        out_specs=[VMEM] * 4,
        compiler_params=SMALL,
        cost_estimate=pl.CostEstimate(
            flops=10 * quarter * width, bytes_accessed=14 * quarter * width, transcendentals=quarter
        ),
    )(*terms, residual, norm_gain[None, :], gate_logit_weight[None, :])

    first_y = join(gather_direct(first, "y"))
    second_z = join(gather_direct(second, "z"))
    first_all = gather_ring(first_y, "z")
    swap_a, second_z = lax.optimization_barrier((swap_a, second_z))
    second_all = gather_direct(second_z, "y")
    swap_b = fetch(swap_a, "core", 1)
    weights = pl.pallas_call(
        assemble_kernel,
        out_shape=[
            jax.ShapeDtypeStruct((4 * hidden, width), bf16),
            jax.ShapeDtypeStruct((2 * hidden, width), bf16),
        ],
        in_specs=[HBM] * 5,
        out_specs=[VMEM] * 2,
        scratch_shapes=[pltpu.SemaphoreType.DMA((24,))],
        compiler_params=pltpu.CompilerParams(vmem_limit_bytes=16 << 20),
        cost_estimate=pl.CostEstimate(
            flops=0, bytes_accessed=12 * hidden * width, transcendentals=0
        ),
    )(gate_t, up_t, down_weight, swap_a, swap_b)
    first_parts = expert(first_all, weights)
    second_parts = expert(second_all, weights)

    first_sum = add(scatter_ring(first_parts, "z"), pieces=4)
    second_sum = add(scatter_direct(second_parts, "y"), pieces=8)
    first_terms = scatter_direct(first_sum, "y")
    second_terms = scatter_direct(second_sum, "z")
    return pl.pallas_call(
        final_kernel,
        out_shape=jax.ShapeDtypeStruct((quarter, width), bf16),
        in_specs=[VMEM] * 14,
        out_specs=VMEM,
        compiler_params=SMALL,
        cost_estimate=pl.CostEstimate(
            flops=10 * quarter * width, bytes_accessed=16 * quarter * width, transcendentals=0
        ),
    )(attended, prob, *first_terms, *second_terms)


def solution(mesh):
    fine = Mesh(mesh.devices.reshape(tuple(SIZES.values())), tuple(SIZES))
    return jax.shard_map(
        per_device,
        mesh=fine,
        in_specs=(
            P(CTX, TP),
            P(CTX, TP),
            P(CTX, TP),
            P(),
            P(CTX + TP, None),
            P(TP, None),
            P(),
            P(),
            P(None, CTX),
            P(None, CTX),
            P(CTX, None),
        ),
        out_specs=P(CTX + TP, None),
        check_vma=False,
    )
```

```python
import functools

import jax
import jax.numpy as jnp
from jax import lax
from jax.experimental import pallas as pl
from jax.experimental.pallas import tpu as pltpu
from jax.sharding import Mesh
from jax.sharding import PartitionSpec as P

HEADS = 28
KV_HEADS = 4
HEAD_DIM = 128
GROUP = HEADS // KV_HEADS
SIZES = {"y": 4, "z": 8, "xh": 2, "xl": 2, "core": 2}
CTX = ("y", "z", "xh")
TP = ("xl", "core")
f32 = jnp.float32
bf16 = jnp.bfloat16
VMEM = pl.BlockSpec(memory_space=pltpu.VMEM)
SMEM = pl.BlockSpec(memory_space=pltpu.SMEM)
HBM = pl.BlockSpec(memory_space=pltpu.HBM)
SMALL = pltpu.CompilerParams(vmem_limit_bytes=8 << 20)
NEG = -1e30
FLOOR = -1e29
EXP2 = 1.4426950408889634


def fetch(x, axis, k):
    n = SIZES[axis]
    k %= n
    if k == 0:
        return x
    return lax.ppermute(x, axis, [((i + k) % n, i) for i in range(n)])


def gather_direct(x, axis):
    return [fetch(x, axis, k) for k in range(SIZES[axis])]


def gather_ring(x, axis):
    n = SIZES[axis]
    r = [None] * n
    r[0] = x
    for k in range(1, n // 2 + 1):
        r[k] = fetch(r[k - 1], axis, 1)
        if n - k > n // 2:
            r[n - k] = fetch(r[(n - k + 1) % n], axis, -1)
    return r


def add_kernel(n_in, *refs):
    ins, outs = refs[:n_in], refs[n_in:]
    rows = outs[0].shape[0]
    for i, out in enumerate(outs):
        part = ins[0][i * rows : (i + 1) * rows, :].astype(f32)
        for other in ins[1:]:
            part += other[i * rows : (i + 1) * rows, :].astype(f32)
        out[...] = part.astype(out.dtype)


def add(xs, pieces=1):
    rows, width = xs[0].shape
    size = rows * width
    out = pl.pallas_call(
        functools.partial(add_kernel, len(xs)),
        out_shape=[jax.ShapeDtypeStruct((rows // pieces, width), bf16)] * pieces,
        in_specs=[VMEM] * len(xs),
        out_specs=[VMEM] * pieces,
        compiler_params=SMALL,
        cost_estimate=pl.CostEstimate(
            flops=size * len(xs), bytes_accessed=2 * size * (len(xs) + 1), transcendentals=0
        ),
    )(*xs)
    return out[0] if pieces == 1 else out


def scatter_direct(chunks, axis):
    return [chunks[0]] + [fetch(chunks[k], axis, -k) for k in range(1, SIZES[axis])]


def scatter_ring(chunks, axis):
    n = SIZES[axis]
    h = n // 2
    up = fetch(chunks[h], axis, -1)
    down = fetch(chunks[h + 1], axis, 1)
    for k in range(h - 1, 0, -1):
        up = fetch(add([chunks[k], up]), axis, -1)
        if k > 1:
            down = fetch(add([chunks[n - k + 1], down]), axis, 1)
    return [chunks[0], up, down]


def attention_kernel(t_ref, q_ref, kp_ref, qp_ref, *refs):
    kvs, w_any, outs = refs[:8], refs[8], refs[9:13]
    w_ref, kv_ref, q_all, sem = refs[13:]
    copy = pltpu.make_async_copy(w_any, w_ref, sem)
    copy.start()
    t = t_ref[0]
    quarter = q_ref.shape[0] // 4
    rows = [
        q_ref[pl.ds(pl.multiple_of((t ^ k) * quarter, quarter), quarter), :] for k in range(4)
    ]
    q = jnp.concatenate(rows, axis=0)
    tokens = q.shape[0]
    q = jnp.concatenate([q[:, g * HEAD_DIM : (g + 1) * HEAD_DIM] for g in range(GROUP)], axis=0)
    qp = qp_ref[...]
    total_rows = GROUP * tokens
    top = jnp.full((total_rows, 1), FLOOR, f32)
    total = jnp.zeros((total_rows, 1), f32)
    acc = jnp.zeros((total_rows, HEAD_DIM), f32)
    for j in range(8):
        kv_ref[j] = kvs[j][...]
    q_all[...] = q

    def step(j, carry):
        top, total, acc = carry
        k = kv_ref[j, :, :HEAD_DIM]
        v = kv_ref[j, :, HEAD_DIM:]
        count = k.shape[0]
        score = lax.dot_general(
            q_all[...], k, (((1,), (1,)), ((), ())), preferred_element_type=f32
        )
        score = score * (HEAD_DIM**-0.5 * EXP2)
        visible = kp_ref[pl.ds(j, 1), :] <= qp
        score = jnp.where(visible[None], score.reshape(GROUP, tokens, count), NEG)
        score = score.reshape(total_rows, count)
        new_top = jnp.maximum(top, jnp.max(score, axis=-1, keepdims=True))
        weight = jnp.exp2(score - new_top)
        keep = jnp.exp2(top - new_top)
        total = total * keep + jnp.sum(weight, axis=-1, keepdims=True)
        acc = acc * keep + jnp.dot(weight.astype(bf16), v, preferred_element_type=f32)
        return new_top, total, acc

    top, total, acc = lax.fori_loop(0, 8, step, (top, total, acc))
    summed = (acc / total).astype(bf16)
    heads = jnp.concatenate([summed[g * tokens : (g + 1) * tokens] for g in range(GROUP)], axis=1)
    copy.wait()
    width = 512

    @pl.loop(0, w_ref.shape[1] // width)
    def _(n):
        cols = pl.ds(pl.multiple_of(n * width, width), width)
        part = jnp.dot(heads, w_ref[:, cols], preferred_element_type=f32).astype(bf16)
        for k in range(4):
            outs[k][:, cols] = part[k * quarter : (k + 1) * quarter]


def norm_kernel(p0, p1, p2, p3, residual, gain, gate_w, attended, first, second, prob):
    head_sum = p0[...].astype(f32) + p1[...].astype(f32) + p2[...].astype(f32) + p3[...].astype(f32)
    kept = (residual[...].astype(f32) + head_sum).astype(bf16)
    attended[...] = kept
    wide = kept.astype(f32)
    mean_square = jnp.mean(wide * wide, axis=-1, keepdims=True)
    normed = (wide * lax.rsqrt(mean_square + 1e-06) * gain[...].astype(f32)).astype(bf16)
    half = first.shape[0]
    first[...] = normed[:half]
    second[...] = normed[half:]
    logit = jnp.sum(normed.astype(f32) * gate_w[...].astype(f32), axis=-1, keepdims=True)
    prob[...] = jnp.broadcast_to(1.0 / (1.0 + jnp.exp(-logit)), prob.shape)


def send_kernel(core_ref, g_any, u_any, d_any, out_any, sems):
    n = out_any.shape[0] // 3
    at = pl.multiple_of(core_ref[0] * n, n)
    copies = [
        pltpu.make_async_copy(w.at[pl.ds(at, n)], out_any.at[pl.ds(i * n, n)], sems.at[i])
        for i, w in enumerate((g_any, u_any, d_any))
    ]
    for copy in copies:
        copy.start()
    for copy in copies:
        copy.wait()


def assemble_kernel(g_any, u_any, d_any, a_any, b_any, w_ref, d_ref, sems):
    own = g_any.shape[0]
    swap = a_any.shape[0] // 3
    block = 128
    copies = []

    def start(src, at, dst, to, n):
        copy = pltpu.make_async_copy(
            src.at[pl.ds(at, n)], dst.at[pl.ds(to, n)], sems.at[len(copies)]
        )
        copy.start()
        copies.append(copy)

    for part in range(2):
        pos = 0
        for source, at, length in (
            ((g_any, u_any)[part], 0, own),
            (a_any, part * swap, swap),
            (b_any, part * swap, swap),
        ):
            done = 0
            while done < length:
                b, inside = divmod(pos, block)
                n = min(block - inside, length - done)
                start(source, at + done, w_ref, b * 2 * block + part * block + inside, n)
                done += n
                pos += n
    start(d_any, 0, d_ref, 0, own)
    start(a_any, 2 * swap, d_ref, own, swap)
    start(b_any, 2 * swap, d_ref, own + swap, swap)
    for copy in copies:
        copy.wait()


def expert_kernel(count, *refs):
    xs, w_ref, d_ref, outs = refs[:count], refs[count], refs[count + 1], refs[count + 2 : -2]
    x_ref, h_ref = refs[-2:]
    n = xs[0].shape[0]
    for i, x in enumerate(xs):
        x_ref[i * n : (i + 1) * n, :] = x[...]
    block = 128

    @pl.loop(0, w_ref.shape[0] // (2 * block))
    def _(b):
        both = lax.dot_general(
            x_ref[...],
            w_ref[pl.ds(pl.multiple_of(b * 2 * block, 2 * block), 2 * block), :],
            (((1,), (1,)), ((), ())),
            preferred_element_type=f32,
        )
        gate, up = both[:, :block], both[:, block:]
        value = (gate / (1.0 + jnp.exp(-gate)) * up).astype(bf16)
        h_ref[:, pl.ds(pl.multiple_of(b * block, block), block)] = value

    width = 512

    @pl.loop(0, d_ref.shape[1] // width)
    def _(c):
        cols = pl.ds(pl.multiple_of(c * width, width), width)
        part = jnp.dot(h_ref[...], d_ref[:, cols], preferred_element_type=f32).astype(bf16)
        for i, out in enumerate(outs):
            out[:, cols] = part[i * n : (i + 1) * n]


def join_kernel(*refs):
    out = refs[-1]
    n = refs[0].shape[0]
    for i, ref in enumerate(refs[:-1]):
        out[i * n : (i + 1) * n, :] = ref[...]


def join(xs):
    rows, width = xs[0].shape
    return pl.pallas_call(
        join_kernel,
        out_shape=jax.ShapeDtypeStruct((rows * len(xs), width), bf16),
        in_specs=[VMEM] * len(xs),
        out_specs=VMEM,
        compiler_params=SMALL,
        cost_estimate=pl.CostEstimate(
            flops=0, bytes_accessed=4 * rows * len(xs) * width, transcendentals=0
        ),
    )(*xs)


def expert(xs, weights):
    w, d = weights
    rows, width = sum(x.shape[0] for x in xs), xs[0].shape[1]
    units = d.shape[0]
    return pl.pallas_call(
        functools.partial(expert_kernel, len(xs)),
        out_shape=[jax.ShapeDtypeStruct(x.shape, bf16) for x in xs],
        in_specs=[VMEM] * (len(xs) + 2),
        out_specs=[VMEM] * len(xs),
        scratch_shapes=[pltpu.VMEM((rows, width), bf16), pltpu.VMEM((rows, units), bf16)],
        compiler_params=pltpu.CompilerParams(vmem_limit_bytes=30 << 20),
        cost_estimate=pl.CostEstimate(
            flops=6 * rows * units * width,
            bytes_accessed=6 * units * width + 4 * rows * width,
            transcendentals=rows * units,
        ),
    )(*xs, w, d)


def final_kernel(*refs):
    attended, prob = refs[:2]
    first, second, out = refs[2:6], refs[6:14], refs[14]
    half = first[0].shape[0]

    def total(terms):
        t = terms[0][...].astype(f32)
        for term in terms[1:]:
            t += term[...].astype(f32)
        return t

    for i, terms in enumerate((first, second)):
        rows = slice(i * half, (i + 1) * half)
        out[rows, :] = (
            attended[rows, :].astype(f32) + prob[rows, :1] * total(terms)
        ).astype(bf16)


def per_device(
    queries,
    keys,
    values,
    block_table,
    residual,
    out_weight,
    norm_gain,
    gate_logit_weight,
    gate_weight,
    up_weight,
    down_weight,
):
    tokens = queries.shape[0]
    half = tokens // 2
    quarter = tokens // 4
    width = residual.shape[1]
    hidden = down_weight.shape[0]
    y, z, xh = (lax.axis_index(a) for a in CTX)
    core = lax.axis_index("core")
    t = lax.axis_index(TP)

    gate_t, up_t = gate_weight.T, up_weight.T
    piece = hidden // 2
    to_send = pl.pallas_call(
        send_kernel,
        out_shape=jax.ShapeDtypeStruct((3 * piece, width), bf16),
        in_specs=[SMEM, HBM, HBM, HBM],
        out_specs=VMEM,
        scratch_shapes=[pltpu.SemaphoreType.DMA((3,))],
        cost_estimate=pl.CostEstimate(
            flops=0, bytes_accessed=12 * piece * width, transcendentals=0
        ),
    )(core.astype(jnp.int32)[None], gate_t, up_t, down_weight)
    swap_a = lax.ppermute(to_send, ("xh", "xl"), [(0, 3), (3, 0), (1, 2), (2, 1)])

    kv = jnp.concatenate([keys, values], axis=1)
    along_z = jnp.concatenate(gather_direct(kv, "z"), axis=0)
    across = fetch(along_z, "xh", 1)
    kvs = gather_direct(along_z, "y") + gather_direct(across, "y")

    ids = jnp.arange(64, dtype=jnp.int32)
    slot = (
        ((y + (ids // 8) % 4) % 4 * 8 + (z + ids % 8) % 8) * 2 + (xh + ids // 32) % 2
    ).astype(jnp.int32)
    all_slots = jnp.arange(block_table.shape[0], dtype=jnp.int32)
    mirror = 2 * block_table.shape[0] - 1

    def pair_of(s):
        onehot = (s[:, None] == all_slots[None, :]).astype(jnp.int32)
        return jnp.sum(onehot * block_table[None, :], axis=1)

    def place(pair, local):
        return jnp.where(local < half, pair * half + local, (mirror - pair) * half + local - half)

    pairs = pair_of(slot)
    local = jnp.arange(tokens, dtype=jnp.int32)
    key_place = place(pairs[:, None], local[None, :]).reshape(8, 8 * tokens)
    rel = jnp.arange(tokens, dtype=jnp.int32)
    own_local = ((rel // quarter) ^ t.astype(jnp.int32)) * quarter + rel % quarter
    query_place = place(pairs[0], own_local)[:, None]

    rows = GROUP * tokens
    span = 64 * tokens
    partial = pl.pallas_call(
        attention_kernel,
        out_shape=[jax.ShapeDtypeStruct((quarter, width), bf16)] * 4,
        in_specs=[SMEM, VMEM, VMEM, VMEM] + [VMEM] * 8 + [HBM],
        out_specs=[VMEM] * 4,
        scratch_shapes=[
            pltpu.VMEM(out_weight.shape, bf16),
            pltpu.VMEM((8, 8 * tokens, 2 * HEAD_DIM), bf16),
            pltpu.VMEM((GROUP * tokens, HEAD_DIM), bf16),
            pltpu.SemaphoreType.DMA,
        ],
        compiler_params=pltpu.CompilerParams(vmem_limit_bytes=46 << 20),
        cost_estimate=pl.CostEstimate(
            flops=4 * rows * span * HEAD_DIM + 2 * tokens * out_weight.size,
            bytes_accessed=2 * out_weight.size + 4 * span * HEAD_DIM,
            transcendentals=rows * span,
        ),
    )(t.astype(jnp.int32)[None], queries, key_place, query_place, *kvs, out_weight)

    terms = [partial[0]] + [
        lax.ppermute(partial[k], TP, [(i, i ^ k) for i in range(4)]) for k in (1, 2, 3)
    ]
    eighth = quarter // 2
    attended, first, second, prob = pl.pallas_call(
        norm_kernel,
        out_shape=[
            jax.ShapeDtypeStruct((quarter, width), bf16),
            jax.ShapeDtypeStruct((eighth, width), bf16),
            jax.ShapeDtypeStruct((eighth, width), bf16),
            jax.ShapeDtypeStruct((quarter, 128), f32),
        ],
        in_specs=[VMEM] * 7,
        out_specs=[VMEM] * 4,
        compiler_params=SMALL,
        cost_estimate=pl.CostEstimate(
            flops=10 * quarter * width, bytes_accessed=14 * quarter * width, transcendentals=quarter
        ),
    )(*terms, residual, norm_gain[None, :], gate_logit_weight[None, :])

    first_y = join(gather_direct(first, "y"))
    second_z = join(gather_direct(second, "z"))
    first_all = gather_ring(first_y, "z")
    swap_a, second_z = lax.optimization_barrier((swap_a, second_z))
    second_all = gather_direct(second_z, "y")
    swap_b = fetch(swap_a, "core", 1)
    weights = pl.pallas_call(
        assemble_kernel,
        out_shape=[
            jax.ShapeDtypeStruct((4 * hidden, width), bf16),
            jax.ShapeDtypeStruct((2 * hidden, width), bf16),
        ],
        in_specs=[HBM] * 5,
        out_specs=[VMEM] * 2,
        scratch_shapes=[pltpu.SemaphoreType.DMA((24,))],
        compiler_params=pltpu.CompilerParams(vmem_limit_bytes=16 << 20),
        cost_estimate=pl.CostEstimate(
            flops=0, bytes_accessed=12 * hidden * width, transcendentals=0
        ),
    )(gate_t, up_t, down_weight, swap_a, swap_b)
    first_parts = expert(first_all, weights)
    second_parts = expert(second_all, weights)

    first_sum = add(scatter_ring(first_parts, "z"), pieces=4)
    second_sum = add(scatter_direct(second_parts, "y"), pieces=8)
    first_terms = scatter_direct(first_sum, "y")
    second_terms = scatter_direct(second_sum, "z")
    return pl.pallas_call(
        final_kernel,
        out_shape=jax.ShapeDtypeStruct((quarter, width), bf16),
        in_specs=[VMEM] * 14,
        out_specs=VMEM,
        compiler_params=SMALL,
        cost_estimate=pl.CostEstimate(
            flops=10 * quarter * width, bytes_accessed=16 * quarter * width, transcendentals=0
        ),
    )(attended, prob, *first_terms, *second_terms)


def solution(mesh):
    fine = Mesh(mesh.devices.reshape(tuple(SIZES.values())), tuple(SIZES))
    return jax.shard_map(
        per_device,
        mesh=fine,
        in_specs=(
            P(CTX, TP),
            P(CTX, TP),
            P(CTX, TP),
            P(),
            P(CTX + TP, None),
            P(TP, None),
            P(),
            P(),
            P(None, CTX),
            P(None, CTX),
            P(CTX, None),
        ),
        out_specs=P(CTX + TP, None),
        check_vma=False,
    )
```

```python
import functools

import jax
import jax.numpy as jnp
from jax import lax
from jax.experimental import pallas as pl
from jax.experimental.pallas import tpu as pltpu
from jax.sharding import Mesh
from jax.sharding import PartitionSpec as P

HEADS = 28
KV_HEADS = 4
HEAD_DIM = 128
GROUP = HEADS // KV_HEADS
SIZES = {"y": 4, "z": 8, "xh": 2, "xl": 2, "core": 2}
CTX = ("y", "z", "xh")
TP = ("xl", "core")
f32 = jnp.float32
bf16 = jnp.bfloat16
VMEM = pl.BlockSpec(memory_space=pltpu.VMEM)
SMEM = pl.BlockSpec(memory_space=pltpu.SMEM)
HBM = pl.BlockSpec(memory_space=pltpu.HBM)
SMALL = pltpu.CompilerParams(vmem_limit_bytes=8 << 20)
NEG = -1e30
FLOOR = -1e29
EXP2 = 1.4426950408889634


def fetch(x, axis, k):
    n = SIZES[axis]
    k %= n
    if k == 0:
        return x
    return lax.ppermute(x, axis, [((i + k) % n, i) for i in range(n)])


def gather_direct(x, axis):
    return [fetch(x, axis, k) for k in range(SIZES[axis])]


def add_kernel(n_in, *refs):
    ins, outs = refs[:n_in], refs[n_in:]
    rows = outs[0].shape[0]
    for i, out in enumerate(outs):
        part = ins[0][i * rows : (i + 1) * rows, :].astype(f32)
        for other in ins[1:]:
            part += other[i * rows : (i + 1) * rows, :].astype(f32)
        out[...] = part.astype(out.dtype)


def add(xs, pieces=1):
    rows, width = xs[0].shape
    size = rows * width
    out = pl.pallas_call(
        functools.partial(add_kernel, len(xs)),
        out_shape=[jax.ShapeDtypeStruct((rows // pieces, width), bf16)] * pieces,
        in_specs=[VMEM] * len(xs),
        out_specs=[VMEM] * pieces,
        compiler_params=SMALL,
        cost_estimate=pl.CostEstimate(
            flops=size * len(xs), bytes_accessed=2 * size * (len(xs) + 1), transcendentals=0
        ),
    )(*xs)
    return out[0] if pieces == 1 else out


def scatter_direct(chunks, axis):
    return [chunks[0]] + [fetch(chunks[k], axis, -k) for k in range(1, SIZES[axis])]


def scatter_halving(low, high, axis):
    k = SIZES[axis] // 2
    while k > 1:
        low, high = add([low, fetch(high, axis, -k)], pieces=2)
        k //= 2
    return [low, fetch(high, axis, -1)]


def scatter_ring(chunks, axis):
    n = SIZES[axis]
    h = n // 2
    up = fetch(chunks[h], axis, -1)
    down = fetch(chunks[h + 1], axis, 1)
    for k in range(h - 1, 0, -1):
        up = fetch(add([chunks[k], up]), axis, -1)
        if k > 1:
            down = fetch(add([chunks[n - k + 1], down]), axis, 1)
    return [chunks[0], up, down]


def attention_kernel(t_ref, pair_ref, q_ref, kp_ref, *refs):
    kvs, w_any, outs = refs[:8], refs[8], refs[9:13]
    w_ref, kv_ref, q_all, sem = refs[13:]
    copy = pltpu.make_async_copy(w_any, w_ref, sem)
    copy.start()
    t = t_ref[0]
    quarter = q_ref.shape[0] // 4
    rows = [
        q_ref[pl.ds(pl.multiple_of((t ^ k) * quarter, quarter), quarter), :] for k in range(4)
    ]
    q = jnp.concatenate(rows, axis=0)
    tokens = q.shape[0]
    q = jnp.concatenate([q[:, g * HEAD_DIM : (g + 1) * HEAD_DIM] for g in range(GROUP)], axis=0)
    half = tokens // 2
    row = lax.broadcasted_iota(jnp.int32, (tokens, 1), 0)
    local = (row // quarter ^ t) * quarter + row % quarter
    pair = pair_ref[0]
    mirror = 2 * 8 * kp_ref.shape[0] - 1
    qp = jnp.where(local < half, pair * half + local, (mirror - pair) * half + local - half)
    total_rows = GROUP * tokens
    top = jnp.full((total_rows, 1), FLOOR, f32)
    total = jnp.zeros((total_rows, 1), f32)
    acc = jnp.zeros((total_rows, HEAD_DIM), f32)
    for j in range(8):
        kv_ref[j] = kvs[j][...]
    q_all[...] = q

    def step(j, carry):
        top, total, acc = carry
        k = kv_ref[j, :, :HEAD_DIM]
        v = kv_ref[j, :, HEAD_DIM:]
        count = k.shape[0]
        score = lax.dot_general(
            q_all[...], k, (((1,), (1,)), ((), ())), preferred_element_type=f32
        )
        score = score * (HEAD_DIM**-0.5 * EXP2)
        visible = kp_ref[pl.ds(j, 1), :] <= qp
        score = jnp.where(visible[None], score.reshape(GROUP, tokens, count), NEG)
        score = score.reshape(total_rows, count)
        new_top = jnp.maximum(top, jnp.max(score, axis=-1, keepdims=True))
        weight = jnp.exp2(score - new_top)
        keep = jnp.exp2(top - new_top)
        total = total * keep + jnp.sum(weight, axis=-1, keepdims=True)
        acc = acc * keep + jnp.dot(weight.astype(bf16), v, preferred_element_type=f32)
        return new_top, total, acc

    top, total, acc = lax.fori_loop(0, 8, step, (top, total, acc))
    summed = (acc / total).astype(bf16)
    heads = jnp.concatenate([summed[g * tokens : (g + 1) * tokens] for g in range(GROUP)], axis=1)
    copy.wait()
    width = 512

    @pl.loop(0, w_ref.shape[1] // width)
    def _(n):
        cols = pl.ds(pl.multiple_of(n * width, width), width)
        part = jnp.dot(heads, w_ref[:, cols], preferred_element_type=f32).astype(bf16)
        for k in range(4):
            outs[k][:, cols] = part[k * quarter : (k + 1) * quarter]


def norm_kernel(p0, p1, p2, p3, residual, gain, gate_w, attended, first, second, prob):
    head_sum = p0[...].astype(f32) + p1[...].astype(f32) + p2[...].astype(f32) + p3[...].astype(f32)
    kept = (residual[...].astype(f32) + head_sum).astype(bf16)
    attended[...] = kept
    wide = kept.astype(f32)
    mean_square = jnp.mean(wide * wide, axis=-1, keepdims=True)
    normed = (wide * lax.rsqrt(mean_square + 1e-06) * gain[...].astype(f32)).astype(bf16)
    half = first.shape[0]
    first[...] = normed[:half]
    second[...] = normed[half:]
    logit = jnp.sum(normed.astype(f32) * gate_w[...].astype(f32), axis=-1, keepdims=True)
    prob[...] = jnp.broadcast_to(1.0 / (1.0 + jnp.exp(-logit)), prob.shape)


def send_kernel(core_ref, g_any, u_any, d_any, out_any, sems):
    n = out_any.shape[0] // 3
    at = pl.multiple_of(core_ref[0] * n, n)
    copies = [
        pltpu.make_async_copy(w.at[pl.ds(at, n)], out_any.at[pl.ds(i * n, n)], sems.at[i])
        for i, w in enumerate((g_any, u_any, d_any))
    ]
    for copy in copies:
        copy.start()
    for copy in copies:
        copy.wait()


def assemble_kernel(g_any, u_any, d_any, a_any, b_any, w_ref, d_ref, sems):
    own = g_any.shape[0]
    swap = a_any.shape[0] // 3
    block = 128
    copies = []

    def start(src, at, dst, to, n):
        copy = pltpu.make_async_copy(
            src.at[pl.ds(at, n)], dst.at[pl.ds(to, n)], sems.at[len(copies)]
        )
        copy.start()
        copies.append(copy)

    for part in range(2):
        pos = 0
        for source, at, length in (
            ((g_any, u_any)[part], 0, own),
            (a_any, part * swap, swap),
            (b_any, part * swap, swap),
        ):
            done = 0
            while done < length:
                b, inside = divmod(pos, block)
                n = min(block - inside, length - done)
                start(source, at + done, w_ref, b * 2 * block + part * block + inside, n)
                done += n
                pos += n
    start(d_any, 0, d_ref, 0, own)
    start(a_any, 2 * swap, d_ref, own, swap)
    start(b_any, 2 * swap, d_ref, own + swap, swap)
    for copy in copies:
        copy.wait()


def expert_kernel(count, *refs):
    xs, w_ref, d_ref, outs = refs[:count], refs[count], refs[count + 1], refs[count + 2 : -2]
    x_ref, h_ref = refs[-2:]
    n = xs[0].shape[0]
    for i, x in enumerate(xs):
        x_ref[i * n : (i + 1) * n, :] = x[...]
    block = 128

    @pl.loop(0, w_ref.shape[0] // (2 * block))
    def _(b):
        both = lax.dot_general(
            x_ref[...],
            w_ref[pl.ds(pl.multiple_of(b * 2 * block, 2 * block), 2 * block), :],
            (((1,), (1,)), ((), ())),
            preferred_element_type=f32,
        )
        gate, up = both[:, :block], both[:, block:]
        value = (gate / (1.0 + jnp.exp(-gate)) * up).astype(bf16)
        h_ref[:, pl.ds(pl.multiple_of(b * block, block), block)] = value

    width = 512

    @pl.loop(0, d_ref.shape[1] // width)
    def _(c):
        cols = pl.ds(pl.multiple_of(c * width, width), width)
        part = jnp.dot(h_ref[...], d_ref[:, cols], preferred_element_type=f32).astype(bf16)
        for i, out in enumerate(outs):
            out[:, cols] = part[i * n : (i + 1) * n]


def join_kernel(*refs):
    out = refs[-1]
    n = refs[0].shape[0]
    for i, ref in enumerate(refs[:-1]):
        out[i * n : (i + 1) * n, :] = ref[...]


def join(xs):
    rows, width = xs[0].shape
    return pl.pallas_call(
        join_kernel,
        out_shape=jax.ShapeDtypeStruct((rows * len(xs), width), bf16),
        in_specs=[VMEM] * len(xs),
        out_specs=VMEM,
        compiler_params=SMALL,
        cost_estimate=pl.CostEstimate(
            flops=0, bytes_accessed=4 * rows * len(xs) * width, transcendentals=0
        ),
    )(*xs)


def expert(xs, weights):
    w, d = weights
    rows, width = sum(x.shape[0] for x in xs), xs[0].shape[1]
    units = d.shape[0]
    return pl.pallas_call(
        functools.partial(expert_kernel, len(xs)),
        out_shape=[jax.ShapeDtypeStruct(x.shape, bf16) for x in xs],
        in_specs=[VMEM] * (len(xs) + 2),
        out_specs=[VMEM] * len(xs),
        scratch_shapes=[pltpu.VMEM((rows, width), bf16), pltpu.VMEM((rows, units), bf16)],
        compiler_params=pltpu.CompilerParams(vmem_limit_bytes=30 << 20),
        cost_estimate=pl.CostEstimate(
            flops=6 * rows * units * width,
            bytes_accessed=6 * units * width + 4 * rows * width,
            transcendentals=rows * units,
        ),
    )(*xs, w, d)


def final_kernel(*refs):
    attended, prob = refs[:2]
    first, second, out = refs[2:6], refs[6:8], refs[8]
    half = first[0].shape[0]

    def total(terms):
        t = terms[0][...].astype(f32)
        for term in terms[1:]:
            t += term[...].astype(f32)
        return t

    for i, terms in enumerate((first, second)):
        rows = slice(i * half, (i + 1) * half)
        out[rows, :] = (
            attended[rows, :].astype(f32) + prob[rows, :1] * total(terms)
        ).astype(bf16)


def per_device(
    queries,
    keys,
    values,
    block_table,
    residual,
    out_weight,
    norm_gain,
    gate_logit_weight,
    gate_weight,
    up_weight,
    down_weight,
):
    tokens = queries.shape[0]
    half = tokens // 2
    quarter = tokens // 4
    width = residual.shape[1]
    hidden = down_weight.shape[0]
    y, z, xh = (lax.axis_index(a) for a in CTX)
    core = lax.axis_index("core")
    t = lax.axis_index(TP)

    gate_t, up_t = gate_weight.T, up_weight.T
    piece = hidden // 2
    to_send = pl.pallas_call(
        send_kernel,
        out_shape=jax.ShapeDtypeStruct((3 * piece, width), bf16),
        in_specs=[SMEM, HBM, HBM, HBM],
        out_specs=VMEM,
        scratch_shapes=[pltpu.SemaphoreType.DMA((3,))],
        cost_estimate=pl.CostEstimate(
            flops=0, bytes_accessed=12 * piece * width, transcendentals=0
        ),
    )(core.astype(jnp.int32)[None], gate_t, up_t, down_weight)
    swap_a = lax.ppermute(to_send, ("xh", "xl"), [(0, 3), (3, 0), (1, 2), (2, 1)])

    kv = jnp.concatenate([keys, values], axis=1)
    along_z = kv
    for k in (1, 2, 4):
        along_z = jnp.concatenate([along_z, fetch(along_z, "z", k)], axis=0)
    across = fetch(along_z, "xh", 1)
    kvs = gather_direct(along_z, "y") + gather_direct(across, "y")

    ids = jnp.arange(64, dtype=jnp.int32)
    slot = (
        ((y + (ids // 8) % 4) % 4 * 8 + (z + ids % 8) % 8) * 2 + (xh + ids // 32) % 2
    ).astype(jnp.int32)
    all_slots = jnp.arange(block_table.shape[0], dtype=jnp.int32)
    mirror = 2 * block_table.shape[0] - 1

    def pair_of(s):
        onehot = (s[:, None] == all_slots[None, :]).astype(jnp.int32)
        return jnp.sum(onehot * block_table[None, :], axis=1)

    def place(pair, local):
        return jnp.where(local < half, pair * half + local, (mirror - pair) * half + local - half)

    pairs = pair_of(slot)
    local = jnp.arange(tokens, dtype=jnp.int32)
    key_place = place(pairs[:, None], local[None, :]).reshape(8, 8 * tokens)
    rows = GROUP * tokens
    span = 64 * tokens
    partial = pl.pallas_call(
        attention_kernel,
        out_shape=[jax.ShapeDtypeStruct((quarter, width), bf16)] * 4,
        in_specs=[SMEM, SMEM, VMEM, VMEM] + [VMEM] * 8 + [HBM],
        out_specs=[VMEM] * 4,
        scratch_shapes=[
            pltpu.VMEM(out_weight.shape, bf16),
            pltpu.VMEM((8, 8 * tokens, 2 * HEAD_DIM), bf16),
            pltpu.VMEM((GROUP * tokens, HEAD_DIM), bf16),
            pltpu.SemaphoreType.DMA,
        ],
        compiler_params=pltpu.CompilerParams(vmem_limit_bytes=46 << 20),
        cost_estimate=pl.CostEstimate(
            flops=4 * rows * span * HEAD_DIM + 2 * tokens * out_weight.size,
            bytes_accessed=2 * out_weight.size + 4 * span * HEAD_DIM,
            transcendentals=rows * span,
        ),
    )(t.astype(jnp.int32)[None], pairs[:1], queries, key_place, *kvs, out_weight)

    terms = [partial[0]] + [
        lax.ppermute(partial[k], TP, [(i, i ^ k) for i in range(4)]) for k in (1, 2, 3)
    ]
    eighth = quarter // 2
    attended, first, second, prob = pl.pallas_call(
        norm_kernel,
        out_shape=[
            jax.ShapeDtypeStruct((quarter, width), bf16),
            jax.ShapeDtypeStruct((eighth, width), bf16),
            jax.ShapeDtypeStruct((eighth, width), bf16),
            jax.ShapeDtypeStruct((quarter, 128), f32),
        ],
        in_specs=[VMEM] * 7,
        out_specs=[VMEM] * 4,
        compiler_params=SMALL,
        cost_estimate=pl.CostEstimate(
            flops=10 * quarter * width, bytes_accessed=14 * quarter * width, transcendentals=quarter
        ),
    )(*terms, residual, norm_gain[None, :], gate_logit_weight[None, :])

    first_y = join(gather_direct(first, "y"))
    second_z = join([second, fetch(second, "z", 1)])
    second_z, _ = lax.optimization_barrier((second_z, first_y))
    ahead = [first_y, fetch(first_y, "z", 1)]
    behind = [fetch(first_y, "z", -1)]
    second_z = join([second_z, fetch(second_z, "z", 2)])
    second_z, _ = lax.optimization_barrier((second_z, (ahead[1], behind[0])))
    ahead.append(fetch(ahead[1], "z", 1))
    behind.append(fetch(behind[0], "z", -1))
    second_z = join([second_z, fetch(second_z, "z", 4)])
    ahead.append(fetch(ahead[2], "z", 1))
    behind.append(fetch(behind[1], "z", -1))
    second_all = gather_direct(second_z, "y")
    swap_a, _ = lax.optimization_barrier((swap_a, second_z))
    swap_b = fetch(swap_a, "core", 1)
    weights = pl.pallas_call(
        assemble_kernel,
        out_shape=[
            jax.ShapeDtypeStruct((4 * hidden, width), bf16),
            jax.ShapeDtypeStruct((2 * hidden, width), bf16),
        ],
        in_specs=[HBM] * 5,
        out_specs=[VMEM] * 2,
        scratch_shapes=[pltpu.SemaphoreType.DMA((24,))],
        compiler_params=pltpu.CompilerParams(vmem_limit_bytes=16 << 20),
        cost_estimate=pl.CostEstimate(
            flops=0, bytes_accessed=12 * hidden * width, transcendentals=0
        ),
    )(gate_t, up_t, down_weight, swap_a, swap_b)
    last, weights = lax.optimization_barrier((ahead[3], weights))
    first_all = ahead + [fetch(last, "z", 1)] + behind[::-1]
    first_parts = expert(first_all, weights)
    second_parts = expert(second_all, weights)

    first_sum = add(scatter_ring(first_parts, "z"), pieces=4)
    second_sum = add(scatter_direct(second_parts, "y"), pieces=2)
    first_terms = scatter_direct(first_sum, "y")
    second_terms = scatter_halving(*second_sum, "z")
    return pl.pallas_call(
        final_kernel,
        out_shape=jax.ShapeDtypeStruct((quarter, width), bf16),
        in_specs=[VMEM] * 8,
        out_specs=VMEM,
        compiler_params=SMALL,
        cost_estimate=pl.CostEstimate(
            flops=10 * quarter * width, bytes_accessed=16 * quarter * width, transcendentals=0
        ),
    )(attended, prob, *first_terms, *second_terms)


def solution(mesh):
    fine = Mesh(mesh.devices.reshape(tuple(SIZES.values())), tuple(SIZES))
    return jax.shard_map(
        per_device,
        mesh=fine,
        in_specs=(
            P(CTX, TP),
            P(CTX, TP),
            P(CTX, TP),
            P(),
            P(CTX + TP, None),
            P(TP, None),
            P(),
            P(),
            P(None, CTX),
            P(None, CTX),
            P(CTX, None),
        ),
        out_specs=P(CTX + TP, None),
        check_vma=False,
    )
```

```python
import functools

import jax
import jax.numpy as jnp
from jax import lax
from jax.experimental import pallas as pl
from jax.experimental.pallas import tpu as pltpu
from jax.sharding import Mesh
from jax.sharding import PartitionSpec as P

HEADS = 28
KV_HEADS = 4
HEAD_DIM = 128
GROUP = HEADS // KV_HEADS
SIZES = {"y": 4, "z": 8, "xh": 2, "xl": 2, "core": 2}
CTX = ("y", "z", "xh")
TP = ("xl", "core")
f32 = jnp.float32
bf16 = jnp.bfloat16
VMEM = pl.BlockSpec(memory_space=pltpu.VMEM)
SMEM = pl.BlockSpec(memory_space=pltpu.SMEM)
HBM = pl.BlockSpec(memory_space=pltpu.HBM)
SMALL = pltpu.CompilerParams(vmem_limit_bytes=8 << 20)
NEG = -1e30
FLOOR = -1e29
EXP2 = 1.4426950408889634


def fetch(x, axis, k):
    n = SIZES[axis]
    k %= n
    if k == 0:
        return x
    return lax.ppermute(x, axis, [((i + k) % n, i) for i in range(n)])


def gather_direct(x, axis):
    return [fetch(x, axis, k) for k in range(SIZES[axis])]


def gather_ring(x, axis):
    n = SIZES[axis]
    h = n // 2
    ahead, behind = [x], [x]
    for k in range(1, h):
        ahead.append(fetch(ahead[-1], axis, 1))
        behind.append(fetch(behind[-1], axis, -1))
    rows = x.shape[0] // 2
    far = [fetch(ahead[-1][:rows], axis, 1), fetch(behind[-1][rows:], axis, -1)]
    return ahead, behind, far


def add_kernel(n_in, first, *refs):
    ins, outs = refs[:n_in], refs[n_in:]
    rows = outs[0].shape[0]
    for i, out in enumerate(outs):
        part = ins[0][i * rows : (i + 1) * rows, :].astype(f32)
        for other in ins[1:]:
            if other.shape[0] == ins[0].shape[0]:
                part += other[i * rows : (i + 1) * rows, :].astype(f32)
        out[...] = part.astype(out.dtype)
    last = ins[-1]
    if last.shape[0] < ins[0].shape[0]:
        mine = slice(first, first + last.shape[0])
        outs[0][mine, :] = (ins[0][mine, :].astype(f32) + last[...].astype(f32)).astype(bf16)


def add(xs, pieces=1, first=0):
    rows, width = xs[0].shape
    size = rows * width
    out = pl.pallas_call(
        functools.partial(add_kernel, len(xs), first),
        out_shape=[jax.ShapeDtypeStruct((rows // pieces, width), bf16)] * pieces,
        in_specs=[VMEM] * len(xs),
        out_specs=[VMEM] * pieces,
        compiler_params=SMALL,
        cost_estimate=pl.CostEstimate(
            flops=size * len(xs), bytes_accessed=2 * size * (len(xs) + 1), transcendentals=0
        ),
    )(*xs)
    return out[0] if pieces == 1 else out


def scatter_direct(chunks, axis):
    return [chunks[0]] + [fetch(chunks[k], axis, -k) for k in range(1, SIZES[axis])]


def scatter_ring(near, far, axis):
    n = SIZES[axis]
    h = n // 2
    up = fetch(far[0], axis, -1)
    down = fetch(far[1], axis, 1)
    for k in range(h - 1, 0, -1):
        first = near[k].shape[0] - down.shape[0]
        up = fetch(add([near[k], up]), axis, -1)
        down = fetch(add([near[n - k], down], first=first), axis, 1)
    return [near[0], up, down]


def attention_kernel(at_ref, table_ref, q_ref, *refs):
    kvs, w_any, keep_ref, send_ref = refs[:9], refs[9], refs[10], refs[11]
    w_ref, kv_ref, q_all, kp_ref, sems = refs[12:]
    half_rows = kvs[7].shape[0]
    places = [kv_ref.at[j] for j in (0, 1, 2, 3, 5, 6, 7)]
    places += [kv_ref.at[4, pl.ds(i * half_rows, half_rows)] for i in range(2)]
    copies = [
        pltpu.make_async_copy(src, dst, sems.at[i]) for i, (src, dst) in enumerate(zip(kvs, places))
    ]
    copy = pltpu.make_async_copy(w_any, w_ref, sems.at[9])
    for one in copies:
        one.start()
    copy.start()
    y, z, xh, t = (at_ref[i] for i in range(4))
    tokens = q_ref.shape[0]
    half = tokens // 2
    mirror = 2 * table_ref.shape[0] - 1

    def place(pair, local):
        return jnp.where(local < half, pair * half + local, (mirror - pair) * half + local - half)

    def pair_of(dy, dz, dx):
        slot = ((y + dy) % 4 * 8 + (z + dz) % 8) * 2 + (xh + dx) % 2
        return table_ref[slot]

    lane = lax.broadcasted_iota(jnp.int32, (1, 8 * tokens), 1)
    for j in range(8):
        pair = jnp.zeros_like(lane)
        for b in range(8):
            pair = jnp.where(lane // tokens == b, pair_of(b // 2, j, b % 2), pair)
        kp_ref[j : j + 1, :] = place(pair, lane % tokens)
    quarter = tokens // 4
    parts = [
        q_ref[pl.ds(pl.multiple_of((t ^ k) * quarter, quarter), quarter), :] for k in (0, 2, 1, 3)
    ]
    q = jnp.concatenate(parts, axis=0)
    q = jnp.concatenate([q[:, g * HEAD_DIM : (g + 1) * HEAD_DIM] for g in range(GROUP)], axis=0)
    row = lax.broadcasted_iota(jnp.int32, (tokens, 1), 0)
    order = row // quarter
    order = (order % 2) * 2 + order // 2
    qp = place(pair_of(0, 0, 0), (order ^ t) * quarter + row % quarter)
    total_rows = GROUP * tokens
    top = jnp.full((total_rows, 1), FLOOR, f32)
    total = jnp.zeros((total_rows, 1), f32)
    acc = jnp.zeros((total_rows, HEAD_DIM), f32)
    q_all[...] = q
    for one in copies:
        one.wait()

    def step(j, carry):
        top, total, acc = carry
        k = kv_ref[j, :, :HEAD_DIM]
        v = kv_ref[j, :, HEAD_DIM:]
        count = k.shape[0]
        score = lax.dot_general(
            q_all[...], k, (((1,), (1,)), ((), ())), preferred_element_type=f32
        )
        score = score * (HEAD_DIM**-0.5 * EXP2)
        visible = kp_ref[pl.ds(j, 1), :] <= qp
        score = jnp.where(visible[None], score.reshape(GROUP, tokens, count), NEG)
        score = score.reshape(total_rows, count)
        new_top = jnp.maximum(top, jnp.max(score, axis=-1, keepdims=True))
        weight = jnp.exp2(score - new_top)
        keep = jnp.exp2(top - new_top)
        total = total * keep + jnp.sum(weight, axis=-1, keepdims=True)
        acc = acc * keep + jnp.dot(weight.astype(bf16), v, preferred_element_type=f32)
        return new_top, total, acc

    top, total, acc = lax.fori_loop(0, 8, step, (top, total, acc))
    summed = (acc / total).astype(bf16)
    heads = jnp.concatenate([summed[g * tokens : (g + 1) * tokens] for g in range(GROUP)], axis=1)
    copy.wait()
    width = 512

    @pl.loop(0, w_ref.shape[1] // width)
    def _(n):
        cols = pl.ds(pl.multiple_of(n * width, width), width)
        part = jnp.dot(heads, w_ref[:, cols], preferred_element_type=f32).astype(bf16)
        keep_ref[:, cols] = part[:half]
        send_ref[:, cols] = part[half:]


def norm_kernel(keep, near, far, residual, gain, gate_w, attended, normed_ref, prob):
    rows = far.shape[0]
    head_sum = keep[:rows, :].astype(f32) + near[:rows, :].astype(f32) + far[...].astype(f32)
    kept = (residual[...].astype(f32) + head_sum).astype(bf16)
    attended[...] = kept
    wide = kept.astype(f32)
    mean_square = jnp.mean(wide * wide, axis=-1, keepdims=True)
    normed = (wide * lax.rsqrt(mean_square + 1e-06) * gain[...].astype(f32)).astype(bf16)
    normed_ref[...] = normed
    logit = jnp.sum(normed.astype(f32) * gate_w[...].astype(f32), axis=-1, keepdims=True)
    prob[...] = jnp.broadcast_to(1.0 / (1.0 + jnp.exp(-logit)), prob.shape)


def send_kernel(core_ref, g_any, u_any, d_any, out_any, sems):
    n = out_any.shape[0] // 3
    at = pl.multiple_of(core_ref[0] * n, n)
    copies = [
        pltpu.make_async_copy(w.at[pl.ds(at, n)], out_any.at[pl.ds(i * n, n)], sems.at[i])
        for i, w in enumerate((g_any, u_any, d_any))
    ]
    for copy in copies:
        copy.start()
    for copy in copies:
        copy.wait()


def assemble_kernel(g_any, u_any, d_any, a_any, b_any, w_ref, d_ref, sems):
    own = g_any.shape[0]
    swap = a_any.shape[0] // 3
    block = 128
    copies = []

    def start(src, at, dst, to, n):
        copy = pltpu.make_async_copy(
            src.at[pl.ds(at, n)], dst.at[pl.ds(to, n)], sems.at[len(copies)]
        )
        copy.start()
        copies.append(copy)

    for part in range(2):
        pos = 0
        for source, at, length in (
            ((g_any, u_any)[part], 0, own),
            (a_any, part * swap, swap),
            (b_any, part * swap, swap),
        ):
            done = 0
            while done < length:
                b, inside = divmod(pos, block)
                n = min(block - inside, length - done)
                start(source, at + done, w_ref, b * 2 * block + part * block + inside, n)
                done += n
                pos += n
    start(d_any, 0, d_ref, 0, own)
    start(a_any, 2 * swap, d_ref, own, swap)
    start(b_any, 2 * swap, d_ref, own + swap, swap)
    for copy in copies:
        copy.wait()


def expert_kernel(count, *refs):
    xs, w_ref, d_ref, outs = refs[:count], refs[count], refs[count + 1], refs[count + 2 : -2]
    x_ref, h_ref = refs[-2:]
    at = 0
    for x in xs:
        x_ref[at : at + x.shape[0], :] = x[...]
        at += x.shape[0]
    block = 128

    @pl.loop(0, w_ref.shape[0] // (2 * block))
    def _(b):
        both = lax.dot_general(
            x_ref[...],
            w_ref[pl.ds(pl.multiple_of(b * 2 * block, 2 * block), 2 * block), :],
            (((1,), (1,)), ((), ())),
            preferred_element_type=f32,
        )
        gate, up = both[:, :block], both[:, block:]
        value = (gate / (1.0 + jnp.exp(-gate)) * up).astype(bf16)
        h_ref[:, pl.ds(pl.multiple_of(b * block, block), block)] = value

    width = 512

    @pl.loop(0, d_ref.shape[1] // width)
    def _(c):
        cols = pl.ds(pl.multiple_of(c * width, width), width)
        part = jnp.dot(h_ref[...], d_ref[:, cols], preferred_element_type=f32).astype(bf16)
        at = 0
        for out in outs:
            out[:, cols] = part[at : at + out.shape[0]]
            at += out.shape[0]


def join_kernel(*refs):
    out = refs[-1]
    n = refs[0].shape[0]
    for i, ref in enumerate(refs[:-1]):
        out[i * n : (i + 1) * n, :] = ref[...]


def join(xs):
    rows, width = xs[0].shape
    return pl.pallas_call(
        join_kernel,
        out_shape=jax.ShapeDtypeStruct((rows * len(xs), width), bf16),
        in_specs=[VMEM] * len(xs),
        out_specs=VMEM,
        compiler_params=SMALL,
        cost_estimate=pl.CostEstimate(
            flops=0, bytes_accessed=4 * rows * len(xs) * width, transcendentals=0
        ),
    )(*xs)


def expert(xs, weights):
    w, d = weights
    rows, width = sum(x.shape[0] for x in xs), xs[0].shape[1]
    units = d.shape[0]
    return pl.pallas_call(
        functools.partial(expert_kernel, len(xs)),
        out_shape=[jax.ShapeDtypeStruct(x.shape, bf16) for x in xs],
        in_specs=[VMEM] * (len(xs) + 2),
        out_specs=[VMEM] * len(xs),
        scratch_shapes=[pltpu.VMEM((rows, width), bf16), pltpu.VMEM((rows, units), bf16)],
        compiler_params=pltpu.CompilerParams(vmem_limit_bytes=30 << 20),
        cost_estimate=pl.CostEstimate(
            flops=6 * rows * units * width,
            bytes_accessed=6 * units * width + 4 * rows * width,
            transcendentals=rows * units,
        ),
    )(*xs, w, d)


def final_kernel(attended, prob, *refs):
    terms, out = refs[:-1], refs[-1]
    shared = terms[0][...].astype(f32)
    for term in terms[1:]:
        shared += term[...].astype(f32)
    out[...] = (attended[...].astype(f32) + prob[:, :1] * shared).astype(bf16)


def per_device(
    queries,
    keys,
    values,
    block_table,
    residual,
    out_weight,
    norm_gain,
    gate_logit_weight,
    gate_weight,
    up_weight,
    down_weight,
):
    tokens = queries.shape[0]
    half = tokens // 2
    quarter = tokens // 4
    width = residual.shape[1]
    hidden = down_weight.shape[0]
    y, z, xh = (lax.axis_index(a) for a in CTX)
    core = lax.axis_index("core")
    t = lax.axis_index(TP)

    gate_t, up_t = gate_weight.T, up_weight.T
    piece = hidden // 2
    to_send = pl.pallas_call(
        send_kernel,
        out_shape=jax.ShapeDtypeStruct((3 * piece, width), bf16),
        in_specs=[SMEM, HBM, HBM, HBM],
        out_specs=VMEM,
        scratch_shapes=[pltpu.SemaphoreType.DMA((3,))],
        cost_estimate=pl.CostEstimate(
            flops=0, bytes_accessed=12 * piece * width, transcendentals=0
        ),
    )(core.astype(jnp.int32)[None], gate_t, up_t, down_weight)
    swap_a = lax.ppermute(to_send, ("xh", "xl"), [(0, 3), (3, 0), (1, 2), (2, 1)])

    kv = jnp.concatenate([keys, values], axis=1)
    kv = jnp.concatenate([kv, fetch(kv, "xh", 1)], axis=0)
    kv = jnp.concatenate(gather_direct(kv, "y"), axis=0)
    ahead, behind, far = gather_ring(kv, "z")
    kvs = ahead + behind[:0:-1] + far
    at = jnp.stack([y, z, xh, t]).astype(jnp.int32)

    rows = GROUP * tokens
    span = 64 * tokens
    keep, send = pl.pallas_call(
        attention_kernel,
        out_shape=[jax.ShapeDtypeStruct((half, width), bf16)] * 2,
        in_specs=[SMEM, SMEM, VMEM] + [HBM] * 10,
        out_specs=[VMEM] * 2,
        scratch_shapes=[
            pltpu.VMEM(out_weight.shape, bf16),
            pltpu.VMEM((8, 8 * tokens, 2 * HEAD_DIM), bf16),
            pltpu.VMEM((GROUP * tokens, HEAD_DIM), bf16),
            pltpu.VMEM((8, 8 * tokens), jnp.int32),
            pltpu.SemaphoreType.DMA((10,)),
        ],
        compiler_params=pltpu.CompilerParams(vmem_limit_bytes=46 << 20),
        cost_estimate=pl.CostEstimate(
            flops=4 * rows * span * HEAD_DIM + 2 * tokens * out_weight.size,
            bytes_accessed=2 * out_weight.size + 4 * span * HEAD_DIM,
            transcendentals=rows * span,
        ),
    )(at, block_table, queries, *kvs, out_weight)

    near = fetch(send, "core", 1)
    _, beyond = add([keep, near], pieces=2)
    beyond = fetch(beyond, "xl", 1)
    attended, normed, prob = pl.pallas_call(
        norm_kernel,
        out_shape=[
            jax.ShapeDtypeStruct((quarter, width), bf16),
            jax.ShapeDtypeStruct((quarter, width), bf16),
            jax.ShapeDtypeStruct((quarter, 128), f32),
        ],
        in_specs=[VMEM] * 6,
        out_specs=[VMEM] * 3,
        compiler_params=SMALL,
        cost_estimate=pl.CostEstimate(
            flops=10 * quarter * width, bytes_accessed=14 * quarter * width, transcendentals=quarter
        ),
    )(keep, near, beyond, residual, norm_gain[None, :], gate_logit_weight[None, :])

    by_y = join(gather_direct(normed, "y"))
    ahead, behind, far = gather_ring(by_y, "z")
    swap_a, _ = lax.optimization_barrier((swap_a, by_y))
    swap_b = fetch(swap_a, "core", 1)
    weights = pl.pallas_call(
        assemble_kernel,
        out_shape=[
            jax.ShapeDtypeStruct((4 * hidden, width), bf16),
            jax.ShapeDtypeStruct((2 * hidden, width), bf16),
        ],
        in_specs=[HBM] * 5,
        out_specs=[VMEM] * 2,
        scratch_shapes=[pltpu.SemaphoreType.DMA((24,))],
        compiler_params=pltpu.CompilerParams(vmem_limit_bytes=16 << 20),
        cost_estimate=pl.CostEstimate(
            flops=0, bytes_accessed=12 * hidden * width, transcendentals=0
        ),
    )(gate_t, up_t, down_weight, swap_a, swap_b)
    own, after, before = expert([ahead[0], ahead[1], behind[1]], weights)
    after_2, before_2, after_3, before_3 = expert([ahead[2], behind[2], ahead[3], behind[3]], weights)
    far_parts = expert(far, weights)
    near_parts = [own, after, after_2, after_3, None, before_3, before_2, before]
    by_y = add(scatter_ring(near_parts, far_parts, "z"), pieces=4)
    terms = scatter_direct(by_y, "y")
    return pl.pallas_call(
        final_kernel,
        out_shape=jax.ShapeDtypeStruct((quarter, width), bf16),
        in_specs=[VMEM] * 6,
        out_specs=VMEM,
        compiler_params=SMALL,
        cost_estimate=pl.CostEstimate(
            flops=10 * quarter * width, bytes_accessed=16 * quarter * width, transcendentals=0
        ),
    )(attended, prob, *terms)


def solution(mesh):
    fine = Mesh(mesh.devices.reshape(tuple(SIZES.values())), tuple(SIZES))
    return jax.shard_map(
        per_device,
        mesh=fine,
        in_specs=(
            P(CTX, TP),
            P(CTX, TP),
            P(CTX, TP),
            P(),
            P(CTX + TP, None),
            P(TP, None),
            P(),
            P(),
            P(None, CTX),
            P(None, CTX),
            P(CTX, None),
        ),
        out_specs=P(CTX + TP, None),
        check_vma=False,
    )
```

```python
import functools

import jax
import jax.numpy as jnp
from jax import lax
from jax.experimental import pallas as pl
from jax.experimental.pallas import tpu as pltpu
from jax.sharding import Mesh
from jax.sharding import PartitionSpec as P

HEADS = 28
KV_HEADS = 4
HEAD_DIM = 128
GROUP = HEADS // KV_HEADS
SIZES = {"y": 4, "z": 8, "xh": 2, "xl": 2, "core": 2}
CTX = ("y", "z", "xh")
TP = ("xl", "core")
f32 = jnp.float32
bf16 = jnp.bfloat16
VMEM = pl.BlockSpec(memory_space=pltpu.VMEM)
SMEM = pl.BlockSpec(memory_space=pltpu.SMEM)
HBM = pl.BlockSpec(memory_space=pltpu.HBM)
SMALL = pltpu.CompilerParams(vmem_limit_bytes=8 << 20)
NEG = -1e30
FLOOR = -1e29
EXP2 = 1.4426950408889634


def fetch(x, axis, k):
    n = SIZES[axis]
    k %= n
    if k == 0:
        return x
    return lax.ppermute(x, axis, [((i + k) % n, i) for i in range(n)])


def gather_direct(x, axis):
    return [fetch(x, axis, k) for k in range(SIZES[axis])]


def gather_ring(x, axis):
    n = SIZES[axis]
    h = n // 2
    ahead, behind = [x], [x]
    for k in range(1, h):
        ahead.append(fetch(ahead[-1], axis, 1))
        behind.append(fetch(behind[-1], axis, -1))
    return ahead, behind


def gather_far(ahead, behind, axis):
    rows = ahead.shape[0] // 2
    return [fetch(ahead[:rows], axis, 1), fetch(behind[rows:], axis, -1)]


def add_kernel(n_in, first, *refs):
    ins, outs = refs[:n_in], refs[n_in:]
    rows = outs[0].shape[0]
    for i, out in enumerate(outs):
        part = ins[0][i * rows : (i + 1) * rows, :].astype(f32)
        for other in ins[1:]:
            if other.shape[0] == ins[0].shape[0]:
                part += other[i * rows : (i + 1) * rows, :].astype(f32)
        out[...] = part.astype(out.dtype)
    last = ins[-1]
    if last.shape[0] < ins[0].shape[0]:
        mine = slice(first, first + last.shape[0])
        outs[0][mine, :] = (ins[0][mine, :].astype(f32) + last[...].astype(f32)).astype(bf16)


def add(xs, pieces=1, first=0):
    rows, width = xs[0].shape
    size = rows * width
    out = pl.pallas_call(
        functools.partial(add_kernel, len(xs), first),
        out_shape=[jax.ShapeDtypeStruct((rows // pieces, width), bf16)] * pieces,
        in_specs=[VMEM] * len(xs),
        out_specs=[VMEM] * pieces,
        compiler_params=SMALL,
        cost_estimate=pl.CostEstimate(
            flops=size * len(xs), bytes_accessed=2 * size * (len(xs) + 1), transcendentals=0
        ),
    )(*xs)
    return out[0] if pieces == 1 else out


def scatter_direct(chunks, axis):
    return [chunks[0]] + [fetch(chunks[k], axis, -k) for k in range(1, SIZES[axis])]


def scatter_ring(near, far, axis):
    n = SIZES[axis]
    h = n // 2
    up = fetch(far[0], axis, -1)
    down = fetch(far[1], axis, 1)
    for k in range(h - 1, 0, -1):
        first = near[k].shape[0] - down.shape[0]
        up = fetch(add([near[k], up]), axis, -1)
        down = fetch(add([near[n - k], down], first=first), axis, 1)
    return [near[0], up, down]


def attention_kernel(at_ref, table_ref, q_ref, *refs):
    kvs, w_any, keep_ref, send_ref = refs[:9], refs[9], refs[10], refs[11]
    w_ref, kv_ref, q_all, kp_ref, sems = refs[12:]
    half_rows = kvs[7].shape[0]
    places = [kv_ref.at[j] for j in (0, 1, 2, 3, 5, 6, 7)]
    places += [kv_ref.at[4, pl.ds(i * half_rows, half_rows)] for i in range(2)]
    copies = [
        pltpu.make_async_copy(src, dst, sems.at[i]) for i, (src, dst) in enumerate(zip(kvs, places))
    ]
    copy = pltpu.make_async_copy(w_any, w_ref, sems.at[9])
    for one in copies:
        one.start()
    copy.start()
    y, z, xh, t = (at_ref[i] for i in range(4))
    tokens = q_ref.shape[0]
    half = tokens // 2
    mirror = 2 * table_ref.shape[0] - 1

    def place(pair, local):
        return jnp.where(local < half, pair * half + local, (mirror - pair) * half + local - half)

    def pair_of(dy, dz, dx):
        slot = ((y + dy) % 4 * 8 + (z + dz) % 8) * 2 + (xh + dx) % 2
        return table_ref[slot]

    lane = lax.broadcasted_iota(jnp.int32, (1, 8 * tokens), 1)
    for j in range(8):
        pair = jnp.zeros_like(lane)
        for b in range(8):
            pair = jnp.where(lane // tokens == b, pair_of(b // 2, j, b % 2), pair)
        kp_ref[j : j + 1, :] = place(pair, lane % tokens)
    quarter = tokens // 4
    parts = [
        q_ref[pl.ds(pl.multiple_of((t ^ k) * quarter, quarter), quarter), :] for k in (0, 2, 1, 3)
    ]
    q = jnp.concatenate(parts, axis=0)
    q = jnp.concatenate([q[:, g * HEAD_DIM : (g + 1) * HEAD_DIM] for g in range(GROUP)], axis=0)
    row = lax.broadcasted_iota(jnp.int32, (tokens, 1), 0)
    order = row // quarter
    order = (order % 2) * 2 + order // 2
    qp = place(pair_of(0, 0, 0), (order ^ t) * quarter + row % quarter)
    total_rows = GROUP * tokens
    top = jnp.full((total_rows, 1), FLOOR, f32)
    total = jnp.zeros((total_rows, 1), f32)
    acc = jnp.zeros((total_rows, HEAD_DIM), f32)
    q_all[...] = q
    for one in copies:
        one.wait()

    def step(j, carry):
        top, total, acc = carry
        k = kv_ref[j, :, :HEAD_DIM]
        v = kv_ref[j, :, HEAD_DIM:]
        count = k.shape[0]
        score = lax.dot_general(
            q_all[...], k, (((1,), (1,)), ((), ())), preferred_element_type=f32
        )
        score = score * (HEAD_DIM**-0.5 * EXP2)
        visible = kp_ref[pl.ds(j, 1), :] <= qp
        score = jnp.where(visible[None], score.reshape(GROUP, tokens, count), NEG)
        score = score.reshape(total_rows, count)
        new_top = jnp.maximum(top, jnp.max(score, axis=-1, keepdims=True))
        weight = jnp.exp2(score - new_top)
        keep = jnp.exp2(top - new_top)
        total = total * keep + jnp.sum(weight, axis=-1, keepdims=True)
        acc = acc * keep + jnp.dot(weight.astype(bf16), v, preferred_element_type=f32)
        return new_top, total, acc

    top, total, acc = lax.fori_loop(0, 8, step, (top, total, acc))
    summed = (acc / total).astype(bf16)
    heads = jnp.concatenate([summed[g * tokens : (g + 1) * tokens] for g in range(GROUP)], axis=1)
    copy.wait()
    width = 512

    @pl.loop(0, w_ref.shape[1] // width)
    def _(n):
        cols = pl.ds(pl.multiple_of(n * width, width), width)
        part = jnp.dot(heads, w_ref[:, cols], preferred_element_type=f32).astype(bf16)
        keep_ref[:, cols] = part[:half]
        send_ref[:, cols] = part[half:]


def norm_kernel(keep, near, far, residual, gain, gate_w, attended, normed_ref, prob):
    rows = far.shape[0]
    head_sum = keep[:rows, :].astype(f32) + near[:rows, :].astype(f32) + far[...].astype(f32)
    kept = (residual[...].astype(f32) + head_sum).astype(bf16)
    attended[...] = kept
    wide = kept.astype(f32)
    mean_square = jnp.mean(wide * wide, axis=-1, keepdims=True)
    normed = (wide * lax.rsqrt(mean_square + 1e-06) * gain[...].astype(f32)).astype(bf16)
    normed_ref[...] = normed
    logit = jnp.sum(normed.astype(f32) * gate_w[...].astype(f32), axis=-1, keepdims=True)
    prob[...] = jnp.broadcast_to(1.0 / (1.0 + jnp.exp(-logit)), prob.shape)


def send_kernel(core_ref, g_any, u_any, d_any, out_any, sems):
    n = out_any.shape[0] // 3
    at = pl.multiple_of(core_ref[0] * n, n)
    copies = [
        pltpu.make_async_copy(w.at[pl.ds(at, n)], out_any.at[pl.ds(i * n, n)], sems.at[i])
        for i, w in enumerate((g_any, u_any, d_any))
    ]
    for copy in copies:
        copy.start()
    for copy in copies:
        copy.wait()


def assemble_kernel(g_any, u_any, d_any, a_any, b_any, w_ref, d_ref, sems):
    own = g_any.shape[0]
    swap = a_any.shape[0] // 3
    block = 128
    copies = []

    def start(src, at, dst, to, n):
        copy = pltpu.make_async_copy(
            src.at[pl.ds(at, n)], dst.at[pl.ds(to, n)], sems.at[len(copies)]
        )
        copy.start()
        copies.append(copy)

    for part in range(2):
        pos = 0
        for source, at, length in (
            ((g_any, u_any)[part], 0, own),
            (a_any, part * swap, swap),
            (b_any, part * swap, swap),
        ):
            done = 0
            while done < length:
                b, inside = divmod(pos, block)
                n = min(block - inside, length - done)
                start(source, at + done, w_ref, b * 2 * block + part * block + inside, n)
                done += n
                pos += n
    start(d_any, 0, d_ref, 0, own)
    start(a_any, 2 * swap, d_ref, own, swap)
    start(b_any, 2 * swap, d_ref, own + swap, swap)
    for copy in copies:
        copy.wait()


def expert_kernel(count, *refs):
    xs, w_ref, d_ref, outs = refs[:count], refs[count], refs[count + 1], refs[count + 2 : -2]
    x_ref, h_ref = refs[-2:]
    at = 0
    for x in xs:
        x_ref[at : at + x.shape[0], :] = x[...]
        at += x.shape[0]
    block = 128

    @pl.loop(0, w_ref.shape[0] // (2 * block))
    def _(b):
        both = lax.dot_general(
            x_ref[...],
            w_ref[pl.ds(pl.multiple_of(b * 2 * block, 2 * block), 2 * block), :],
            (((1,), (1,)), ((), ())),
            preferred_element_type=f32,
        )
        gate, up = both[:, :block], both[:, block:]
        value = (gate / (1.0 + jnp.exp(-gate)) * up).astype(bf16)
        h_ref[:, pl.ds(pl.multiple_of(b * block, block), block)] = value

    width = 512

    @pl.loop(0, d_ref.shape[1] // width)
    def _(c):
        cols = pl.ds(pl.multiple_of(c * width, width), width)
        part = jnp.dot(h_ref[...], d_ref[:, cols], preferred_element_type=f32).astype(bf16)
        at = 0
        for out in outs:
            out[:, cols] = part[at : at + out.shape[0]]
            at += out.shape[0]


def join_kernel(*refs):
    out = refs[-1]
    n = refs[0].shape[0]
    for i, ref in enumerate(refs[:-1]):
        out[i * n : (i + 1) * n, :] = ref[...]


def join(xs):
    rows, width = xs[0].shape
    return pl.pallas_call(
        join_kernel,
        out_shape=jax.ShapeDtypeStruct((rows * len(xs), width), bf16),
        in_specs=[VMEM] * len(xs),
        out_specs=VMEM,
        compiler_params=SMALL,
        cost_estimate=pl.CostEstimate(
            flops=0, bytes_accessed=4 * rows * len(xs) * width, transcendentals=0
        ),
    )(*xs)


def expert(xs, weights):
    w, d = weights
    rows, width = sum(x.shape[0] for x in xs), xs[0].shape[1]
    units = d.shape[0]
    return pl.pallas_call(
        functools.partial(expert_kernel, len(xs)),
        out_shape=[jax.ShapeDtypeStruct(x.shape, bf16) for x in xs],
        in_specs=[VMEM] * (len(xs) + 2),
        out_specs=[VMEM] * len(xs),
        scratch_shapes=[pltpu.VMEM((rows, width), bf16), pltpu.VMEM((rows, units), bf16)],
        compiler_params=pltpu.CompilerParams(vmem_limit_bytes=30 << 20),
        cost_estimate=pl.CostEstimate(
            flops=6 * rows * units * width,
            bytes_accessed=6 * units * width + 4 * rows * width,
            transcendentals=rows * units,
        ),
    )(*xs, w, d)


def final_kernel(attended, prob, *refs):
    terms, out = refs[:-1], refs[-1]
    shared = terms[0][...].astype(f32)
    for term in terms[1:]:
        shared += term[...].astype(f32)
    out[...] = (attended[...].astype(f32) + prob[:, :1] * shared).astype(bf16)


def per_device(
    queries,
    keys,
    values,
    block_table,
    residual,
    out_weight,
    norm_gain,
    gate_logit_weight,
    gate_weight,
    up_weight,
    down_weight,
):
    tokens = queries.shape[0]
    half = tokens // 2
    quarter = tokens // 4
    width = residual.shape[1]
    hidden = down_weight.shape[0]
    y, z, xh = (lax.axis_index(a) for a in CTX)
    core = lax.axis_index("core")
    t = lax.axis_index(TP)

    gate_t, up_t = gate_weight.T, up_weight.T
    piece = hidden // 2
    kv = jnp.concatenate([keys, values], axis=1)
    kv = jnp.concatenate([kv, fetch(kv, "xh", 1)], axis=0)
    core_at, _ = lax.optimization_barrier((core.astype(jnp.int32)[None], kv))

    to_send = pl.pallas_call(
        send_kernel,
        out_shape=jax.ShapeDtypeStruct((3 * piece, width), bf16),
        in_specs=[SMEM, HBM, HBM, HBM],
        out_specs=VMEM,
        scratch_shapes=[pltpu.SemaphoreType.DMA((3,))],
        cost_estimate=pl.CostEstimate(
            flops=0, bytes_accessed=12 * piece * width, transcendentals=0
        ),
    )(core_at, gate_t, up_t, down_weight)
    swap_a = lax.ppermute(to_send, ("xh", "xl"), [(0, 3), (3, 0), (1, 2), (2, 1)])

    kv = jnp.concatenate(gather_direct(kv, "y"), axis=0)
    ahead, behind = gather_ring(kv, "z")
    far = gather_far(ahead[3], behind[3], "z")
    kvs = ahead + behind[:0:-1] + far
    at = jnp.stack([y, z, xh, t]).astype(jnp.int32)

    rows = GROUP * tokens
    span = 64 * tokens
    keep, send = pl.pallas_call(
        attention_kernel,
        out_shape=[jax.ShapeDtypeStruct((half, width), bf16)] * 2,
        in_specs=[SMEM, SMEM, VMEM] + [HBM] * 10,
        out_specs=[VMEM] * 2,
        scratch_shapes=[
            pltpu.VMEM(out_weight.shape, bf16),
            pltpu.VMEM((8, 8 * tokens, 2 * HEAD_DIM), bf16),
            pltpu.VMEM((GROUP * tokens, HEAD_DIM), bf16),
            pltpu.VMEM((8, 8 * tokens), jnp.int32),
            pltpu.SemaphoreType.DMA((10,)),
        ],
        compiler_params=pltpu.CompilerParams(vmem_limit_bytes=46 << 20),
        cost_estimate=pl.CostEstimate(
            flops=4 * rows * span * HEAD_DIM + 2 * tokens * out_weight.size,
            bytes_accessed=2 * out_weight.size + 4 * span * HEAD_DIM,
            transcendentals=rows * span,
        ),
    )(at, block_table, queries, *kvs, out_weight)

    near = fetch(send, "core", 1)
    _, beyond = add([keep, near], pieces=2)
    beyond = fetch(beyond, "xl", 1)
    attended, normed, prob = pl.pallas_call(
        norm_kernel,
        out_shape=[
            jax.ShapeDtypeStruct((quarter, width), bf16),
            jax.ShapeDtypeStruct((quarter, width), bf16),
            jax.ShapeDtypeStruct((quarter, 128), f32),
        ],
        in_specs=[VMEM] * 6,
        out_specs=[VMEM] * 3,
        compiler_params=SMALL,
        cost_estimate=pl.CostEstimate(
            flops=10 * quarter * width, bytes_accessed=14 * quarter * width, transcendentals=quarter
        ),
    )(keep, near, beyond, residual, norm_gain[None, :], gate_logit_weight[None, :])

    by_y = join(gather_direct(normed, "y"))
    ahead, behind = gather_ring(by_y, "z")
    swap_a, _ = lax.optimization_barrier((swap_a, ahead[1]))
    swap_b = fetch(swap_a, "core", 1)
    weights = pl.pallas_call(
        assemble_kernel,
        out_shape=[
            jax.ShapeDtypeStruct((4 * hidden, width), bf16),
            jax.ShapeDtypeStruct((2 * hidden, width), bf16),
        ],
        in_specs=[HBM] * 5,
        out_specs=[VMEM] * 2,
        scratch_shapes=[pltpu.SemaphoreType.DMA((24,))],
        compiler_params=pltpu.CompilerParams(vmem_limit_bytes=16 << 20),
        cost_estimate=pl.CostEstimate(
            flops=0, bytes_accessed=12 * hidden * width, transcendentals=0
        ),
    )(gate_t, up_t, down_weight, swap_a, swap_b)
    ahead_3, behind_3, weights = lax.optimization_barrier((ahead[3], behind[3], weights))
    far = gather_far(ahead_3, behind_3, "z")
    own, after, before = expert([ahead[0], ahead[1], behind[1]], weights)
    after_2, before_2, after_3, before_3 = expert(
        [ahead[2], behind[2], ahead[3], behind[3]], weights
    )
    far_parts = expert(far, weights)
    near_parts = [own, after, after_2, after_3, None, before_3, before_2, before]
    by_y = add(scatter_ring(near_parts, far_parts, "z"), pieces=4)
    terms = scatter_direct(by_y, "y")
    return pl.pallas_call(
        final_kernel,
        out_shape=jax.ShapeDtypeStruct((quarter, width), bf16),
        in_specs=[VMEM] * 6,
        out_specs=VMEM,
        compiler_params=SMALL,
        cost_estimate=pl.CostEstimate(
            flops=10 * quarter * width, bytes_accessed=16 * quarter * width, transcendentals=0
        ),
    )(attended, prob, *terms)


def solution(mesh):
    fine = Mesh(mesh.devices.reshape(tuple(SIZES.values())), tuple(SIZES))
    return jax.shard_map(
        per_device,
        mesh=fine,
        in_specs=(
            P(CTX, TP),
            P(CTX, TP),
            P(CTX, TP),
            P(),
            P(CTX + TP, None),
            P(TP, None),
            P(),
            P(),
            P(None, CTX),
            P(None, CTX),
            P(CTX, None),
        ),
        out_specs=P(CTX + TP, None),
        check_vma=False,
    )
```

```python
import functools

import jax
import jax.numpy as jnp
from jax import lax
from jax.experimental import pallas as pl
from jax.experimental.pallas import tpu as pltpu
from jax.sharding import Mesh
from jax.sharding import PartitionSpec as P

HEADS = 28
KV_HEADS = 4
HEAD_DIM = 128
GROUP = HEADS // KV_HEADS
SIZES = {"y": 4, "z": 8, "xh": 2, "xl": 2, "core": 2}
CTX = ("y", "z", "xh")
TP = ("xl", "core")
f32 = jnp.float32
bf16 = jnp.bfloat16
VMEM = pl.BlockSpec(memory_space=pltpu.VMEM)
SMEM = pl.BlockSpec(memory_space=pltpu.SMEM)
HBM = pl.BlockSpec(memory_space=pltpu.HBM)
SMALL = pltpu.CompilerParams(vmem_limit_bytes=8 << 20)
NEG = -1e30
FLOOR = -1e29
EXP2 = 1.4426950408889634


def fetch(x, axis, k):
    n = SIZES[axis]
    k %= n
    if k == 0:
        return x
    return lax.ppermute(x, axis, [((i + k) % n, i) for i in range(n)])


def gather_direct(x, axis):
    return [fetch(x, axis, k) for k in range(SIZES[axis])]


def gather_ring(x, axis):
    n = SIZES[axis]
    h = n // 2
    ahead, behind = [x], [x]
    for k in range(1, h):
        ahead.append(fetch(ahead[-1], axis, 1))
        behind.append(fetch(behind[-1], axis, -1))
    return ahead, behind


def gather_far(ahead, behind, axis):
    rows = ahead.shape[0] // 2
    return [fetch(ahead[:rows], axis, 1), fetch(behind[rows:], axis, -1)]


def add_kernel(n_in, first, *refs):
    ins, outs = refs[:n_in], refs[n_in:]
    rows = outs[0].shape[0]
    for i, out in enumerate(outs):
        part = ins[0][i * rows : (i + 1) * rows, :].astype(f32)
        for other in ins[1:]:
            if other.shape[0] == ins[0].shape[0]:
                part += other[i * rows : (i + 1) * rows, :].astype(f32)
        out[...] = part.astype(out.dtype)
    last = ins[-1]
    if last.shape[0] < ins[0].shape[0]:
        mine = slice(first, first + last.shape[0])
        outs[0][mine, :] = (ins[0][mine, :].astype(f32) + last[...].astype(f32)).astype(bf16)


def add(xs, pieces=1, first=0):
    rows, width = xs[0].shape
    size = rows * width
    out = pl.pallas_call(
        functools.partial(add_kernel, len(xs), first),
        out_shape=[jax.ShapeDtypeStruct((rows // pieces, width), bf16)] * pieces,
        in_specs=[VMEM] * len(xs),
        out_specs=[VMEM] * pieces,
        compiler_params=SMALL,
        cost_estimate=pl.CostEstimate(
            flops=size * len(xs), bytes_accessed=2 * size * (len(xs) + 1), transcendentals=0
        ),
    )(*xs)
    return out[0] if pieces == 1 else out


def scatter_direct(chunks, axis):
    return [chunks[0]] + [fetch(chunks[k], axis, -k) for k in range(1, SIZES[axis])]


def scatter_ring(near, far, axis):
    n = SIZES[axis]
    h = n // 2
    up = fetch(far[0], axis, -1)
    down = fetch(far[1], axis, 1)
    for k in range(h - 1, 0, -1):
        first = near[k].shape[0] - down.shape[0]
        up = fetch(add([near[k], up]), axis, -1)
        down = fetch(add([near[n - k], down], first=first), axis, 1)
    return [near[0], up, down]


def attend(at_ref, table_ref, q_all, kv_ref, kp_ref, steps, carry):
    y, z, xh, t = (at_ref[i] for i in range(4))
    count = kv_ref.shape[1]
    tokens = count // 8
    half = tokens // 2
    quarter = tokens // 4
    mirror = 2 * table_ref.shape[0] - 1

    def place(pair, local):
        return jnp.where(local < half, pair * half + local, (mirror - pair) * half + local - half)

    def pair_of(dy, dz, dx):
        slot = ((y + dy) % 4 * 8 + (z + dz) % 8) * 2 + (xh + dx) % 2
        return table_ref[slot]

    lane = lax.broadcasted_iota(jnp.int32, (1, count), 1)
    for j, dz in enumerate(steps):
        pair = jnp.zeros_like(lane)
        for b in range(8):
            pair = jnp.where(lane // tokens == b, pair_of(b // 2, dz, b % 2), pair)
        kp_ref[j : j + 1, :] = place(pair, lane % tokens)
    row = lax.broadcasted_iota(jnp.int32, (tokens, 1), 0)
    order = row // quarter
    order = (order % 2) * 2 + order // 2
    qp = place(pair_of(0, 0, 0), (order ^ t) * quarter + row % quarter)

    def step(j, carry):
        top, total, acc = carry
        k = kv_ref[j, :, :HEAD_DIM]
        v = kv_ref[j, :, HEAD_DIM:]
        score = lax.dot_general(
            q_all[...], k, (((1,), (1,)), ((), ())), preferred_element_type=f32
        )
        score = score * (HEAD_DIM**-0.5 * EXP2)
        visible = kp_ref[pl.ds(j, 1), :] <= qp
        score = jnp.where(visible[None], score.reshape(GROUP, tokens, count), NEG)
        score = score.reshape(GROUP * tokens, count)
        new_top = jnp.maximum(top, jnp.max(score, axis=-1, keepdims=True))
        weight = jnp.exp2(score - new_top)
        keep = jnp.exp2(top - new_top)
        total = total * keep + jnp.sum(weight, axis=-1, keepdims=True)
        acc = acc * keep + jnp.dot(weight.astype(bf16), v, preferred_element_type=f32)
        return new_top, total, acc

    return lax.fori_loop(0, len(steps), step, carry)


def attention_kernel(steps, at_ref, table_ref, q_ref, *refs):
    n = len(steps)
    kvs, (q_all, top_ref, total_ref, acc_ref) = refs[:n], refs[n : n + 4]
    kv_ref, kp_ref, sems = refs[n + 4 :]
    copies = [pltpu.make_async_copy(kvs[i], kv_ref.at[i], sems.at[i]) for i in range(n)]
    for one in copies:
        one.start()
    t = at_ref[3]
    tokens = q_ref.shape[0]
    quarter = tokens // 4
    parts = [
        q_ref[pl.ds(pl.multiple_of((t ^ k) * quarter, quarter), quarter), :] for k in (0, 2, 1, 3)
    ]
    q = jnp.concatenate(parts, axis=0)
    for g in range(GROUP):
        q_all[g * tokens : (g + 1) * tokens, :] = q[:, g * HEAD_DIM : (g + 1) * HEAD_DIM]
    rows = GROUP * tokens
    carry = (
        jnp.full((rows, 1), FLOOR, f32),
        jnp.zeros((rows, 1), f32),
        jnp.zeros((rows, HEAD_DIM), f32),
    )
    for one in copies:
        one.wait()
    top, total, acc = attend(at_ref, table_ref, q_all, kv_ref, kp_ref, steps, carry)
    top_ref[...] = jnp.broadcast_to(top, top_ref.shape)
    total_ref[...] = jnp.broadcast_to(total, total_ref.shape)
    acc_ref[...] = acc


def project_kernel(steps, at_ref, table_ref, q_all, top_ref, total_ref, acc_ref, *refs):
    kvs, w_any, keep_ref, send_ref = refs[:4], refs[4], refs[5], refs[6]
    w_ref, kv_ref, kp_ref, sems = refs[7:]
    rows = kvs[2].shape[0]
    places = [kv_ref.at[0], kv_ref.at[1]]
    places += [kv_ref.at[2, pl.ds(i * rows, rows)] for i in range(2)]
    copies = [pltpu.make_async_copy(kvs[i], places[i], sems.at[i]) for i in range(4)]
    copy = pltpu.make_async_copy(w_any, w_ref, sems.at[4])
    for one in copies:
        one.start()
    copy.start()
    carry = top_ref[:, :1], total_ref[:, :1], acc_ref[...]
    for one in copies:
        one.wait()
    top, total, acc = attend(at_ref, table_ref, q_all, kv_ref, kp_ref, steps, carry)
    tokens = kv_ref.shape[1] // 8
    half = tokens // 2
    summed = (acc / total).astype(bf16)
    heads = jnp.concatenate([summed[g * tokens : (g + 1) * tokens] for g in range(GROUP)], axis=1)
    copy.wait()
    width = 512

    @pl.loop(0, w_ref.shape[1] // width)
    def _(n):
        cols = pl.ds(pl.multiple_of(n * width, width), width)
        part = jnp.dot(heads, w_ref[:, cols], preferred_element_type=f32).astype(bf16)
        keep_ref[:, cols] = part[:half]
        send_ref[:, cols] = part[half:]


def norm_kernel(keep, near, far, residual, gain, gate_w, attended, normed_ref, prob):
    rows = far.shape[0]
    head_sum = keep[:rows, :].astype(f32) + near[:rows, :].astype(f32) + far[...].astype(f32)
    kept = (residual[...].astype(f32) + head_sum).astype(bf16)
    attended[...] = kept
    wide = kept.astype(f32)
    mean_square = jnp.mean(wide * wide, axis=-1, keepdims=True)
    normed = (wide * lax.rsqrt(mean_square + 1e-06) * gain[...].astype(f32)).astype(bf16)
    normed_ref[...] = normed
    logit = jnp.sum(normed.astype(f32) * gate_w[...].astype(f32), axis=-1, keepdims=True)
    prob[...] = jnp.broadcast_to(1.0 / (1.0 + jnp.exp(-logit)), prob.shape)


def send_kernel(core_ref, g_any, u_any, d_any, out_any, sems):
    n = out_any.shape[0] // 3
    at = pl.multiple_of(core_ref[0] * n, n)
    copies = [
        pltpu.make_async_copy(w.at[pl.ds(at, n)], out_any.at[pl.ds(i * n, n)], sems.at[i])
        for i, w in enumerate((g_any, u_any, d_any))
    ]
    for copy in copies:
        copy.start()
    for copy in copies:
        copy.wait()


def assemble_kernel(g_any, u_any, d_any, a_any, b_any, w_ref, d_ref, sems):
    own = g_any.shape[0]
    swap = a_any.shape[0] // 3
    block = 128
    copies = []

    def start(src, at, dst, to, n):
        copy = pltpu.make_async_copy(
            src.at[pl.ds(at, n)], dst.at[pl.ds(to, n)], sems.at[len(copies)]
        )
        copy.start()
        copies.append(copy)

    for part in range(2):
        pos = 0
        for source, at, length in (
            ((g_any, u_any)[part], 0, own),
            (a_any, part * swap, swap),
            (b_any, part * swap, swap),
        ):
            done = 0
            while done < length:
                b, inside = divmod(pos, block)
                n = min(block - inside, length - done)
                start(source, at + done, w_ref, b * 2 * block + part * block + inside, n)
                done += n
                pos += n
    start(d_any, 0, d_ref, 0, own)
    start(a_any, 2 * swap, d_ref, own, swap)
    start(b_any, 2 * swap, d_ref, own + swap, swap)
    for copy in copies:
        copy.wait()


def expert_kernel(count, *refs):
    xs, w_ref, d_ref, outs = refs[:count], refs[count], refs[count + 1], refs[count + 2 : -2]
    x_ref, h_ref = refs[-2:]
    at = 0
    for x in xs:
        x_ref[at : at + x.shape[0], :] = x[...]
        at += x.shape[0]
    block = 128

    @pl.loop(0, w_ref.shape[0] // (2 * block))
    def _(b):
        both = lax.dot_general(
            x_ref[...],
            w_ref[pl.ds(pl.multiple_of(b * 2 * block, 2 * block), 2 * block), :],
            (((1,), (1,)), ((), ())),
            preferred_element_type=f32,
        )
        gate, up = both[:, :block], both[:, block:]
        value = (gate / (1.0 + jnp.exp(-gate)) * up).astype(bf16)
        h_ref[:, pl.ds(pl.multiple_of(b * block, block), block)] = value

    width = 512

    @pl.loop(0, d_ref.shape[1] // width)
    def _(c):
        cols = pl.ds(pl.multiple_of(c * width, width), width)
        part = jnp.dot(h_ref[...], d_ref[:, cols], preferred_element_type=f32).astype(bf16)
        at = 0
        for out in outs:
            out[:, cols] = part[at : at + out.shape[0]]
            at += out.shape[0]


def join_kernel(*refs):
    out = refs[-1]
    n = refs[0].shape[0]
    for i, ref in enumerate(refs[:-1]):
        out[i * n : (i + 1) * n, :] = ref[...]


def join(xs):
    rows, width = xs[0].shape
    return pl.pallas_call(
        join_kernel,
        out_shape=jax.ShapeDtypeStruct((rows * len(xs), width), bf16),
        in_specs=[VMEM] * len(xs),
        out_specs=VMEM,
        compiler_params=SMALL,
        cost_estimate=pl.CostEstimate(
            flops=0, bytes_accessed=4 * rows * len(xs) * width, transcendentals=0
        ),
    )(*xs)


def expert(xs, weights):
    w, d = weights
    rows, width = sum(x.shape[0] for x in xs), xs[0].shape[1]
    units = d.shape[0]
    return pl.pallas_call(
        functools.partial(expert_kernel, len(xs)),
        out_shape=[jax.ShapeDtypeStruct(x.shape, bf16) for x in xs],
        in_specs=[VMEM] * (len(xs) + 2),
        out_specs=[VMEM] * len(xs),
        scratch_shapes=[pltpu.VMEM((rows, width), bf16), pltpu.VMEM((rows, units), bf16)],
        compiler_params=pltpu.CompilerParams(vmem_limit_bytes=30 << 20),
        cost_estimate=pl.CostEstimate(
            flops=6 * rows * units * width,
            bytes_accessed=6 * units * width + 4 * rows * width,
            transcendentals=rows * units,
        ),
    )(*xs, w, d)


def final_kernel(attended, prob, *refs):
    terms, out = refs[:-1], refs[-1]
    shared = terms[0][...].astype(f32)
    for term in terms[1:]:
        shared += term[...].astype(f32)
    out[...] = (attended[...].astype(f32) + prob[:, :1] * shared).astype(bf16)


def per_device(
    queries,
    keys,
    values,
    block_table,
    residual,
    out_weight,
    norm_gain,
    gate_logit_weight,
    gate_weight,
    up_weight,
    down_weight,
):
    tokens = queries.shape[0]
    half = tokens // 2
    quarter = tokens // 4
    width = residual.shape[1]
    hidden = down_weight.shape[0]
    y, z, xh = (lax.axis_index(a) for a in CTX)
    core = lax.axis_index("core")
    t = lax.axis_index(TP)

    gate_t, up_t = gate_weight.T, up_weight.T
    piece = hidden // 2
    kv = jnp.concatenate([keys, values], axis=1)
    kv = jnp.concatenate([kv, fetch(kv, "xh", 1)], axis=0)
    core_at, _ = lax.optimization_barrier((core.astype(jnp.int32)[None], kv))

    to_send = pl.pallas_call(
        send_kernel,
        out_shape=jax.ShapeDtypeStruct((3 * piece, width), bf16),
        in_specs=[SMEM, HBM, HBM, HBM],
        out_specs=VMEM,
        scratch_shapes=[pltpu.SemaphoreType.DMA((3,))],
        cost_estimate=pl.CostEstimate(
            flops=0, bytes_accessed=12 * piece * width, transcendentals=0
        ),
    )(core_at, gate_t, up_t, down_weight)
    swap_a = lax.ppermute(to_send, ("xh", "xl"), [(0, 3), (3, 0), (1, 2), (2, 1)])

    kv = jnp.concatenate(gather_direct(kv, "y"), axis=0)
    ahead, behind = gather_ring(kv, "z")
    far = gather_far(ahead[3], behind[3], "z")
    at = jnp.stack([y, z, xh, t]).astype(jnp.int32)

    rows = GROUP * tokens
    piece_rows = kv.shape[0]
    steps = (0, 1, 7, 2, 6)
    state = pl.pallas_call(
        functools.partial(attention_kernel, steps),
        out_shape=[jax.ShapeDtypeStruct((rows, HEAD_DIM), bf16)]
        + [jax.ShapeDtypeStruct((rows, HEAD_DIM), f32)] * 3,
        in_specs=[SMEM, SMEM, VMEM] + [HBM] * 5,
        out_specs=[VMEM] * 4,
        scratch_shapes=[
            pltpu.VMEM((5,) + kv.shape, bf16),
            pltpu.VMEM((8, piece_rows), jnp.int32),
            pltpu.SemaphoreType.DMA((5,)),
        ],
        compiler_params=pltpu.CompilerParams(vmem_limit_bytes=16 << 20),
        cost_estimate=pl.CostEstimate(
            flops=20 * rows * piece_rows * HEAD_DIM,
            bytes_accessed=20 * piece_rows * HEAD_DIM,
            transcendentals=5 * rows * piece_rows,
        ),
    )(at, block_table, queries, ahead[0], ahead[1], behind[1], ahead[2], behind[2])
    steps = (3, 5, 4)
    keep, send = pl.pallas_call(
        functools.partial(project_kernel, steps),
        out_shape=[jax.ShapeDtypeStruct((half, width), bf16)] * 2,
        in_specs=[SMEM, SMEM] + [VMEM] * 4 + [HBM] * 5,
        out_specs=[VMEM] * 2,
        scratch_shapes=[
            pltpu.VMEM(out_weight.shape, bf16),
            pltpu.VMEM((3,) + kv.shape, bf16),
            pltpu.VMEM((8, piece_rows), jnp.int32),
            pltpu.SemaphoreType.DMA((5,)),
        ],
        compiler_params=pltpu.CompilerParams(vmem_limit_bytes=46 << 20),
        cost_estimate=pl.CostEstimate(
            flops=12 * rows * piece_rows * HEAD_DIM + 2 * tokens * out_weight.size,
            bytes_accessed=2 * out_weight.size + 12 * piece_rows * HEAD_DIM,
            transcendentals=3 * rows * piece_rows,
        ),
    )(at, block_table, *state, ahead[3], behind[3], *far, out_weight)

    near = fetch(send, "core", 1)
    _, beyond = add([keep, near], pieces=2)
    beyond = fetch(beyond, "xl", 1)
    attended, normed, prob = pl.pallas_call(
        norm_kernel,
        out_shape=[
            jax.ShapeDtypeStruct((quarter, width), bf16),
            jax.ShapeDtypeStruct((quarter, width), bf16),
            jax.ShapeDtypeStruct((quarter, 128), f32),
        ],
        in_specs=[VMEM] * 6,
        out_specs=[VMEM] * 3,
        compiler_params=SMALL,
        cost_estimate=pl.CostEstimate(
            flops=10 * quarter * width, bytes_accessed=14 * quarter * width, transcendentals=quarter
        ),
    )(keep, near, beyond, residual, norm_gain[None, :], gate_logit_weight[None, :])

    by_y = join(gather_direct(normed, "y"))
    ahead, behind = gather_ring(by_y, "z")
    swap_a, _ = lax.optimization_barrier((swap_a, (ahead[1], behind[1])))
    swap_b = fetch(swap_a, "core", 1)
    weights = pl.pallas_call(
        assemble_kernel,
        out_shape=[
            jax.ShapeDtypeStruct((4 * hidden, width), bf16),
            jax.ShapeDtypeStruct((2 * hidden, width), bf16),
        ],
        in_specs=[HBM] * 5,
        out_specs=[VMEM] * 2,
        scratch_shapes=[pltpu.SemaphoreType.DMA((24,))],
        compiler_params=pltpu.CompilerParams(vmem_limit_bytes=16 << 20),
        cost_estimate=pl.CostEstimate(
            flops=0, bytes_accessed=12 * hidden * width, transcendentals=0
        ),
    )(gate_t, up_t, down_weight, swap_a, swap_b)
    ahead_3, behind_3, weights = lax.optimization_barrier((ahead[3], behind[3], weights))
    far = gather_far(ahead_3, behind_3, "z")
    own, after, before = expert([ahead[0], ahead[1], behind[1]], weights)
    after_2, before_2, after_3, before_3 = expert(
        [ahead[2], behind[2], ahead[3], behind[3]], weights
    )
    far_parts = expert(far, weights)
    near_parts = [own, after, after_2, after_3, None, before_3, before_2, before]
    by_y = add(scatter_ring(near_parts, far_parts, "z"), pieces=4)
    terms = scatter_direct(by_y, "y")
    return pl.pallas_call(
        final_kernel,
        out_shape=jax.ShapeDtypeStruct((quarter, width), bf16),
        in_specs=[VMEM] * 6,
        out_specs=VMEM,
        compiler_params=SMALL,
        cost_estimate=pl.CostEstimate(
            flops=10 * quarter * width, bytes_accessed=16 * quarter * width, transcendentals=0
        ),
    )(attended, prob, *terms)


def solution(mesh):
    fine = Mesh(mesh.devices.reshape(tuple(SIZES.values())), tuple(SIZES))
    return jax.shard_map(
        per_device,
        mesh=fine,
        in_specs=(
            P(CTX, TP),
            P(CTX, TP),
            P(CTX, TP),
            P(),
            P(CTX + TP, None),
            P(TP, None),
            P(),
            P(),
            P(None, CTX),
            P(None, CTX),
            P(CTX, None),
        ),
        out_specs=P(CTX + TP, None),
        check_vma=False,
    )
```

```python
import functools

import jax
import jax.numpy as jnp
from jax import lax
from jax.experimental import pallas as pl
from jax.experimental.pallas import tpu as pltpu
from jax.sharding import Mesh
from jax.sharding import PartitionSpec as P

HEADS = 28
KV_HEADS = 4
HEAD_DIM = 128
GROUP = HEADS // KV_HEADS
SIZES = {"y": 4, "z": 8, "xh": 2, "xl": 2, "core": 2}
CTX = ("y", "z", "xh")
TP = ("xl", "core")
f32 = jnp.float32
bf16 = jnp.bfloat16
VMEM = pl.BlockSpec(memory_space=pltpu.VMEM)
SMEM = pl.BlockSpec(memory_space=pltpu.SMEM)
HBM = pl.BlockSpec(memory_space=pltpu.HBM)
SMALL = pltpu.CompilerParams(vmem_limit_bytes=8 << 20)
NEG = -1e30
FLOOR = -1e29
EXP2 = 1.4426950408889634


def fetch(x, axis, k):
    n = SIZES[axis]
    k %= n
    if k == 0:
        return x
    return lax.ppermute(x, axis, [((i + k) % n, i) for i in range(n)])


def gather_direct(x, axis):
    return [fetch(x, axis, k) for k in range(SIZES[axis])]


def gather_ring(x, axis):
    n = SIZES[axis]
    h = n // 2
    ahead, behind = [x], [x]
    for k in range(1, h):
        ahead.append(fetch(ahead[-1], axis, 1))
        behind.append(fetch(behind[-1], axis, -1))
    return ahead, behind


def gather_far(ahead, behind, axis):
    rows = ahead.shape[0] // 2
    return [fetch(ahead[:rows], axis, 1), fetch(behind[rows:], axis, -1)]


def add_kernel(n_in, first, *refs):
    ins, outs = refs[:n_in], refs[n_in:]
    rows = outs[0].shape[0]
    for i, out in enumerate(outs):
        part = ins[0][i * rows : (i + 1) * rows, :].astype(f32)
        for other in ins[1:]:
            if other.shape[0] == ins[0].shape[0]:
                part += other[i * rows : (i + 1) * rows, :].astype(f32)
        out[...] = part.astype(out.dtype)
    last = ins[-1]
    if last.shape[0] < ins[0].shape[0]:
        mine = slice(first, first + last.shape[0])
        outs[0][mine, :] = (ins[0][mine, :].astype(f32) + last[...].astype(f32)).astype(bf16)


def add(xs, pieces=1, first=0):
    rows, width = xs[0].shape
    size = rows * width
    out = pl.pallas_call(
        functools.partial(add_kernel, len(xs), first),
        out_shape=[jax.ShapeDtypeStruct((rows // pieces, width), bf16)] * pieces,
        in_specs=[VMEM] * len(xs),
        out_specs=[VMEM] * pieces,
        compiler_params=SMALL,
        cost_estimate=pl.CostEstimate(
            flops=size * len(xs), bytes_accessed=2 * size * (len(xs) + 1), transcendentals=0
        ),
    )(*xs)
    return out[0] if pieces == 1 else out


def scatter_direct(chunks, axis):
    return [chunks[0]] + [fetch(chunks[k], axis, -k) for k in range(1, SIZES[axis])]


def scatter_ring(near, far, axis):
    n = SIZES[axis]
    h = n // 2
    up = fetch(far[0], axis, -1)
    down = fetch(far[1], axis, 1)
    for k in range(h - 1, 0, -1):
        first = near[k].shape[0] - down.shape[0]
        up = fetch(add([near[k], up]), axis, -1)
        down = fetch(add([near[n - k], down], first=first), axis, 1)
    return [near[0], up, down]


def attend(at_ref, table_ref, q_all, kv_ref, kp_ref, steps, carry):
    y, z, xh, t = (at_ref[i] for i in range(4))
    count = kv_ref.shape[1]
    tokens = count // 8
    half = tokens // 2
    quarter = tokens // 4
    mirror = 2 * table_ref.shape[0] - 1

    def place(pair, local):
        return jnp.where(local < half, pair * half + local, (mirror - pair) * half + local - half)

    def pair_of(dy, dz, dx):
        slot = ((y + dy) % 4 * 8 + (z + dz) % 8) * 2 + (xh + dx) % 2
        return table_ref[slot]

    lane = lax.broadcasted_iota(jnp.int32, (1, count), 1)
    for j, dz in enumerate(steps):
        pair = jnp.zeros_like(lane)
        for b in range(8):
            pair = jnp.where(lane // tokens == b, pair_of(b // 2, dz, b % 2), pair)
        kp_ref[j : j + 1, :] = place(pair, lane % tokens)
    row = lax.broadcasted_iota(jnp.int32, (tokens, 1), 0)
    order = row // quarter
    order = (order % 2) * 2 + order // 2
    qp = place(pair_of(0, 0, 0), (order ^ t) * quarter + row % quarter)

    def step(j, carry):
        top, total, acc = carry
        k = kv_ref[j, :, :HEAD_DIM]
        v = kv_ref[j, :, HEAD_DIM:]
        score = lax.dot_general(
            q_all[...], k, (((1,), (1,)), ((), ())), preferred_element_type=f32
        )
        score = score * (HEAD_DIM**-0.5 * EXP2)
        visible = kp_ref[pl.ds(j, 1), :] <= qp
        score = jnp.where(visible[None], score.reshape(GROUP, tokens, count), NEG)
        score = score.reshape(GROUP * tokens, count)
        new_top = jnp.maximum(top, jnp.max(score, axis=-1, keepdims=True))
        weight = jnp.exp2(score - new_top)
        keep = jnp.exp2(top - new_top)
        total = total * keep + jnp.sum(weight, axis=-1, keepdims=True)
        acc = acc * keep + jnp.dot(weight.astype(bf16), v, preferred_element_type=f32)
        return new_top, total, acc

    return lax.fori_loop(0, len(steps), step, carry)


def attention_kernel(steps, at_ref, table_ref, q_ref, *refs):
    n = len(steps)
    kvs, (q_all, top_ref, total_ref, acc_ref) = refs[:n], refs[n : n + 4]
    kv_ref, kp_ref, sems = refs[n + 4 :]
    copies = [pltpu.make_async_copy(kvs[i], kv_ref.at[i], sems.at[i]) for i in range(n)]
    for one in copies:
        one.start()
    t = at_ref[3]
    tokens = q_ref.shape[0]
    quarter = tokens // 4
    parts = [
        q_ref[pl.ds(pl.multiple_of((t ^ k) * quarter, quarter), quarter), :] for k in (0, 2, 1, 3)
    ]
    q = jnp.concatenate(parts, axis=0)
    for g in range(GROUP):
        q_all[g * tokens : (g + 1) * tokens, :] = q[:, g * HEAD_DIM : (g + 1) * HEAD_DIM]
    rows = GROUP * tokens
    carry = (
        jnp.full((rows, 1), FLOOR, f32),
        jnp.zeros((rows, 1), f32),
        jnp.zeros((rows, HEAD_DIM), f32),
    )
    for one in copies:
        one.wait()
    top, total, acc = attend(at_ref, table_ref, q_all, kv_ref, kp_ref, steps, carry)
    top_ref[...] = jnp.broadcast_to(top, top_ref.shape)
    total_ref[...] = jnp.broadcast_to(total, total_ref.shape)
    acc_ref[...] = acc


def project_kernel(steps, at_ref, table_ref, q_all, top_ref, total_ref, acc_ref, *refs):
    kvs, w_any, keep_ref, send_ref = refs[:4], refs[4], refs[5], refs[6]
    w_ref, kv_ref, kp_ref, sems = refs[7:]
    rows = kvs[2].shape[0]
    places = [kv_ref.at[0], kv_ref.at[1]]
    places += [kv_ref.at[2, pl.ds(i * rows, rows)] for i in range(2)]
    copies = [pltpu.make_async_copy(kvs[i], places[i], sems.at[i]) for i in range(4)]
    copy = pltpu.make_async_copy(w_any, w_ref, sems.at[4])
    for one in copies:
        one.start()
    copy.start()
    carry = top_ref[:, :1], total_ref[:, :1], acc_ref[...]
    for one in copies:
        one.wait()
    top, total, acc = attend(at_ref, table_ref, q_all, kv_ref, kp_ref, steps, carry)
    tokens = kv_ref.shape[1] // 8
    half = tokens // 2
    summed = (acc / total).astype(bf16)
    heads = jnp.concatenate([summed[g * tokens : (g + 1) * tokens] for g in range(GROUP)], axis=1)
    copy.wait()
    width = 512

    @pl.loop(0, w_ref.shape[1] // width)
    def _(n):
        cols = pl.ds(pl.multiple_of(n * width, width), width)
        part = jnp.dot(heads, w_ref[:, cols], preferred_element_type=f32).astype(bf16)
        keep_ref[:, cols] = part[:half]
        send_ref[:, cols] = part[half:]


def norm_kernel(keep, near, far, residual, gain, gate_w, attended, normed_ref, prob):
    rows = far.shape[0]
    head_sum = keep[:rows, :].astype(f32) + near[:rows, :].astype(f32) + far[...].astype(f32)
    kept = (residual[...].astype(f32) + head_sum).astype(bf16)
    attended[...] = kept
    wide = kept.astype(f32)
    mean_square = jnp.mean(wide * wide, axis=-1, keepdims=True)
    normed = (wide * lax.rsqrt(mean_square + 1e-06) * gain[...].astype(f32)).astype(bf16)
    normed_ref[...] = normed
    logit = jnp.sum(normed.astype(f32) * gate_w[...].astype(f32), axis=-1, keepdims=True)
    prob[...] = jnp.broadcast_to(1.0 / (1.0 + jnp.exp(-logit)), prob.shape)


def send_kernel(core_ref, g_any, u_any, d_any, out_any, buf, in_sems, out_sems):
    n = out_any.shape[0] // 3
    at = pl.multiple_of(core_ref[0] * n, n)
    ins, outs = [], []
    for i, w in enumerate((g_any, u_any, d_any)):
        here = buf.at[pl.ds(i * n, n)]
        ins.append(pltpu.make_async_copy(w.at[pl.ds(at, n)], here, in_sems.at[i]))
        outs.append(pltpu.make_async_copy(here, out_any.at[pl.ds(i * n, n)], out_sems.at[i]))
    for copy in ins:
        copy.start()
    for copy, out in zip(ins, outs):
        copy.wait()
        out.start()
    for out in outs:
        out.wait()


def assemble_kernel(g_any, u_any, d_any, a_any, b_any, w_ref, d_ref, sems):
    own = g_any.shape[0]
    swap = a_any.shape[0] // 3
    block = 128
    copies = []

    def start(src, at, dst, to, n):
        copy = pltpu.make_async_copy(
            src.at[pl.ds(at, n)], dst.at[pl.ds(to, n)], sems.at[len(copies)]
        )
        copy.start()
        copies.append(copy)

    for part in range(2):
        pos = 0
        for source, at, length in (
            ((g_any, u_any)[part], 0, own),
            (a_any, part * swap, swap),
            (b_any, part * swap, swap),
        ):
            done = 0
            while done < length:
                b, inside = divmod(pos, block)
                n = min(block - inside, length - done)
                start(source, at + done, w_ref, b * 2 * block + part * block + inside, n)
                done += n
                pos += n
    start(d_any, 0, d_ref, 0, own)
    start(a_any, 2 * swap, d_ref, own, swap)
    start(b_any, 2 * swap, d_ref, own + swap, swap)
    for copy in copies:
        copy.wait()


def expert_kernel(count, *refs):
    xs, w_ref, d_ref, outs = refs[:count], refs[count], refs[count + 1], refs[count + 2 : -2]
    x_ref, h_ref = refs[-2:]
    at = 0
    for x in xs:
        x_ref[at : at + x.shape[0], :] = x[...]
        at += x.shape[0]
    block = 128

    @pl.loop(0, w_ref.shape[0] // (2 * block))
    def _(b):
        both = lax.dot_general(
            x_ref[...],
            w_ref[pl.ds(pl.multiple_of(b * 2 * block, 2 * block), 2 * block), :],
            (((1,), (1,)), ((), ())),
            preferred_element_type=f32,
        )
        gate, up = both[:, :block], both[:, block:]
        value = (gate / (1.0 + jnp.exp(-gate)) * up).astype(bf16)
        h_ref[:, pl.ds(pl.multiple_of(b * block, block), block)] = value

    width = 512

    @pl.loop(0, d_ref.shape[1] // width)
    def _(c):
        cols = pl.ds(pl.multiple_of(c * width, width), width)
        part = jnp.dot(h_ref[...], d_ref[:, cols], preferred_element_type=f32).astype(bf16)
        at = 0
        for out in outs:
            out[:, cols] = part[at : at + out.shape[0]]
            at += out.shape[0]


def join_kernel(*refs):
    out = refs[-1]
    n = refs[0].shape[0]
    for i, ref in enumerate(refs[:-1]):
        out[i * n : (i + 1) * n, :] = ref[...]


def join(xs):
    rows, width = xs[0].shape
    return pl.pallas_call(
        join_kernel,
        out_shape=jax.ShapeDtypeStruct((rows * len(xs), width), bf16),
        in_specs=[VMEM] * len(xs),
        out_specs=VMEM,
        compiler_params=SMALL,
        cost_estimate=pl.CostEstimate(
            flops=0, bytes_accessed=4 * rows * len(xs) * width, transcendentals=0
        ),
    )(*xs)


def expert(xs, weights):
    w, d = weights
    rows, width = sum(x.shape[0] for x in xs), xs[0].shape[1]
    units = d.shape[0]
    return pl.pallas_call(
        functools.partial(expert_kernel, len(xs)),
        out_shape=[jax.ShapeDtypeStruct(x.shape, bf16) for x in xs],
        in_specs=[VMEM] * (len(xs) + 2),
        out_specs=[VMEM] * len(xs),
        scratch_shapes=[pltpu.VMEM((rows, width), bf16), pltpu.VMEM((rows, units), bf16)],
        compiler_params=pltpu.CompilerParams(vmem_limit_bytes=30 << 20),
        cost_estimate=pl.CostEstimate(
            flops=6 * rows * units * width,
            bytes_accessed=6 * units * width + 4 * rows * width,
            transcendentals=rows * units,
        ),
    )(*xs, w, d)


def final_kernel(attended, prob, *refs):
    terms, out = refs[:-1], refs[-1]
    shared = terms[0][...].astype(f32)
    for term in terms[1:]:
        shared += term[...].astype(f32)
    out[...] = (attended[...].astype(f32) + prob[:, :1] * shared).astype(bf16)


def per_device(
    queries,
    keys,
    values,
    block_table,
    residual,
    out_weight,
    norm_gain,
    gate_logit_weight,
    gate_weight,
    up_weight,
    down_weight,
):
    tokens = queries.shape[0]
    half = tokens // 2
    quarter = tokens // 4
    width = residual.shape[1]
    hidden = down_weight.shape[0]
    y, z, xh = (lax.axis_index(a) for a in CTX)
    core = lax.axis_index("core")
    t = lax.axis_index(TP)

    gate_t, up_t = gate_weight.T, up_weight.T
    piece = hidden // 2
    kv = jnp.concatenate([keys, values], axis=1)
    kv = jnp.concatenate([kv, fetch(kv, "xh", 1)], axis=0)
    core_at, _ = lax.optimization_barrier((core.astype(jnp.int32)[None], kv))

    to_send = pl.pallas_call(
        send_kernel,
        out_shape=jax.ShapeDtypeStruct((3 * piece, width), bf16),
        in_specs=[SMEM, HBM, HBM, HBM],
        out_specs=HBM,
        scratch_shapes=[
            pltpu.VMEM((3 * piece, width), bf16),
            pltpu.SemaphoreType.DMA((3,)),
            pltpu.SemaphoreType.DMA((3,)),
        ],
        cost_estimate=pl.CostEstimate(
            flops=0, bytes_accessed=12 * piece * width, transcendentals=0
        ),
    )(core_at, gate_t, up_t, down_weight)
    swap_a = lax.ppermute(to_send, ("xh", "xl"), [(0, 3), (3, 0), (1, 2), (2, 1)])

    kv = jnp.concatenate(gather_direct(kv, "y"), axis=0)
    ahead, behind = gather_ring(kv, "z")
    far = gather_far(ahead[3], behind[3], "z")
    at = jnp.stack([y, z, xh, t]).astype(jnp.int32)

    rows = GROUP * tokens
    piece_rows = kv.shape[0]
    steps = (0, 1, 7, 2, 6)
    state = pl.pallas_call(
        functools.partial(attention_kernel, steps),
        out_shape=[jax.ShapeDtypeStruct((rows, HEAD_DIM), bf16)]
        + [jax.ShapeDtypeStruct((rows, HEAD_DIM), f32)] * 3,
        in_specs=[SMEM, SMEM, VMEM] + [HBM] * 5,
        out_specs=[VMEM] * 4,
        scratch_shapes=[
            pltpu.VMEM((5,) + kv.shape, bf16),
            pltpu.VMEM((8, piece_rows), jnp.int32),
            pltpu.SemaphoreType.DMA((5,)),
        ],
        compiler_params=pltpu.CompilerParams(vmem_limit_bytes=16 << 20),
        cost_estimate=pl.CostEstimate(
            flops=20 * rows * piece_rows * HEAD_DIM,
            bytes_accessed=20 * piece_rows * HEAD_DIM,
            transcendentals=5 * rows * piece_rows,
        ),
    )(at, block_table, queries, ahead[0], ahead[1], behind[1], ahead[2], behind[2])
    steps = (3, 5, 4)
    keep, send = pl.pallas_call(
        functools.partial(project_kernel, steps),
        out_shape=[jax.ShapeDtypeStruct((half, width), bf16)] * 2,
        in_specs=[SMEM, SMEM] + [VMEM] * 4 + [HBM] * 5,
        out_specs=[VMEM] * 2,
        scratch_shapes=[
            pltpu.VMEM(out_weight.shape, bf16),
            pltpu.VMEM((3,) + kv.shape, bf16),
            pltpu.VMEM((8, piece_rows), jnp.int32),
            pltpu.SemaphoreType.DMA((5,)),
        ],
        compiler_params=pltpu.CompilerParams(vmem_limit_bytes=46 << 20),
        cost_estimate=pl.CostEstimate(
            flops=12 * rows * piece_rows * HEAD_DIM + 2 * tokens * out_weight.size,
            bytes_accessed=2 * out_weight.size + 12 * piece_rows * HEAD_DIM,
            transcendentals=3 * rows * piece_rows,
        ),
    )(at, block_table, *state, ahead[3], behind[3], *far, out_weight)

    near = fetch(send, "core", 1)
    _, beyond = add([keep, near], pieces=2)
    beyond = fetch(beyond, "xl", 1)
    attended, normed, prob = pl.pallas_call(
        norm_kernel,
        out_shape=[
            jax.ShapeDtypeStruct((quarter, width), bf16),
            jax.ShapeDtypeStruct((quarter, width), bf16),
            jax.ShapeDtypeStruct((quarter, 128), f32),
        ],
        in_specs=[VMEM] * 6,
        out_specs=[VMEM] * 3,
        compiler_params=SMALL,
        cost_estimate=pl.CostEstimate(
            flops=10 * quarter * width, bytes_accessed=14 * quarter * width, transcendentals=quarter
        ),
    )(keep, near, beyond, residual, norm_gain[None, :], gate_logit_weight[None, :])

    by_y = join(gather_direct(normed, "y"))
    ahead, behind = gather_ring(by_y, "z")
    swap_a, _ = lax.optimization_barrier((swap_a, (ahead[1], behind[1])))
    swap_b = fetch(swap_a, "core", 1)
    weights = pl.pallas_call(
        assemble_kernel,
        out_shape=[
            jax.ShapeDtypeStruct((4 * hidden, width), bf16),
            jax.ShapeDtypeStruct((2 * hidden, width), bf16),
        ],
        in_specs=[HBM] * 5,
        out_specs=[VMEM] * 2,
        scratch_shapes=[pltpu.SemaphoreType.DMA((24,))],
        compiler_params=pltpu.CompilerParams(vmem_limit_bytes=16 << 20),
        cost_estimate=pl.CostEstimate(
            flops=0, bytes_accessed=12 * hidden * width, transcendentals=0
        ),
    )(gate_t, up_t, down_weight, swap_a, swap_b)
    ahead_3, behind_3, weights = lax.optimization_barrier((ahead[3], behind[3], weights))
    far = gather_far(ahead_3, behind_3, "z")
    after_2, before_2, after_3, before_3 = expert(
        [ahead[2], behind[2], ahead[3], behind[3]], weights
    )
    weights, after_3 = lax.optimization_barrier((weights, after_3))
    far_parts = expert(far, weights)
    own, after, before = expert([ahead[0], ahead[1], behind[1]], weights)
    near_parts = [own, after, after_2, after_3, None, before_3, before_2, before]
    by_y = add(scatter_ring(near_parts, far_parts, "z"), pieces=4)
    terms = scatter_direct(by_y, "y")
    return pl.pallas_call(
        final_kernel,
        out_shape=jax.ShapeDtypeStruct((quarter, width), bf16),
        in_specs=[VMEM] * 6,
        out_specs=VMEM,
        compiler_params=SMALL,
        cost_estimate=pl.CostEstimate(
            flops=10 * quarter * width, bytes_accessed=16 * quarter * width, transcendentals=0
        ),
    )(attended, prob, *terms)


def solution(mesh):
    fine = Mesh(mesh.devices.reshape(tuple(SIZES.values())), tuple(SIZES))
    return jax.shard_map(
        per_device,
        mesh=fine,
        in_specs=(
            P(CTX, TP),
            P(CTX, TP),
            P(CTX, TP),
            P(),
            P(CTX + TP, None),
            P(TP, None),
            P(),
            P(),
            P(None, CTX),
            P(None, CTX),
            P(CTX, None),
        ),
        out_specs=P(CTX + TP, None),
        check_vma=False,
    )
```

```python
import functools

import jax
import jax.numpy as jnp
from jax import lax
from jax.experimental import pallas as pl
from jax.experimental.pallas import tpu as pltpu
from jax.sharding import Mesh
from jax.sharding import PartitionSpec as P

HEADS = 28
KV_HEADS = 4
HEAD_DIM = 128
GROUP = HEADS // KV_HEADS
SIZES = {"y": 4, "z": 8, "xh": 2, "xl": 2, "core": 2}
CTX = ("y", "z", "xh")
TP = ("xl", "core")
f32 = jnp.float32
bf16 = jnp.bfloat16
VMEM = pl.BlockSpec(memory_space=pltpu.VMEM)
SMEM = pl.BlockSpec(memory_space=pltpu.SMEM)
HBM = pl.BlockSpec(memory_space=pltpu.HBM)
SMALL = pltpu.CompilerParams(vmem_limit_bytes=8 << 20)
NEG = -1e30
FLOOR = -1e29
EXP2 = 1.4426950408889634


def fetch(x, axis, k):
    n = SIZES[axis]
    k %= n
    if k == 0:
        return x
    return lax.ppermute(x, axis, [((i + k) % n, i) for i in range(n)])


def gather_direct(x, axis):
    return [fetch(x, axis, k) for k in range(SIZES[axis])]


def gather_ring(x, axis):
    n = SIZES[axis]
    h = n // 2
    ahead, behind = [x], [x]
    for k in range(1, h):
        ahead.append(fetch(ahead[-1], axis, 1))
        behind.append(fetch(behind[-1], axis, -1))
    return ahead, behind


def gather_far(ahead, behind, axis):
    rows = ahead.shape[0] // 2
    return [fetch(ahead[:rows], axis, 1), fetch(behind[rows:], axis, -1)]


def add_kernel(n_in, *refs):
    ins, outs = refs[:n_in], refs[n_in:]
    rows = outs[0].shape[0]
    for i, out in enumerate(outs):
        part = ins[0][i * rows : (i + 1) * rows, :].astype(f32)
        for other in ins[1:]:
            part += other[i * rows : (i + 1) * rows, :].astype(f32)
        out[...] = part.astype(out.dtype)


def halves_kernel(x, low, high, out):
    rows = low.shape[0]
    out[:rows, :] = (x[:rows, :].astype(f32) + low[...].astype(f32)).astype(bf16)
    out[rows:, :] = (x[rows:, :].astype(f32) + high[...].astype(f32)).astype(bf16)


def cost_of_add(size, terms):
    return pl.CostEstimate(
        flops=size * terms, bytes_accessed=2 * size * (terms + 1), transcendentals=0
    )


def add(xs, pieces=1):
    rows, width = xs[0].shape
    out = pl.pallas_call(
        functools.partial(add_kernel, len(xs)),
        out_shape=[jax.ShapeDtypeStruct((rows // pieces, width), bf16)] * pieces,
        in_specs=[VMEM] * len(xs),
        out_specs=[VMEM] * pieces,
        compiler_params=SMALL,
        cost_estimate=cost_of_add(rows * width, len(xs)),
    )(*xs)
    return out[0] if pieces == 1 else out


def add_halves(x, low, high):
    return pl.pallas_call(
        halves_kernel,
        out_shape=jax.ShapeDtypeStruct(x.shape, bf16),
        in_specs=[VMEM] * 3,
        out_specs=VMEM,
        compiler_params=SMALL,
        cost_estimate=cost_of_add(x.size, 2),
    )(x, low, high)


def scatter_direct(chunks, axis):
    return [chunks[0]] + [fetch(chunks[k], axis, -k) for k in range(1, SIZES[axis])]


def scatter_ring(near, far, axis):
    n = SIZES[axis]
    h = n // 2
    low, up_high = near[h - 1]
    down_low, high = near[h + 1]
    early = fetch(up_high, axis, -1), fetch(down_low, axis, 1)
    far, (up_high, down_low) = lax.optimization_barrier((list(far), early))
    up_low = fetch(add([low, fetch(far[0], axis, -1)]), axis, -1)
    down_high = fetch(add([high, fetch(far[1], axis, 1)]), axis, 1)
    up = fetch(add_halves(near[h - 2], up_low, up_high), axis, -1)
    down = fetch(add_halves(near[h + 2], down_low, down_high), axis, 1)
    for k in range(h - 3, 0, -1):
        up = fetch(add([near[k], up]), axis, -1)
        down = fetch(add([near[n - k], down]), axis, 1)
    return [near[0], up, down]


def attend(at_ref, table_ref, q_all, kv_ref, kp_ref, steps, carry):
    y, z, xh, t = (at_ref[i] for i in range(4))
    count = kv_ref.shape[1]
    tokens = count // 8
    half = tokens // 2
    quarter = tokens // 4
    mirror = 2 * table_ref.shape[0] - 1

    def place(pair, local):
        return jnp.where(local < half, pair * half + local, (mirror - pair) * half + local - half)

    def pair_of(dy, dz, dx):
        slot = ((y + dy) % 4 * 8 + (z + dz) % 8) * 2 + (xh + dx) % 2
        return table_ref[slot]

    lane = lax.broadcasted_iota(jnp.int32, (1, count), 1)
    for j, dz in enumerate(steps):
        pair = jnp.zeros_like(lane)
        for b in range(8):
            pair = jnp.where(lane // tokens == b, pair_of(b // 2, dz, b % 2), pair)
        kp_ref[j : j + 1, :] = place(pair, lane % tokens)
    row = lax.broadcasted_iota(jnp.int32, (tokens, 1), 0)
    order = row // quarter
    order = (order % 2) * 2 + order // 2
    qp = place(pair_of(0, 0, 0), (order ^ t) * quarter + row % quarter)

    def step(j, carry):
        top, total, acc = carry
        k = kv_ref[j, :, :HEAD_DIM]
        v = kv_ref[j, :, HEAD_DIM:]
        score = lax.dot_general(
            q_all[...], k, (((1,), (1,)), ((), ())), preferred_element_type=f32
        )
        score = score * (HEAD_DIM**-0.5 * EXP2)
        visible = kp_ref[pl.ds(j, 1), :] <= qp
        score = jnp.where(visible[None], score.reshape(GROUP, tokens, count), NEG)
        score = score.reshape(GROUP * tokens, count)
        new_top = jnp.maximum(top, jnp.max(score, axis=-1, keepdims=True))
        weight = jnp.exp2(score - new_top)
        keep = jnp.exp2(top - new_top)
        total = total * keep + jnp.sum(weight, axis=-1, keepdims=True)
        acc = acc * keep + jnp.dot(weight.astype(bf16), v, preferred_element_type=f32)
        return new_top, total, acc

    return lax.fori_loop(0, len(steps), step, carry)


def attention_kernel(steps, at_ref, table_ref, q_ref, *refs):
    n = len(steps)
    kvs, (q_all, top_ref, total_ref, acc_ref) = refs[:n], refs[n : n + 4]
    kv_ref, kp_ref, sems = refs[n + 4 :]
    copies = [pltpu.make_async_copy(kvs[i], kv_ref.at[i], sems.at[i]) for i in range(n)]
    for one in copies:
        one.start()
    t = at_ref[3]
    tokens = q_ref.shape[0]
    quarter = tokens // 4
    parts = [
        q_ref[pl.ds(pl.multiple_of((t ^ k) * quarter, quarter), quarter), :] for k in (0, 2, 1, 3)
    ]
    q = jnp.concatenate(parts, axis=0)
    for g in range(GROUP):
        q_all[g * tokens : (g + 1) * tokens, :] = q[:, g * HEAD_DIM : (g + 1) * HEAD_DIM]
    rows = GROUP * tokens
    carry = (
        jnp.full((rows, 1), FLOOR, f32),
        jnp.zeros((rows, 1), f32),
        jnp.zeros((rows, HEAD_DIM), f32),
    )
    for one in copies:
        one.wait()
    top, total, acc = attend(at_ref, table_ref, q_all, kv_ref, kp_ref, steps, carry)
    top_ref[...] = jnp.broadcast_to(top, top_ref.shape)
    total_ref[...] = jnp.broadcast_to(total, total_ref.shape)
    acc_ref[...] = acc


def project_kernel(steps, at_ref, table_ref, q_all, top_ref, total_ref, acc_ref, *refs):
    kvs, w_any, keep_ref, send_ref = refs[:4], refs[4], refs[5], refs[6]
    w_ref, kv_ref, kp_ref, sems = refs[7:]
    rows = kvs[2].shape[0]
    places = [kv_ref.at[0], kv_ref.at[1]]
    places += [kv_ref.at[2, pl.ds(i * rows, rows)] for i in range(2)]
    copies = [pltpu.make_async_copy(kvs[i], places[i], sems.at[i]) for i in range(4)]
    copy = pltpu.make_async_copy(w_any, w_ref, sems.at[4])
    for one in copies:
        one.start()
    copy.start()
    carry = top_ref[:, :1], total_ref[:, :1], acc_ref[...]
    for one in copies:
        one.wait()
    top, total, acc = attend(at_ref, table_ref, q_all, kv_ref, kp_ref, steps, carry)
    tokens = kv_ref.shape[1] // 8
    half = tokens // 2
    summed = (acc / total).astype(bf16)
    heads = jnp.concatenate([summed[g * tokens : (g + 1) * tokens] for g in range(GROUP)], axis=1)
    copy.wait()
    width = 512

    @pl.loop(0, w_ref.shape[1] // width)
    def _(n):
        cols = pl.ds(pl.multiple_of(n * width, width), width)
        part = jnp.dot(heads, w_ref[:, cols], preferred_element_type=f32).astype(bf16)
        keep_ref[:, cols] = part[:half]
        send_ref[:, cols] = part[half:]


def norm_kernel(keep, near, far, residual, gain, gate_w, attended, normed_ref, prob):
    rows = far.shape[0]
    head_sum = keep[:rows, :].astype(f32) + near[:rows, :].astype(f32) + far[...].astype(f32)
    kept = (residual[...].astype(f32) + head_sum).astype(bf16)
    attended[...] = kept
    wide = kept.astype(f32)
    mean_square = jnp.mean(wide * wide, axis=-1, keepdims=True)
    normed = (wide * lax.rsqrt(mean_square + 1e-06) * gain[...].astype(f32)).astype(bf16)
    normed_ref[...] = normed
    logit = jnp.sum(normed.astype(f32) * gate_w[...].astype(f32), axis=-1, keepdims=True)
    prob[...] = jnp.broadcast_to(1.0 / (1.0 + jnp.exp(-logit)), prob.shape)


def send_kernel(core_ref, g_any, u_any, d_any, out_any, buf, in_sems, out_sems):
    n = out_any.shape[0] // 3
    at = pl.multiple_of(core_ref[0] * n, n)
    ins, outs = [], []
    for i, w in enumerate((g_any, u_any, d_any)):
        here = buf.at[pl.ds(i * n, n)]
        ins.append(pltpu.make_async_copy(w.at[pl.ds(at, n)], here, in_sems.at[i]))
        outs.append(pltpu.make_async_copy(here, out_any.at[pl.ds(i * n, n)], out_sems.at[i]))
    for copy in ins:
        copy.start()
    for copy, out in zip(ins, outs):
        copy.wait()
        out.start()
    for out in outs:
        out.wait()


def assemble_kernel(g_any, u_any, d_any, a_any, b_any, w_ref, d_ref, sems):
    own = g_any.shape[0]
    swap = a_any.shape[0] // 3
    block = 128
    copies = []

    def start(src, at, dst, to, n):
        copy = pltpu.make_async_copy(
            src.at[pl.ds(at, n)], dst.at[pl.ds(to, n)], sems.at[len(copies)]
        )
        copy.start()
        copies.append(copy)

    for part in range(2):
        pos = 0
        for source, at, length in (
            ((g_any, u_any)[part], 0, own),
            (a_any, part * swap, swap),
            (b_any, part * swap, swap),
        ):
            done = 0
            while done < length:
                b, inside = divmod(pos, block)
                n = min(block - inside, length - done)
                start(source, at + done, w_ref, b * 2 * block + part * block + inside, n)
                done += n
                pos += n
    start(d_any, 0, d_ref, 0, own)
    start(a_any, 2 * swap, d_ref, own, swap)
    start(b_any, 2 * swap, d_ref, own + swap, swap)
    for copy in copies:
        copy.wait()


def expert_kernel(count, *refs):
    xs, w_ref, d_ref, outs = refs[:count], refs[count], refs[count + 1], refs[count + 2 : -2]
    x_ref, h_ref = refs[-2:]
    at = 0
    for x in xs:
        x_ref[at : at + x.shape[0], :] = x[...]
        at += x.shape[0]
    block = 128

    @pl.loop(0, w_ref.shape[0] // (2 * block))
    def _(b):
        both = lax.dot_general(
            x_ref[...],
            w_ref[pl.ds(pl.multiple_of(b * 2 * block, 2 * block), 2 * block), :],
            (((1,), (1,)), ((), ())),
            preferred_element_type=f32,
        )
        gate, up = both[:, :block], both[:, block:]
        value = (gate / (1.0 + jnp.exp(-gate)) * up).astype(bf16)
        h_ref[:, pl.ds(pl.multiple_of(b * block, block), block)] = value

    width = 512

    @pl.loop(0, d_ref.shape[1] // width)
    def _(c):
        cols = pl.ds(pl.multiple_of(c * width, width), width)
        part = jnp.dot(h_ref[...], d_ref[:, cols], preferred_element_type=f32).astype(bf16)
        at = 0
        for out in outs:
            out[:, cols] = part[at : at + out.shape[0]]
            at += out.shape[0]


def join_kernel(*refs):
    out = refs[-1]
    n = refs[0].shape[0]
    for i, ref in enumerate(refs[:-1]):
        out[i * n : (i + 1) * n, :] = ref[...]


def join(xs):
    rows, width = xs[0].shape
    return pl.pallas_call(
        join_kernel,
        out_shape=jax.ShapeDtypeStruct((rows * len(xs), width), bf16),
        in_specs=[VMEM] * len(xs),
        out_specs=VMEM,
        compiler_params=SMALL,
        cost_estimate=pl.CostEstimate(
            flops=0, bytes_accessed=4 * rows * len(xs) * width, transcendentals=0
        ),
    )(*xs)


def expert(xs, weights, parts=None):
    w, d = weights
    rows, width = sum(x.shape[0] for x in xs), xs[0].shape[1]
    units = d.shape[0]
    parts = parts or [x.shape[0] for x in xs]
    return pl.pallas_call(
        functools.partial(expert_kernel, len(xs)),
        out_shape=[jax.ShapeDtypeStruct((n, width), bf16) for n in parts],
        in_specs=[VMEM] * (len(xs) + 2),
        out_specs=[VMEM] * len(parts),
        scratch_shapes=[pltpu.VMEM((rows, width), bf16), pltpu.VMEM((rows, units), bf16)],
        compiler_params=pltpu.CompilerParams(vmem_limit_bytes=30 << 20),
        cost_estimate=pl.CostEstimate(
            flops=6 * rows * units * width,
            bytes_accessed=6 * units * width + 4 * rows * width,
            transcendentals=rows * units,
        ),
    )(*xs, w, d)


def final_kernel(attended, prob, *refs):
    terms, out = refs[:-1], refs[-1]
    shared = terms[0][...].astype(f32)
    for term in terms[1:]:
        shared += term[...].astype(f32)
    out[...] = (attended[...].astype(f32) + prob[:, :1] * shared).astype(bf16)


def per_device(
    queries,
    keys,
    values,
    block_table,
    residual,
    out_weight,
    norm_gain,
    gate_logit_weight,
    gate_weight,
    up_weight,
    down_weight,
):
    tokens = queries.shape[0]
    half = tokens // 2
    quarter = tokens // 4
    width = residual.shape[1]
    hidden = down_weight.shape[0]
    y, z, xh = (lax.axis_index(a) for a in CTX)
    core = lax.axis_index("core")
    t = lax.axis_index(TP)

    gate_t, up_t = gate_weight.T, up_weight.T
    piece = hidden // 2
    kv = jnp.concatenate([keys, values], axis=1)
    kv = jnp.concatenate([kv, fetch(kv, "xh", 1)], axis=0)
    core_at, _ = lax.optimization_barrier((core.astype(jnp.int32)[None], kv))

    to_send = pl.pallas_call(
        send_kernel,
        out_shape=jax.ShapeDtypeStruct((3 * piece, width), bf16),
        in_specs=[SMEM, HBM, HBM, HBM],
        out_specs=HBM,
        scratch_shapes=[
            pltpu.VMEM((3 * piece, width), bf16),
            pltpu.SemaphoreType.DMA((3,)),
            pltpu.SemaphoreType.DMA((3,)),
        ],
        cost_estimate=pl.CostEstimate(
            flops=0, bytes_accessed=12 * piece * width, transcendentals=0
        ),
    )(core_at, gate_t, up_t, down_weight)
    swap_a = lax.ppermute(to_send, ("xh", "xl"), [(0, 3), (3, 0), (1, 2), (2, 1)])

    kv = jnp.concatenate(gather_direct(kv, "y"), axis=0)
    ahead, behind = gather_ring(kv, "z")
    far = gather_far(ahead[3], behind[3], "z")
    at = jnp.stack([y, z, xh, t]).astype(jnp.int32)

    rows = GROUP * tokens
    piece_rows = kv.shape[0]
    steps = (0, 1, 7, 2, 6)
    state = pl.pallas_call(
        functools.partial(attention_kernel, steps),
        out_shape=[jax.ShapeDtypeStruct((rows, HEAD_DIM), bf16)]
        + [jax.ShapeDtypeStruct((rows, HEAD_DIM), f32)] * 3,
        in_specs=[SMEM, SMEM, VMEM] + [HBM] * 5,
        out_specs=[VMEM] * 4,
        scratch_shapes=[
            pltpu.VMEM((5,) + kv.shape, bf16),
            pltpu.VMEM((8, piece_rows), jnp.int32),
            pltpu.SemaphoreType.DMA((5,)),
        ],
        compiler_params=pltpu.CompilerParams(vmem_limit_bytes=16 << 20),
        cost_estimate=pl.CostEstimate(
            flops=20 * rows * piece_rows * HEAD_DIM,
            bytes_accessed=20 * piece_rows * HEAD_DIM,
            transcendentals=5 * rows * piece_rows,
        ),
    )(at, block_table, queries, ahead[0], ahead[1], behind[1], ahead[2], behind[2])
    steps = (3, 5, 4)
    keep, send = pl.pallas_call(
        functools.partial(project_kernel, steps),
        out_shape=[jax.ShapeDtypeStruct((half, width), bf16)] * 2,
        in_specs=[SMEM, SMEM] + [VMEM] * 4 + [HBM] * 5,
        out_specs=[VMEM] * 2,
        scratch_shapes=[
            pltpu.VMEM(out_weight.shape, bf16),
            pltpu.VMEM((3,) + kv.shape, bf16),
            pltpu.VMEM((8, piece_rows), jnp.int32),
            pltpu.SemaphoreType.DMA((5,)),
        ],
        compiler_params=pltpu.CompilerParams(vmem_limit_bytes=46 << 20),
        cost_estimate=pl.CostEstimate(
            flops=12 * rows * piece_rows * HEAD_DIM + 2 * tokens * out_weight.size,
            bytes_accessed=2 * out_weight.size + 12 * piece_rows * HEAD_DIM,
            transcendentals=3 * rows * piece_rows,
        ),
    )(at, block_table, *state, ahead[3], behind[3], *far, out_weight)

    near = fetch(send, "core", 1)
    _, beyond = add([keep, near], pieces=2)
    beyond = fetch(beyond, "xl", 1)
    attended, normed, prob = pl.pallas_call(
        norm_kernel,
        out_shape=[
            jax.ShapeDtypeStruct((quarter, width), bf16),
            jax.ShapeDtypeStruct((quarter, width), bf16),
            jax.ShapeDtypeStruct((quarter, 128), f32),
        ],
        in_specs=[VMEM] * 6,
        out_specs=[VMEM] * 3,
        compiler_params=SMALL,
        cost_estimate=pl.CostEstimate(
            flops=10 * quarter * width, bytes_accessed=14 * quarter * width, transcendentals=quarter
        ),
    )(keep, near, beyond, residual, norm_gain[None, :], gate_logit_weight[None, :])

    by_y = join(gather_direct(normed, "y"))
    ahead, behind = gather_ring(by_y, "z")
    swap_a, _ = lax.optimization_barrier((swap_a, (ahead[1], behind[1])))
    swap_b = fetch(swap_a, "core", 1)
    weights = pl.pallas_call(
        assemble_kernel,
        out_shape=[
            jax.ShapeDtypeStruct((4 * hidden, width), bf16),
            jax.ShapeDtypeStruct((2 * hidden, width), bf16),
        ],
        in_specs=[HBM] * 5,
        out_specs=[VMEM] * 2,
        scratch_shapes=[pltpu.SemaphoreType.DMA((24,))],
        compiler_params=pltpu.CompilerParams(vmem_limit_bytes=16 << 20),
        cost_estimate=pl.CostEstimate(
            flops=0, bytes_accessed=12 * hidden * width, transcendentals=0
        ),
    )(gate_t, up_t, down_weight, swap_a, swap_b)
    ahead_3, behind_3, weights = lax.optimization_barrier((ahead[3], behind[3], weights))
    far = gather_far(ahead_3, behind_3, "z")
    after_2, before_2, *third = expert(
        [ahead[2], behind[2], ahead[3], behind[3]], weights, [tokens] * 2 + [half] * 4
    )
    weights, third = lax.optimization_barrier((weights, third))
    far_parts = expert(far, weights)
    own, after, before = expert([ahead[0], ahead[1], behind[1]], weights)
    near_parts = [own, after, after_2, third[:2], None, third[2:], before_2, before]
    by_y = add(scatter_ring(near_parts, far_parts, "z"), pieces=4)
    terms = scatter_direct(by_y, "y")
    return pl.pallas_call(
        final_kernel,
        out_shape=jax.ShapeDtypeStruct((quarter, width), bf16),
        in_specs=[VMEM] * 6,
        out_specs=VMEM,
        compiler_params=SMALL,
        cost_estimate=pl.CostEstimate(
            flops=10 * quarter * width, bytes_accessed=16 * quarter * width, transcendentals=0
        ),
    )(attended, prob, *terms)


def solution(mesh):
    fine = Mesh(mesh.devices.reshape(tuple(SIZES.values())), tuple(SIZES))
    return jax.shard_map(
        per_device,
        mesh=fine,
        in_specs=(
            P(CTX, TP),
            P(CTX, TP),
            P(CTX, TP),
            P(),
            P(CTX + TP, None),
            P(TP, None),
            P(),
            P(),
            P(None, CTX),
            P(None, CTX),
            P(CTX, None),
        ),
        out_specs=P(CTX + TP, None),
        check_vma=False,
    )
```

```python
import functools

import jax
import jax.numpy as jnp
from jax import lax
from jax.experimental import pallas as pl
from jax.experimental.pallas import tpu as pltpu
from jax.sharding import Mesh
from jax.sharding import PartitionSpec as P

HEADS = 28
KV_HEADS = 4
HEAD_DIM = 128
GROUP = HEADS // KV_HEADS
SIZES = {"y": 4, "z": 8, "xh": 2, "xl": 2, "core": 2}
CTX = ("y", "z", "xh")
TP = ("xl", "core")
f32 = jnp.float32
bf16 = jnp.bfloat16
VMEM = pl.BlockSpec(memory_space=pltpu.VMEM)
SMEM = pl.BlockSpec(memory_space=pltpu.SMEM)
HBM = pl.BlockSpec(memory_space=pltpu.HBM)
SMALL = pltpu.CompilerParams(vmem_limit_bytes=8 << 20)
NEG = -1e30
FLOOR = -1e29
EXP2 = 1.4426950408889634


def fetch(x, axis, k):
    n = SIZES[axis]
    k %= n
    if k == 0:
        return x
    return lax.ppermute(x, axis, [((i + k) % n, i) for i in range(n)])


def gather_direct(x, axis):
    return [fetch(x, axis, k) for k in range(SIZES[axis])]


def gather_ring(x, axis):
    n = SIZES[axis]
    h = n // 2
    ahead, behind = [x], [x]
    for k in range(1, h):
        ahead.append(fetch(ahead[-1], axis, 1))
        behind.append(fetch(behind[-1], axis, -1))
    return ahead, behind


def gather_far(ahead, behind, axis):
    rows = ahead.shape[0] // 2
    return [fetch(ahead[:rows], axis, 1), fetch(behind[rows:], axis, -1)]


def add_kernel(n_in, first, *refs):
    ins, outs = refs[:n_in], refs[n_in:]
    rows = outs[0].shape[0]
    for i, out in enumerate(outs):
        part = ins[0][i * rows : (i + 1) * rows, :].astype(f32)
        for other in ins[1:]:
            if other.shape[0] == ins[0].shape[0]:
                part += other[i * rows : (i + 1) * rows, :].astype(f32)
        out[...] = part.astype(out.dtype)
    last = ins[-1]
    if last.shape[0] < ins[0].shape[0]:
        mine = slice(first, first + last.shape[0])
        outs[0][mine, :] = (ins[0][mine, :].astype(f32) + last[...].astype(f32)).astype(bf16)


def add(xs, pieces=1, first=0):
    rows, width = xs[0].shape
    size = rows * width
    out = pl.pallas_call(
        functools.partial(add_kernel, len(xs), first),
        out_shape=[jax.ShapeDtypeStruct((rows // pieces, width), bf16)] * pieces,
        in_specs=[VMEM] * len(xs),
        out_specs=[VMEM] * pieces,
        compiler_params=SMALL,
        cost_estimate=pl.CostEstimate(
            flops=size * len(xs), bytes_accessed=2 * size * (len(xs) + 1), transcendentals=0
        ),
    )(*xs)
    return out[0] if pieces == 1 else out


def scatter_direct(chunks, axis):
    return [chunks[0]] + [fetch(chunks[k], axis, -k) for k in range(1, SIZES[axis])]


def scatter_ring(near, far, axis):
    n = SIZES[axis]
    h = n // 2
    up = fetch(far[0], axis, -1)
    down = fetch(far[1], axis, 1)
    for k in range(h - 1, 0, -1):
        first = near[k].shape[0] - down.shape[0]
        up = fetch(add([near[k], up]), axis, -1)
        down = fetch(add([near[n - k], down], first=first), axis, 1)
    return [near[0], up, down]


def attend(at_ref, table_ref, q_all, kv_ref, kp_ref, steps, carry, unroll):
    y, z, xh, t = (at_ref[i] for i in range(4))
    count = kv_ref.shape[1]
    tokens = count // 8
    half = tokens // 2
    quarter = tokens // 4
    mirror = 2 * table_ref.shape[0] - 1

    def place(pair, local):
        return jnp.where(local < half, pair * half + local, (mirror - pair) * half + local - half)

    def pair_of(dy, dz, dx):
        slot = ((y + dy) % 4 * 8 + (z + dz) % 8) * 2 + (xh + dx) % 2
        return table_ref[slot]

    lane = lax.broadcasted_iota(jnp.int32, (1, count), 1)
    for j, dz in enumerate(steps):
        pair = jnp.zeros_like(lane)
        for b in range(8):
            pair = jnp.where(lane // tokens == b, pair_of(b // 2, dz, b % 2), pair)
        kp_ref[j : j + 1, :] = place(pair, lane % tokens)
    row = lax.broadcasted_iota(jnp.int32, (tokens, 1), 0)
    order = row // quarter
    order = (order % 2) * 2 + order // 2
    qp = place(pair_of(0, 0, 0), (order ^ t) * quarter + row % quarter)

    def step(j, carry):
        top, total, acc = carry
        k = kv_ref[j, :, :HEAD_DIM]
        v = kv_ref[j, :, HEAD_DIM:]
        score = lax.dot_general(
            q_all[...], k, (((1,), (1,)), ((), ())), preferred_element_type=f32
        )
        score = score * (HEAD_DIM**-0.5 * EXP2)
        visible = kp_ref[pl.ds(j, 1), :] <= qp
        score = jnp.where(visible[None], score.reshape(GROUP, tokens, count), NEG)
        score = score.reshape(GROUP * tokens, count)
        new_top = jnp.maximum(top, jnp.max(score, axis=-1, keepdims=True))
        weight = jnp.exp2(score - new_top)
        keep = jnp.exp2(top - new_top)
        total = total * keep + jnp.sum(weight, axis=-1, keepdims=True)
        acc = acc * keep + jnp.dot(weight.astype(bf16), v, preferred_element_type=f32)
        return new_top, total, acc

    return lax.fori_loop(0, len(steps), step, carry, unroll=unroll)


def attention_kernel(steps, at_ref, table_ref, q_ref, *refs):
    n = len(steps)
    kvs, (q_all, top_ref, total_ref, acc_ref) = refs[:n], refs[n : n + 4]
    kv_ref, kp_ref, sems = refs[n + 4 :]
    copies = [pltpu.make_async_copy(kvs[i], kv_ref.at[i], sems.at[i]) for i in range(n)]
    for one in copies:
        one.start()
    t = at_ref[3]
    tokens = q_ref.shape[0]
    quarter = tokens // 4
    parts = [
        q_ref[pl.ds(pl.multiple_of((t ^ k) * quarter, quarter), quarter), :] for k in (0, 2, 1, 3)
    ]
    q = jnp.concatenate(parts, axis=0)
    for g in range(GROUP):
        q_all[g * tokens : (g + 1) * tokens, :] = q[:, g * HEAD_DIM : (g + 1) * HEAD_DIM]
    rows = GROUP * tokens
    carry = (
        jnp.full((rows, 1), FLOOR, f32),
        jnp.zeros((rows, 1), f32),
        jnp.zeros((rows, HEAD_DIM), f32),
    )
    for one in copies:
        one.wait()
    top, total, acc = attend(at_ref, table_ref, q_all, kv_ref, kp_ref, steps, carry, False)
    top_ref[...] = jnp.broadcast_to(top, top_ref.shape)
    total_ref[...] = jnp.broadcast_to(total, total_ref.shape)
    acc_ref[...] = acc


def project_kernel(steps, at_ref, table_ref, q_all, top_ref, total_ref, acc_ref, *refs):
    kvs, w_any, keep_ref, send_ref = refs[:4], refs[4], refs[5], refs[6]
    w_ref, kv_ref, kp_ref, sems = refs[7:]
    rows = kvs[2].shape[0]
    places = [kv_ref.at[0], kv_ref.at[1]]
    places += [kv_ref.at[2, pl.ds(i * rows, rows)] for i in range(2)]
    copies = [pltpu.make_async_copy(kvs[i], places[i], sems.at[i]) for i in range(4)]
    copy = pltpu.make_async_copy(w_any, w_ref, sems.at[4])
    for one in copies:
        one.start()
    copy.start()
    carry = top_ref[:, :1], total_ref[:, :1], acc_ref[...]
    for one in copies:
        one.wait()
    top, total, acc = attend(at_ref, table_ref, q_all, kv_ref, kp_ref, steps, carry, False)
    tokens = kv_ref.shape[1] // 8
    half = tokens // 2
    summed = (acc / total).astype(bf16)
    heads = jnp.concatenate([summed[g * tokens : (g + 1) * tokens] for g in range(GROUP)], axis=1)
    copy.wait()
    width = 512
    for n in range(w_ref.shape[1] // width):
        cols = slice(n * width, (n + 1) * width)
        part = jnp.dot(heads, w_ref[:, cols], preferred_element_type=f32).astype(bf16)
        keep_ref[:, cols] = part[:half]
        send_ref[:, cols] = part[half:]


def norm_kernel(keep, near, far, residual, gain, gate_w, attended, normed_ref, prob):
    rows = far.shape[0]
    head_sum = keep[:rows, :].astype(f32) + near[:rows, :].astype(f32) + far[...].astype(f32)
    kept = (residual[...].astype(f32) + head_sum).astype(bf16)
    attended[...] = kept
    wide = kept.astype(f32)
    mean_square = jnp.mean(wide * wide, axis=-1, keepdims=True)
    normed = (wide * lax.rsqrt(mean_square + 1e-06) * gain[...].astype(f32)).astype(bf16)
    normed_ref[...] = normed
    logit = jnp.sum(normed.astype(f32) * gate_w[...].astype(f32), axis=-1, keepdims=True)
    prob[...] = jnp.broadcast_to(1.0 / (1.0 + jnp.exp(-logit)), prob.shape)


def send_kernel(core_ref, g_any, u_any, d_any, out_any, buf, in_sems, out_sems):
    n = out_any.shape[0] // 3
    at = pl.multiple_of(core_ref[0] * n, n)
    ins, outs = [], []
    for i, w in enumerate((g_any, u_any, d_any)):
        here = buf.at[pl.ds(i * n, n)]
        ins.append(pltpu.make_async_copy(w.at[pl.ds(at, n)], here, in_sems.at[i]))
        outs.append(pltpu.make_async_copy(here, out_any.at[pl.ds(i * n, n)], out_sems.at[i]))
    for copy in ins:
        copy.start()
    for copy, out in zip(ins, outs):
        copy.wait()
        out.start()
    for out in outs:
        out.wait()


def assemble_kernel(g_any, u_any, d_any, a_any, b_any, w_ref, d_ref, sems):
    own = g_any.shape[0]
    swap = a_any.shape[0] // 3
    block = 128
    copies = []

    def start(src, at, dst, to, n):
        copy = pltpu.make_async_copy(
            src.at[pl.ds(at, n)], dst.at[pl.ds(to, n)], sems.at[len(copies)]
        )
        copy.start()
        copies.append(copy)

    for part in range(2):
        pos = 0
        for source, at, length in (
            ((g_any, u_any)[part], 0, own),
            (a_any, part * swap, swap),
            (b_any, part * swap, swap),
        ):
            done = 0
            while done < length:
                b, inside = divmod(pos, block)
                n = min(block - inside, length - done)
                start(source, at + done, w_ref, b * 2 * block + part * block + inside, n)
                done += n
                pos += n
    start(d_any, 0, d_ref, 0, own)
    start(a_any, 2 * swap, d_ref, own, swap)
    start(b_any, 2 * swap, d_ref, own + swap, swap)
    for copy in copies:
        copy.wait()


def aligned(i, step):
    return i * step if isinstance(i, int) else pl.multiple_of(i * step, step)


def repeat(count, unroll, body):
    if unroll:
        for i in range(count):
            body(i)
    else:
        pl.loop(0, count)(body)


def expert_kernel(count, unroll, *refs):
    xs, w_ref, d_ref, outs = refs[:count], refs[count], refs[count + 1], refs[count + 2 : -2]
    x_ref, h_ref = refs[-2:]
    at = 0
    for x in xs:
        x_ref[at : at + x.shape[0], :] = x[...]
        at += x.shape[0]
    block = 128

    def gate_and_up(b):
        both = lax.dot_general(
            x_ref[...],
            w_ref[pl.ds(aligned(b, 2 * block), 2 * block), :],
            (((1,), (1,)), ((), ())),
            preferred_element_type=f32,
        )
        gate, up = both[:, :block], both[:, block:]
        value = (gate / (1.0 + jnp.exp(-gate)) * up).astype(bf16)
        h_ref[:, pl.ds(aligned(b, block), block)] = value

    repeat(w_ref.shape[0] // (2 * block), unroll, gate_and_up)
    width = 256 if unroll else 512

    def down(c):
        cols = pl.ds(aligned(c, width), width)
        part = jnp.dot(h_ref[...], d_ref[:, cols], preferred_element_type=f32).astype(bf16)
        at = 0
        for out in outs:
            out[:, cols] = part[at : at + out.shape[0]]
            at += out.shape[0]

    repeat(d_ref.shape[1] // width, unroll, down)


def join_kernel(*refs):
    out = refs[-1]
    n = refs[0].shape[0]
    for i, ref in enumerate(refs[:-1]):
        out[i * n : (i + 1) * n, :] = ref[...]


def join(xs):
    rows, width = xs[0].shape
    return pl.pallas_call(
        join_kernel,
        out_shape=jax.ShapeDtypeStruct((rows * len(xs), width), bf16),
        in_specs=[VMEM] * len(xs),
        out_specs=VMEM,
        compiler_params=SMALL,
        cost_estimate=pl.CostEstimate(
            flops=0, bytes_accessed=4 * rows * len(xs) * width, transcendentals=0
        ),
    )(*xs)


def expert(xs, weights, unroll):
    w, d = weights
    rows, width = sum(x.shape[0] for x in xs), xs[0].shape[1]
    units = d.shape[0]
    return pl.pallas_call(
        functools.partial(expert_kernel, len(xs), unroll),
        out_shape=[jax.ShapeDtypeStruct(x.shape, bf16) for x in xs],
        in_specs=[VMEM] * (len(xs) + 2),
        out_specs=[VMEM] * len(xs),
        scratch_shapes=[pltpu.VMEM((rows, width), bf16), pltpu.VMEM((rows, units), bf16)],
        compiler_params=pltpu.CompilerParams(vmem_limit_bytes=30 << 20),
        cost_estimate=pl.CostEstimate(
            flops=6 * rows * units * width,
            bytes_accessed=6 * units * width + 4 * rows * width,
            transcendentals=rows * units,
        ),
    )(*xs, w, d)


def final_kernel(attended, prob, *refs):
    terms, out = refs[:-1], refs[-1]
    shared = terms[0][...].astype(f32)
    for term in terms[1:]:
        shared += term[...].astype(f32)
    out[...] = (attended[...].astype(f32) + prob[:, :1] * shared).astype(bf16)


def per_device(
    queries,
    keys,
    values,
    block_table,
    residual,
    out_weight,
    norm_gain,
    gate_logit_weight,
    gate_weight,
    up_weight,
    down_weight,
):
    tokens = queries.shape[0]
    half = tokens // 2
    quarter = tokens // 4
    width = residual.shape[1]
    hidden = down_weight.shape[0]
    y, z, xh = (lax.axis_index(a) for a in CTX)
    core = lax.axis_index("core")
    t = lax.axis_index(TP)

    gate_t, up_t = gate_weight.T, up_weight.T
    piece = hidden // 2
    kv = jnp.concatenate([keys, values], axis=1)
    kv = jnp.concatenate([kv, fetch(kv, "xh", 1)], axis=0)
    core_at, _ = lax.optimization_barrier((core.astype(jnp.int32)[None], kv))

    to_send = pl.pallas_call(
        send_kernel,
        out_shape=jax.ShapeDtypeStruct((3 * piece, width), bf16),
        in_specs=[SMEM, HBM, HBM, HBM],
        out_specs=HBM,
        scratch_shapes=[
            pltpu.VMEM((3 * piece, width), bf16),
            pltpu.SemaphoreType.DMA((3,)),
            pltpu.SemaphoreType.DMA((3,)),
        ],
        cost_estimate=pl.CostEstimate(
            flops=0, bytes_accessed=12 * piece * width, transcendentals=0
        ),
    )(core_at, gate_t, up_t, down_weight)
    swap_a = lax.ppermute(to_send, ("xh", "xl"), [(0, 3), (3, 0), (1, 2), (2, 1)])

    kv = jnp.concatenate(gather_direct(kv, "y"), axis=0)
    ahead, behind = gather_ring(kv, "z")
    far = gather_far(ahead[3], behind[3], "z")
    at = jnp.stack([y, z, xh, t]).astype(jnp.int32)

    rows = GROUP * tokens
    piece_rows = kv.shape[0]
    steps = (0, 1, 7, 2, 6)
    state = pl.pallas_call(
        functools.partial(attention_kernel, steps),
        out_shape=[jax.ShapeDtypeStruct((rows, HEAD_DIM), bf16)]
        + [jax.ShapeDtypeStruct((rows, HEAD_DIM), f32)] * 3,
        in_specs=[SMEM, SMEM, VMEM] + [HBM] * 5,
        out_specs=[VMEM] * 4,
        scratch_shapes=[
            pltpu.VMEM((5,) + kv.shape, bf16),
            pltpu.VMEM((8, piece_rows), jnp.int32),
            pltpu.SemaphoreType.DMA((5,)),
        ],
        compiler_params=pltpu.CompilerParams(vmem_limit_bytes=16 << 20),
        cost_estimate=pl.CostEstimate(
            flops=20 * rows * piece_rows * HEAD_DIM,
            bytes_accessed=20 * piece_rows * HEAD_DIM,
            transcendentals=5 * rows * piece_rows,
        ),
    )(at, block_table, queries, ahead[0], ahead[1], behind[1], ahead[2], behind[2])
    steps = (3, 5, 4)
    keep, send = pl.pallas_call(
        functools.partial(project_kernel, steps),
        out_shape=[jax.ShapeDtypeStruct((half, width), bf16)] * 2,
        in_specs=[SMEM, SMEM] + [VMEM] * 4 + [HBM] * 5,
        out_specs=[VMEM] * 2,
        scratch_shapes=[
            pltpu.VMEM(out_weight.shape, bf16),
            pltpu.VMEM((3,) + kv.shape, bf16),
            pltpu.VMEM((8, piece_rows), jnp.int32),
            pltpu.SemaphoreType.DMA((5,)),
        ],
        compiler_params=pltpu.CompilerParams(vmem_limit_bytes=46 << 20),
        cost_estimate=pl.CostEstimate(
            flops=12 * rows * piece_rows * HEAD_DIM + 2 * tokens * out_weight.size,
            bytes_accessed=2 * out_weight.size + 12 * piece_rows * HEAD_DIM,
            transcendentals=3 * rows * piece_rows,
        ),
    )(at, block_table, *state, ahead[3], behind[3], *far, out_weight)

    near = fetch(send, "core", 1)
    _, beyond = add([keep, near], pieces=2)
    beyond = fetch(beyond, "xl", 1)
    attended, normed, prob = pl.pallas_call(
        norm_kernel,
        out_shape=[
            jax.ShapeDtypeStruct((quarter, width), bf16),
            jax.ShapeDtypeStruct((quarter, width), bf16),
            jax.ShapeDtypeStruct((quarter, 128), f32),
        ],
        in_specs=[VMEM] * 6,
        out_specs=[VMEM] * 3,
        compiler_params=SMALL,
        cost_estimate=pl.CostEstimate(
            flops=10 * quarter * width, bytes_accessed=14 * quarter * width, transcendentals=quarter
        ),
    )(keep, near, beyond, residual, norm_gain[None, :], gate_logit_weight[None, :])

    by_y = join(gather_direct(normed, "y"))
    ahead, behind = gather_ring(by_y, "z")
    swap_a, _ = lax.optimization_barrier((swap_a, (ahead[1], behind[1])))
    swap_b = fetch(swap_a, "core", 1)
    weights = pl.pallas_call(
        assemble_kernel,
        out_shape=[
            jax.ShapeDtypeStruct((4 * hidden, width), bf16),
            jax.ShapeDtypeStruct((2 * hidden, width), bf16),
        ],
        in_specs=[HBM] * 5,
        out_specs=[VMEM] * 2,
        scratch_shapes=[pltpu.SemaphoreType.DMA((24,))],
        compiler_params=pltpu.CompilerParams(vmem_limit_bytes=16 << 20),
        cost_estimate=pl.CostEstimate(
            flops=0, bytes_accessed=12 * hidden * width, transcendentals=0
        ),
    )(gate_t, up_t, down_weight, swap_a, swap_b)
    ahead_3, behind_3, weights = lax.optimization_barrier((ahead[3], behind[3], weights))
    far = gather_far(ahead_3, behind_3, "z")
    after_2, before_2, after_3, before_3 = expert(
        [ahead[2], behind[2], ahead[3], behind[3]], weights, False
    )
    weights, after_3 = lax.optimization_barrier((weights, after_3))
    far_parts = expert(far, weights, True)
    own, after, before = expert([ahead[0], ahead[1], behind[1]], weights, False)
    near_parts = [own, after, after_2, after_3, None, before_3, before_2, before]
    by_y = add(scatter_ring(near_parts, far_parts, "z"), pieces=4)
    terms = scatter_direct(by_y, "y")
    return pl.pallas_call(
        final_kernel,
        out_shape=jax.ShapeDtypeStruct((quarter, width), bf16),
        in_specs=[VMEM] * 6,
        out_specs=VMEM,
        compiler_params=SMALL,
        cost_estimate=pl.CostEstimate(
            flops=10 * quarter * width, bytes_accessed=16 * quarter * width, transcendentals=0
        ),
    )(attended, prob, *terms)


def solution(mesh):
    fine = Mesh(mesh.devices.reshape(tuple(SIZES.values())), tuple(SIZES))
    return jax.shard_map(
        per_device,
        mesh=fine,
        in_specs=(
            P(CTX, TP),
            P(CTX, TP),
            P(CTX, TP),
            P(),
            P(CTX + TP, None),
            P(TP, None),
            P(),
            P(),
            P(None, CTX),
            P(None, CTX),
            P(CTX, None),
        ),
        out_specs=P(CTX + TP, None),
        check_vma=False,
    )
```

```python
import functools

import jax
import jax.numpy as jnp
from jax import lax
from jax.experimental import pallas as pl
from jax.experimental.pallas import tpu as pltpu
from jax.sharding import Mesh
from jax.sharding import PartitionSpec as P

HEADS = 28
KV_HEADS = 4
HEAD_DIM = 128
GROUP = HEADS // KV_HEADS
SIZES = {"y": 4, "z": 8, "xh": 2, "xl": 2, "core": 2}
CTX = ("y", "z", "xh")
TP = ("xl", "core")
f32 = jnp.float32
bf16 = jnp.bfloat16
VMEM = pl.BlockSpec(memory_space=pltpu.VMEM)
SMEM = pl.BlockSpec(memory_space=pltpu.SMEM)
HBM = pl.BlockSpec(memory_space=pltpu.HBM)
SMALL = pltpu.CompilerParams(vmem_limit_bytes=8 << 20)
NEG = -1e30
FLOOR = -1e29
EXP2 = 1.4426950408889634


def fetch(x, axis, k):
    n = SIZES[axis]
    k %= n
    if k == 0:
        return x
    return lax.ppermute(x, axis, [((i + k) % n, i) for i in range(n)])


def gather_direct(x, axis):
    return [fetch(x, axis, k) for k in range(SIZES[axis])]


def gather_ring(x, axis):
    n = SIZES[axis]
    h = n // 2
    ahead, behind = [x], [x]
    for k in range(1, h):
        ahead.append(fetch(ahead[-1], axis, 1))
        behind.append(fetch(behind[-1], axis, -1))
    return ahead, behind


def gather_far(ahead, behind, axis):
    rows = ahead.shape[0] // 2
    return [fetch(ahead[:rows], axis, 1), fetch(behind[rows:], axis, -1)]


def add_kernel(n_in, first, *refs):
    ins, outs = refs[:n_in], refs[n_in:]
    rows = outs[0].shape[0]
    for i, out in enumerate(outs):
        part = ins[0][i * rows : (i + 1) * rows, :].astype(f32)
        for other in ins[1:]:
            if other.shape[0] == ins[0].shape[0]:
                part += other[i * rows : (i + 1) * rows, :].astype(f32)
        out[...] = part.astype(out.dtype)
    last = ins[-1]
    if last.shape[0] < ins[0].shape[0]:
        mine = slice(first, first + last.shape[0])
        outs[0][mine, :] = (ins[0][mine, :].astype(f32) + last[...].astype(f32)).astype(bf16)


def add(xs, pieces=1, first=0):
    rows, width = xs[0].shape
    size = rows * width
    out = pl.pallas_call(
        functools.partial(add_kernel, len(xs), first),
        out_shape=[jax.ShapeDtypeStruct((rows // pieces, width), bf16)] * pieces,
        in_specs=[VMEM] * len(xs),
        out_specs=[VMEM] * pieces,
        compiler_params=SMALL,
        cost_estimate=pl.CostEstimate(
            flops=size * len(xs), bytes_accessed=2 * size * (len(xs) + 1), transcendentals=0
        ),
    )(*xs)
    return out[0] if pieces == 1 else out


def scatter_direct(chunks, axis):
    return [chunks[0]] + [fetch(chunks[k], axis, -k) for k in range(1, SIZES[axis])]


def scatter_ring(near, far, axis):
    n = SIZES[axis]
    h = n // 2
    up = fetch(far[0], axis, -1)
    down = fetch(far[1], axis, 1)
    for k in range(h - 1, 0, -1):
        first = near[k].shape[0] - down.shape[0]
        up = fetch(add([near[k], up]), axis, -1)
        down = fetch(add([near[n - k], down], first=first), axis, 1)
    return [near[0], up, down]


def attend(at_ref, table_ref, q_all, kv_ref, kp_ref, steps, carry, unroll):
    y, z, xh, t = (at_ref[i] for i in range(4))
    count = kv_ref.shape[1]
    tokens = count // 8
    half = tokens // 2
    quarter = tokens // 4
    mirror = 2 * table_ref.shape[0] - 1

    def place(pair, local):
        return jnp.where(local < half, pair * half + local, (mirror - pair) * half + local - half)

    def pair_of(dy, dz, dx):
        slot = ((y + dy) % 4 * 8 + (z + dz) % 8) * 2 + (xh + dx) % 2
        return table_ref[slot]

    lane = lax.broadcasted_iota(jnp.int32, (1, count), 1)
    for j, dz in enumerate(steps):
        pair = jnp.zeros_like(lane)
        for b in range(8):
            pair = jnp.where(lane // tokens == b, pair_of(b // 2, dz, b % 2), pair)
        kp_ref[j : j + 1, :] = place(pair, lane % tokens)
    row = lax.broadcasted_iota(jnp.int32, (tokens, 1), 0)
    order = row // quarter
    order = (order % 2) * 2 + order // 2
    qp = place(pair_of(0, 0, 0), (order ^ t) * quarter + row % quarter)

    def step(j, carry):
        top, total, acc = carry
        k = kv_ref[j, :, :HEAD_DIM]
        v = kv_ref[j, :, HEAD_DIM:]
        score = lax.dot_general(
            q_all[...], k, (((1,), (1,)), ((), ())), preferred_element_type=f32
        )
        score = score * (HEAD_DIM**-0.5 * EXP2)
        visible = kp_ref[pl.ds(j, 1), :] <= qp
        score = jnp.where(visible[None], score.reshape(GROUP, tokens, count), NEG)
        score = score.reshape(GROUP * tokens, count)
        new_top = jnp.maximum(top, jnp.max(score, axis=-1, keepdims=True))
        weight = jnp.exp2(score - new_top)
        keep = jnp.exp2(top - new_top)
        total = total * keep + jnp.sum(weight, axis=-1, keepdims=True)
        acc = acc * keep + jnp.dot(weight.astype(bf16), v, preferred_element_type=f32)
        return new_top, total, acc

    return lax.fori_loop(0, len(steps), step, carry, unroll=unroll)


def attention_kernel(steps, at_ref, table_ref, q_ref, *refs):
    n = len(steps)
    kvs, (q_all, top_ref, total_ref, acc_ref) = refs[:n], refs[n : n + 4]
    kv_ref, kp_ref, sems = refs[n + 4 :]
    copies = [pltpu.make_async_copy(kvs[i], kv_ref.at[i], sems.at[i]) for i in range(n)]
    for one in copies:
        one.start()
    t = at_ref[3]
    tokens = q_ref.shape[0]
    quarter = tokens // 4
    parts = [
        q_ref[pl.ds(pl.multiple_of((t ^ k) * quarter, quarter), quarter), :] for k in (0, 2, 1, 3)
    ]
    q = jnp.concatenate(parts, axis=0)
    for g in range(GROUP):
        q_all[g * tokens : (g + 1) * tokens, :] = q[:, g * HEAD_DIM : (g + 1) * HEAD_DIM]
    rows = GROUP * tokens
    carry = (
        jnp.full((rows, 1), FLOOR, f32),
        jnp.zeros((rows, 1), f32),
        jnp.zeros((rows, HEAD_DIM), f32),
    )
    for one in copies:
        one.wait()
    top, total, acc = attend(at_ref, table_ref, q_all, kv_ref, kp_ref, steps, carry, False)
    top_ref[...] = jnp.broadcast_to(top, top_ref.shape)
    total_ref[...] = jnp.broadcast_to(total, total_ref.shape)
    acc_ref[...] = acc


def project_kernel(steps, at_ref, table_ref, q_all, top_ref, total_ref, acc_ref, *refs):
    kvs, w_any, keep_ref, send_ref = refs[:4], refs[4], refs[5], refs[6]
    w_ref, kv_ref, kp_ref, sems = refs[7:]
    rows = kvs[2].shape[0]
    places = [kv_ref.at[0], kv_ref.at[1]]
    places += [kv_ref.at[2, pl.ds(i * rows, rows)] for i in range(2)]
    copies = [pltpu.make_async_copy(kvs[i], places[i], sems.at[i]) for i in range(4)]
    copy = pltpu.make_async_copy(w_any, w_ref, sems.at[4])
    for one in copies:
        one.start()
    copy.start()
    carry = top_ref[:, :1], total_ref[:, :1], acc_ref[...]
    for one in copies:
        one.wait()
    top, total, acc = attend(at_ref, table_ref, q_all, kv_ref, kp_ref, steps, carry, False)
    tokens = kv_ref.shape[1] // 8
    half = tokens // 2
    summed = (acc / total).astype(bf16)
    heads = jnp.concatenate([summed[g * tokens : (g + 1) * tokens] for g in range(GROUP)], axis=1)
    copy.wait()
    width = 512
    for n in range(w_ref.shape[1] // width):
        cols = slice(n * width, (n + 1) * width)
        part = jnp.dot(heads, w_ref[:, cols], preferred_element_type=f32).astype(bf16)
        keep_ref[:, cols] = part[:half]
        send_ref[:, cols] = part[half:]


def norm_kernel(keep, near, far, residual, gain, gate_w, attended, normed_ref, prob):
    rows = far.shape[0]
    head_sum = keep[:rows, :].astype(f32) + near[:rows, :].astype(f32) + far[...].astype(f32)
    kept = (residual[...].astype(f32) + head_sum).astype(bf16)
    attended[...] = kept
    wide = kept.astype(f32)
    mean_square = jnp.mean(wide * wide, axis=-1, keepdims=True)
    normed = (wide * lax.rsqrt(mean_square + 1e-06) * gain[...].astype(f32)).astype(bf16)
    normed_ref[...] = normed
    logit = jnp.sum(normed.astype(f32) * gate_w[...].astype(f32), axis=-1, keepdims=True)
    prob[...] = jnp.broadcast_to(1.0 / (1.0 + jnp.exp(-logit)), prob.shape)


def send_kernel(core_ref, g_any, u_any, d_any, out_any, buf, in_sems, out_sems):
    n = out_any.shape[0] // 3
    at = pl.multiple_of(core_ref[0] * n, n)
    ins, outs = [], []
    for i, w in enumerate((g_any, u_any, d_any)):
        here = buf.at[pl.ds(i * n, n)]
        ins.append(pltpu.make_async_copy(w.at[pl.ds(at, n)], here, in_sems.at[i]))
        outs.append(pltpu.make_async_copy(here, out_any.at[pl.ds(i * n, n)], out_sems.at[i]))
    for copy in ins:
        copy.start()
    for copy, out in zip(ins, outs):
        copy.wait()
        out.start()
    for out in outs:
        out.wait()


def assemble_kernel(g_any, u_any, d_any, a_any, b_any, w_ref, d_ref, sems):
    own = g_any.shape[0]
    swap = a_any.shape[0] // 3
    block = 128
    copies = []

    def start(src, at, dst, to, n):
        copy = pltpu.make_async_copy(
            src.at[pl.ds(at, n)], dst.at[pl.ds(to, n)], sems.at[len(copies)]
        )
        copy.start()
        copies.append(copy)

    for part in range(2):
        pos = 0
        for source, at, length in (
            ((g_any, u_any)[part], 0, own),
            (a_any, part * swap, swap),
            (b_any, part * swap, swap),
        ):
            done = 0
            while done < length:
                b, inside = divmod(pos, block)
                n = min(block - inside, length - done)
                start(source, at + done, w_ref, b * 2 * block + part * block + inside, n)
                done += n
                pos += n
    start(d_any, 0, d_ref, 0, own)
    start(a_any, 2 * swap, d_ref, own, swap)
    start(b_any, 2 * swap, d_ref, own + swap, swap)
    for copy in copies:
        copy.wait()


def aligned(i, step):
    return i * step if isinstance(i, int) else pl.multiple_of(i * step, step)


def repeat(count, unroll, body):
    if unroll:
        for i in range(count):
            body(i)
    else:
        pl.loop(0, count)(body)


def expert_kernel(count, unroll, *refs):
    xs, w_ref, d_ref, outs = refs[:count], refs[count], refs[count + 1], refs[count + 2 : -2]
    x_ref, h_ref = refs[-2:]
    at = 0
    for x in xs:
        x_ref[at : at + x.shape[0], :] = x[...]
        at += x.shape[0]
    block = 128

    def gate_and_up(b):
        both = lax.dot_general(
            x_ref[...],
            w_ref[pl.ds(aligned(b, 2 * block), 2 * block), :],
            (((1,), (1,)), ((), ())),
            preferred_element_type=f32,
        )
        gate, up = both[:, :block], both[:, block:]
        value = (gate / (1.0 + jnp.exp(-gate)) * up).astype(bf16)
        h_ref[:, pl.ds(aligned(b, block), block)] = value

    repeat(w_ref.shape[0] // (2 * block), unroll, gate_and_up)
    width = 256 if unroll else 896

    def down(c):
        cols = pl.ds(aligned(c, width), width)
        part = jnp.dot(h_ref[...], d_ref[:, cols], preferred_element_type=f32).astype(bf16)
        at = 0
        for out in outs:
            out[:, cols] = part[at : at + out.shape[0]]
            at += out.shape[0]

    repeat(d_ref.shape[1] // width, unroll, down)


def join_kernel(*refs):
    out = refs[-1]
    n = refs[0].shape[0]
    for i, ref in enumerate(refs[:-1]):
        out[i * n : (i + 1) * n, :] = ref[...]


def join(xs):
    rows, width = xs[0].shape
    return pl.pallas_call(
        join_kernel,
        out_shape=jax.ShapeDtypeStruct((rows * len(xs), width), bf16),
        in_specs=[VMEM] * len(xs),
        out_specs=VMEM,
        compiler_params=SMALL,
        cost_estimate=pl.CostEstimate(
            flops=0, bytes_accessed=4 * rows * len(xs) * width, transcendentals=0
        ),
    )(*xs)


def expert(xs, weights, unroll):
    w, d = weights
    rows, width = sum(x.shape[0] for x in xs), xs[0].shape[1]
    units = d.shape[0]
    return pl.pallas_call(
        functools.partial(expert_kernel, len(xs), unroll),
        out_shape=[jax.ShapeDtypeStruct(x.shape, bf16) for x in xs],
        in_specs=[VMEM] * (len(xs) + 2),
        out_specs=[VMEM] * len(xs),
        scratch_shapes=[pltpu.VMEM((rows, width), bf16), pltpu.VMEM((rows, units), bf16)],
        compiler_params=pltpu.CompilerParams(vmem_limit_bytes=30 << 20),
        cost_estimate=pl.CostEstimate(
            flops=6 * rows * units * width,
            bytes_accessed=6 * units * width + 4 * rows * width,
            transcendentals=rows * units,
        ),
    )(*xs, w, d)


def final_kernel(attended, prob, *refs):
    terms, out = refs[:-1], refs[-1]
    shared = terms[0][...].astype(f32)
    for term in terms[1:]:
        shared += term[...].astype(f32)
    out[...] = (attended[...].astype(f32) + prob[:, :1] * shared).astype(bf16)


def per_device(
    queries,
    keys,
    values,
    block_table,
    residual,
    out_weight,
    norm_gain,
    gate_logit_weight,
    gate_weight,
    up_weight,
    down_weight,
):
    tokens = queries.shape[0]
    half = tokens // 2
    quarter = tokens // 4
    width = residual.shape[1]
    hidden = down_weight.shape[0]
    y, z, xh = (lax.axis_index(a) for a in CTX)
    core = lax.axis_index("core")
    t = lax.axis_index(TP)

    gate_t, up_t = gate_weight.T, up_weight.T
    piece = hidden // 2
    kv = jnp.concatenate([keys, values], axis=1)
    kv = jnp.concatenate([kv, fetch(kv, "xh", 1)], axis=0)
    core_at, _ = lax.optimization_barrier((core.astype(jnp.int32)[None], kv))

    to_send = pl.pallas_call(
        send_kernel,
        out_shape=jax.ShapeDtypeStruct((3 * piece, width), bf16),
        in_specs=[SMEM, HBM, HBM, HBM],
        out_specs=HBM,
        scratch_shapes=[
            pltpu.VMEM((3 * piece, width), bf16),
            pltpu.SemaphoreType.DMA((3,)),
            pltpu.SemaphoreType.DMA((3,)),
        ],
        cost_estimate=pl.CostEstimate(
            flops=0, bytes_accessed=12 * piece * width, transcendentals=0
        ),
    )(core_at, gate_t, up_t, down_weight)
    swap_a = lax.ppermute(to_send, ("xh", "xl"), [(0, 3), (3, 0), (1, 2), (2, 1)])

    kv = jnp.concatenate(gather_direct(kv, "y"), axis=0)
    ahead, behind = gather_ring(kv, "z")
    far = gather_far(ahead[3], behind[3], "z")
    at = jnp.stack([y, z, xh, t]).astype(jnp.int32)

    rows = GROUP * tokens
    piece_rows = kv.shape[0]
    steps = (0, 1, 7, 2, 6)
    state = pl.pallas_call(
        functools.partial(attention_kernel, steps),
        out_shape=[jax.ShapeDtypeStruct((rows, HEAD_DIM), bf16)]
        + [jax.ShapeDtypeStruct((rows, HEAD_DIM), f32)] * 3,
        in_specs=[SMEM, SMEM, VMEM] + [HBM] * 5,
        out_specs=[VMEM] * 4,
        scratch_shapes=[
            pltpu.VMEM((5,) + kv.shape, bf16),
            pltpu.VMEM((8, piece_rows), jnp.int32),
            pltpu.SemaphoreType.DMA((5,)),
        ],
        compiler_params=pltpu.CompilerParams(vmem_limit_bytes=16 << 20),
        cost_estimate=pl.CostEstimate(
            flops=20 * rows * piece_rows * HEAD_DIM,
            bytes_accessed=20 * piece_rows * HEAD_DIM,
            transcendentals=5 * rows * piece_rows,
        ),
    )(at, block_table, queries, ahead[0], ahead[1], behind[1], ahead[2], behind[2])
    steps = (3, 5, 4)
    keep, send = pl.pallas_call(
        functools.partial(project_kernel, steps),
        out_shape=[jax.ShapeDtypeStruct((half, width), bf16)] * 2,
        in_specs=[SMEM, SMEM] + [VMEM] * 4 + [HBM] * 5,
        out_specs=[VMEM] * 2,
        scratch_shapes=[
            pltpu.VMEM(out_weight.shape, bf16),
            pltpu.VMEM((3,) + kv.shape, bf16),
            pltpu.VMEM((8, piece_rows), jnp.int32),
            pltpu.SemaphoreType.DMA((5,)),
        ],
        compiler_params=pltpu.CompilerParams(vmem_limit_bytes=46 << 20),
        cost_estimate=pl.CostEstimate(
            flops=12 * rows * piece_rows * HEAD_DIM + 2 * tokens * out_weight.size,
            bytes_accessed=2 * out_weight.size + 12 * piece_rows * HEAD_DIM,
            transcendentals=3 * rows * piece_rows,
        ),
    )(at, block_table, *state, ahead[3], behind[3], *far, out_weight)

    near = fetch(send, "core", 1)
    _, beyond = add([keep, near], pieces=2)
    beyond = fetch(beyond, "xl", 1)
    attended, normed, prob = pl.pallas_call(
        norm_kernel,
        out_shape=[
            jax.ShapeDtypeStruct((quarter, width), bf16),
            jax.ShapeDtypeStruct((quarter, width), bf16),
            jax.ShapeDtypeStruct((quarter, 128), f32),
        ],
        in_specs=[VMEM] * 6,
        out_specs=[VMEM] * 3,
        compiler_params=SMALL,
        cost_estimate=pl.CostEstimate(
            flops=10 * quarter * width, bytes_accessed=14 * quarter * width, transcendentals=quarter
        ),
    )(keep, near, beyond, residual, norm_gain[None, :], gate_logit_weight[None, :])

    by_y = join(gather_direct(normed, "y"))
    ahead, behind = gather_ring(by_y, "z")
    swap_a, _ = lax.optimization_barrier((swap_a, (ahead[1], behind[1])))
    swap_b = fetch(swap_a, "core", 1)
    weights = pl.pallas_call(
        assemble_kernel,
        out_shape=[
            jax.ShapeDtypeStruct((4 * hidden, width), bf16),
            jax.ShapeDtypeStruct((2 * hidden, width), bf16),
        ],
        in_specs=[HBM] * 5,
        out_specs=[VMEM] * 2,
        scratch_shapes=[pltpu.SemaphoreType.DMA((24,))],
        compiler_params=pltpu.CompilerParams(vmem_limit_bytes=16 << 20),
        cost_estimate=pl.CostEstimate(
            flops=0, bytes_accessed=12 * hidden * width, transcendentals=0
        ),
    )(gate_t, up_t, down_weight, swap_a, swap_b)
    ahead_3, behind_3, weights = lax.optimization_barrier((ahead[3], behind[3], weights))
    far = gather_far(ahead_3, behind_3, "z")
    after_2, before_2, after_3, before_3 = expert(
        [ahead[2], behind[2], ahead[3], behind[3]], weights, False
    )
    weights, after_3 = lax.optimization_barrier((weights, after_3))
    far_parts = expert(far, weights, True)
    own, after, before = expert([ahead[0], ahead[1], behind[1]], weights, False)
    near_parts = [own, after, after_2, after_3, None, before_3, before_2, before]
    by_y = add(scatter_ring(near_parts, far_parts, "z"), pieces=4)
    terms = scatter_direct(by_y, "y")
    return pl.pallas_call(
        final_kernel,
        out_shape=jax.ShapeDtypeStruct((quarter, width), bf16),
        in_specs=[VMEM] * 6,
        out_specs=VMEM,
        compiler_params=SMALL,
        cost_estimate=pl.CostEstimate(
            flops=10 * quarter * width, bytes_accessed=16 * quarter * width, transcendentals=0
        ),
    )(attended, prob, *terms)


def solution(mesh):
    fine = Mesh(mesh.devices.reshape(tuple(SIZES.values())), tuple(SIZES))
    return jax.shard_map(
        per_device,
        mesh=fine,
        in_specs=(
            P(CTX, TP),
            P(CTX, TP),
            P(CTX, TP),
            P(),
            P(CTX + TP, None),
            P(TP, None),
            P(),
            P(),
            P(None, CTX),
            P(None, CTX),
            P(CTX, None),
        ),
        out_specs=P(CTX + TP, None),
        check_vma=False,
    )
```
